32 devices in a mesh: dp: 8 (over z, x), tensor: 4 (over y, core).
Axes of the slice: x: 2, y: 2, z: 4, core: 2. Of those that a mesh axis runs over, the one named last changes fastest.
Arguments:
- patches: bfloat16 [16384, 768], P(('dp', 'tensor')), may hold values from -6 to 6
- cotangent: bfloat16 [16384, 768], P(('dp', 'tensor')), may hold values from -6 to 6
- mask_rows: int32 [16384], P(('dp', 'tensor')), may hold values 0 or 1
- count_big: int32 [8], P('dp'), may hold values from 0 to 10
- pos_big: bfloat16 [197, 768], replicated, may hold values from -4 to 4
- pos_small: bfloat16 [101, 768], replicated, may hold values from -4 to 4
- step_count: int32 [1], replicated, may hold values from 1 to 20
- qkv_master: float32 [3, 768, 768], P(None, 'dp', 'tensor'), may hold values from -0.21875 to 0.21875
- qkv_first: float32 [3, 768, 768], P(None, 'dp', 'tensor')
- qkv_second: float32 [3, 768, 768], P(None, 'dp', 'tensor'), as said below
- out_master: float32 [768, 768], P('tensor', 'dp'), may hold values from -0.875 to 0.875
- out_first: float32 [768, 768], P('tensor', 'dp')
- out_second: float32 [768, 768], P('tensor', 'dp'), as said below
- up_master: float32 [768, 3072], P('dp', 'tensor'), may hold values from -0.21875 to 0.21875
- up_first: float32 [768, 3072], P('dp', 'tensor')
- up_second: float32 [768, 3072], P('dp', 'tensor'), as said below
- down_master: float32 [3072, 768], P('tensor', 'dp'), may hold values from -0.109375 to 0.109375
- down_first: float32 [3072, 768], P('tensor', 'dp')
- down_second: float32 [3072, 768], P('tensor', 'dp'), as said below
- norm_gains: float32 [4, 768], replicated, may hold values from 0.25 to 1.75
- gain_first: float32 [4, 768], replicated
- gain_second: float32 [4, 768], replicated, as said below
- shifts: float32 [11, 768], replicated, may hold values from -3 to 3
- shift_first: float32 [11, 768], replicated
- shift_second: float32 [11, 768], replicated, as said below
Outputs:
- layer_out: bfloat16 [16384, 768], P(('dp', 'tensor'))
- patch_grad: float32 [16384, 768], P(('dp', 'tensor'))
- qkv_new: float32 [3, 768, 768], P(None, 'dp', 'tensor')
- qkv_first_new: float32 [3, 768, 768], P(None, 'dp', 'tensor')
- qkv_second_new: float32 [3, 768, 768], P(None, 'dp', 'tensor')
- qkv_copy: bfloat16 [3, 768, 768], P(None, 'dp', 'tensor')
- out_new: float32 [768, 768], P('tensor', 'dp')
- out_first_new: float32 [768, 768], P('tensor', 'dp')
- out_second_new: float32 [768, 768], P('tensor', 'dp')
- out_copy: bfloat16 [768, 768], P('tensor', 'dp')
- up_new: float32 [768, 3072], P('dp', 'tensor')
- up_first_new: float32 [768, 3072], P('dp', 'tensor')
- up_second_new: float32 [768, 3072], P('dp', 'tensor')
- up_copy: bfloat16 [768, 3072], P('dp', 'tensor')
- down_new: float32 [3072, 768], P('tensor', 'dp')
- down_first_new: float32 [3072, 768], P('tensor', 'dp')
- down_second_new: float32 [3072, 768], P('tensor', 'dp')
- down_copy: bfloat16 [3072, 768], P('tensor', 'dp')
- gain_new: float32 [4, 768], replicated
- gain_first_new: float32 [4, 768], replicated
- gain_second_new: float32 [4, 768], replicated
- gain_copy: bfloat16 [4, 768], replicated
- shift_new: float32 [11, 768], replicated
- shift_first_new: float32 [11, 768], replicated
- shift_second_new: float32 [11, 768], replicated
- shift_copy: bfloat16 [11, 768], replicated
The draws below stay inside these ranges and needn't reach their ends.
Inputs may be any that keep to these rules, and one draw needn't show every extreme that they name: `qkv_second`: every entry is positive. `out_second`: every entry is positive. `up_second`: every entry is positive. `down_second`: every entry is positive. `gain_second`: every entry is positive. `shift_second`: every entry is positive.
All inputs are finite; a program needn't handle non-finite values. No bound on the sum of `mask_rows` on one device may be relied on, other than what follows from the above.
Results may differ from the reference program's by a relative error of at most 0.012.
The reference program's roundings to bfloat16 on the way count: a program that leaves them out, or rounds other values in their place, can miss the bound.
Values may be sent and summed in bfloat16 or wider, within the bound.
No kernel may reach another device: no remote copies, remote signals or barrier semaphores. Data moves between devices by JAX's collectives and lax.ppermute only.
A program may use at most 128 MiB of HBM per device.

```python
import jax
import jax.numpy as jnp
from jax import lax

D = 768
HEADS = 12
HEAD_DIM = 64
FF = 3072
BIG_LEN = 197
SMALL_LEN = 101
ROWS = 2048
GAIN_ROWS = 4
SHIFT_ROWS = 11
TOKENS = 16384
N_DP = 8


def first_moment(key, shape, square):
    magnitude = jnp.sqrt(jnp.float32(square))
    return magnitude * jax.random.uniform(key, shape, jnp.float32, -2.0, 2.0)


def second_moment(key, shape, square):
    factor = jax.random.uniform(key, shape, jnp.float32, 0.0, 1.0)
    return jnp.float32(square) * jnp.exp(factor * jnp.log(jnp.float32(4.0)))


def draw_qkv_first(key, part):
    return first_moment(key, (3, D, D), TOKENS / 8)


def draw_qkv_second(key, part):
    return second_moment(key, (3, D, D), TOKENS / 8)


def draw_out_first(key, part):
    return first_moment(key, (D, D), TOKENS / 25)


def draw_out_second(key, part):
    return second_moment(key, (D, D), TOKENS / 25)


def draw_up_first(key, part):
    return first_moment(key, (D, FF), TOKENS / 16)


def draw_up_second(key, part):
    return second_moment(key, (D, FF), TOKENS / 16)


def draw_down_first(key, part):
    return first_moment(key, (FF, D), TOKENS / 3)


def draw_down_second(key, part):
    return second_moment(key, (FF, D), TOKENS / 3)


def draw_gain_first(key, part):
    return first_moment(key, (GAIN_ROWS, D), TOKENS / 2)


def draw_gain_second(key, part):
    return second_moment(key, (GAIN_ROWS, D), TOKENS / 2)


def draw_shift_first(key, part):
    return first_moment(key, (SHIFT_ROWS, D), TOKENS / 4)


def draw_shift_second(key, part):
    return second_moment(key, (SHIFT_ROWS, D), TOKENS / 4)


def with_ends(array, rng, low, high):
    place = [jax.random.randint(jax.random.fold_in(rng, axis), (), 0, length) for axis, length in enumerate(array.shape)]
    longest = array.shape.index(max(array.shape))
    beside = place[:longest] + [(place[longest] + 1) % array.shape[longest]] + place[longest + 1:]
    return array.at[tuple(place)].set(low).at[tuple(beside)].set(high)


def raised(result, stream_key, source, target, parts, factor):
    owner, partner = [(jnp.arange(result.shape[dim]) // (result.shape[dim] // parts)).reshape([-1 if axis == dim else 1 for axis in range(result.ndim)]) for dim in (source, target)]
    chosen = jax.random.permutation(stream_key, parts)[partner]
    strong = (owner == chosen) | (owner == (partner + parts // 2) % parts)
    return jnp.where(strong, factor * result, result)


def block_levels(own_key, extent, cuts, least, largest):
    loudness = 1.0
    for axis_at, blocks in cuts:
        draws = jax.random.uniform(jax.random.fold_in(jax.random.fold_in(own_key, 6), axis_at), (blocks,), jnp.float32, least / len(cuts), largest / len(cuts))
        loudness = loudness * jnp.repeat(jnp.exp(draws), extent[axis_at] // blocks).reshape((-1,) + (1,) * (len(extent) - 1 - axis_at))
    return loudness


def noise(stream_key, extent, spread, bound, pieces=(), kind=jnp.bfloat16):
    result = jax.random.normal(stream_key, extent, jnp.float32) * spread
    if len(pieces) > 0:
        result = block_levels(stream_key, extent, pieces, -0.22, 0.18) * result
    return jnp.clip(result, min=-bound, max=bound).astype(kind)


def heavy_noise(key, extent, scale, most, cuts, heavy, kind=jnp.bfloat16):
    result = scale * jax.random.normal(key, extent, jnp.float32)
    if cuts:
        result = result * block_levels(key, extent, cuts, -0.22, 0.18)
    return jnp.clip(raised(result, jax.random.fold_in(key, 3), *heavy), -most, most).astype(kind)


def setup_inputs(seed: int = 0) -> dict:
    key_list = jax.random.split(jax.random.key(seed), 26)
    patches = heavy_noise(key_list[0], (TOKENS, D), 1.0, 6.0, ((0, 32),), (0, 1, 32, 2.75))
    cotangent = noise(key_list[1], (TOKENS, D), 1.0, 6.0, ((0, 32),))
    mask_rows = with_ends((jax.random.randint(key_list[2], (TOKENS,), 0, 5) < 3).astype(jnp.int32), jax.random.fold_in(key_list[2], 1), 0, 1)
    count_big = with_ends(jax.random.randint(key_list[3], (N_DP,), 0, ROWS // BIG_LEN + 1), jax.random.fold_in(key_list[3], 1), 0, (ROWS // BIG_LEN + 1) - 1).astype(jnp.int32)
    pos_big = noise(key_list[4], (BIG_LEN, D), 0.5, 4.0)
    pos_small = noise(key_list[5], (SMALL_LEN, D), 0.5, 4.0)
    step_count = jax.random.randint(key_list[6], (1,), 1, 21).astype(jnp.int32)
    qkv_master = noise(key_list[7], (3, D, D), D ** -0.5, 0.21875, ((1, 8), (2, 4)), jnp.float32)
    qkv_first = draw_qkv_first(jax.random.fold_in(key_list[25], 71), 0)
    qkv_second = draw_qkv_second(jax.random.fold_in(key_list[25], 71), 0)
    out_master = noise(key_list[10], (D, D), (D // 16) ** -0.5, 0.875, ((0, 4), (1, 8)), jnp.float32)
    out_first = draw_out_first(jax.random.fold_in(key_list[25], 71), 0)
    out_second = draw_out_second(jax.random.fold_in(key_list[25], 71), 0)
    up_master = noise(key_list[13], (D, FF), D ** -0.5, 0.21875, ((0, 8), (1, 4)), jnp.float32)
    up_first = draw_up_first(jax.random.fold_in(key_list[25], 71), 0)
    up_second = draw_up_second(jax.random.fold_in(key_list[25], 71), 0)
    down_master = noise(key_list[16], (FF, D), FF ** -0.5, 0.109375, ((0, 4), (1, 8)), jnp.float32)
    down_first = draw_down_first(jax.random.fold_in(key_list[25], 71), 0)
    down_second = draw_down_second(jax.random.fold_in(key_list[25], 71), 0)
    norm_gains = jnp.clip(1.0 + 0.15 * jax.random.normal(key_list[19], (GAIN_ROWS, D), jnp.float32), 0.25, 1.75)
    gain_first = draw_gain_first(jax.random.fold_in(key_list[25], 71), 0)
    gain_second = draw_gain_second(jax.random.fold_in(key_list[25], 71), 0)
    shifts = noise(key_list[22], (SHIFT_ROWS, D), 0.5, 3.0, (), jnp.float32)
    shift_first = draw_shift_first(jax.random.fold_in(key_list[25], 71), 0)
    shift_second = draw_shift_second(jax.random.fold_in(key_list[25], 71), 0)
    return {"patches": patches, "cotangent": cotangent, "mask_rows": mask_rows, "count_big": count_big, "pos_big": pos_big, "pos_small": pos_small, "step_count": step_count, "qkv_master": qkv_master, "qkv_first": qkv_first, "qkv_second": qkv_second, "out_master": out_master, "out_first": out_first, "out_second": out_second, "up_master": up_master, "up_first": up_first, "up_second": up_second, "down_master": down_master, "down_first": down_first, "down_second": down_second, "norm_gains": norm_gains, "gain_first": gain_first, "gain_second": gain_second, "shifts": shifts, "shift_first": shift_first, "shift_second": shift_second}


@jax.custom_vjp
def low(v):
    return lax.optimization_barrier(v.astype(jnp.bfloat16)).astype(jnp.float32)

@jax.custom_vjp
def low_back(v):
    return v

def low_keep(v):
    return (low(v), None)

def low_pass(kept, grad):
    return (grad,)

def back_keep(v):
    return (v, None)

def back_low(kept, grad):
    return (low(grad),)
low.defvjp(low_keep, low_pass)
low_back.defvjp(back_keep, back_low)
EPS_NORM = 1e-06
ADAM_EPS = 1e-08
DECAY = 0.05
NEGATIVE = -1e+30
HIGHEST = lax.Precision.HIGHEST

def row_layout(count_big):
    row_ids = jnp.arange(ROWS, dtype=jnp.int32)
    big_rows = count_big * BIG_LEN
    count_small = (ROWS - big_rows) // SMALL_LEN
    used_rows = big_rows + count_small * SMALL_LEN
    remainder = row_ids - big_rows
    is_big = row_ids < big_rows
    is_valid = row_ids < used_rows
    segment = jnp.where(is_big, row_ids // BIG_LEN, count_big + remainder // SMALL_LEN)
    segment = jnp.where(is_valid, segment, -1)
    position = jnp.where(is_big, row_ids % BIG_LEN, remainder % SMALL_LEN)
    is_small = is_valid & jnp.logical_not(is_big)
    return (segment, position, is_big, is_small, is_valid)

def matmul(left_rows, right_rows):
    return jnp.dot(left_rows, right_rows, precision=HIGHEST, preferred_element_type=jnp.float32)

def layer_norm(values, gain, shift):
    average = lax.optimization_barrier(jnp.mean(values, axis=-1, keepdims=True))
    centered = values - average
    inverse = lax.rsqrt(lax.optimization_barrier(jnp.mean(centered * centered, axis=-1, keepdims=True)) + EPS_NORM)
    return centered * inverse * gain + shift

def group_forward(weights, norm_gains, shifts, patch_rows, mask_group, count_big, pos_big, pos_small):
    qkv_w, out_w, up_w, down_w = weights
    segment, position, is_big, is_small, is_valid = row_layout(count_big)
    pick_big = ((position[:, None] == jnp.arange(BIG_LEN, dtype=jnp.int32)[None, :]) & is_big[:, None]).astype(jnp.float32)
    pick_small = ((position[:, None] == jnp.arange(SMALL_LEN, dtype=jnp.int32)[None, :]) & is_small[:, None]).astype(jnp.float32)
    placed = matmul(pick_big, pos_big) + matmul(pick_small, pos_small)
    masked = (mask_group == 1) & is_valid
    start_rows = jnp.where(masked[:, None], shifts[6][None, :], patch_rows) + placed
    normed = low(layer_norm(start_rows, norm_gains[0], shifts[0]))
    queries = low(low_back(matmul(normed, qkv_w[0]) + shifts[1]))
    keys_all = low(low_back(matmul(normed, qkv_w[1])))
    values_all = low(low_back(matmul(normed, qkv_w[2]) + shifts[2]))
    row_count = queries.shape[0]
    query_heads = queries.reshape(row_count, HEADS, HEAD_DIM)
    key_heads = keys_all.reshape(row_count, HEADS, HEAD_DIM)
    value_heads = values_all.reshape(row_count, HEADS, HEAD_DIM)
    scores = low_back(jnp.einsum('qhd,khd->hqk', query_heads, key_heads, precision=HIGHEST) * HEAD_DIM ** (-0.5))
    same_image = segment[:, None] == segment[None, :]
    scores = jnp.where(same_image[None], scores, NEGATIVE)
    highest = lax.optimization_barrier(jnp.max(scores, axis=-1, keepdims=True))
    exp_scores = jnp.exp(scores - highest)
    probs = low(exp_scores / lax.optimization_barrier(jnp.sum(exp_scores, axis=-1, keepdims=True)))
    mixed = jnp.einsum('hqk,khd->qhd', probs, value_heads, precision=HIGHEST).reshape(row_count, D)
    mixed = low(low_back(mixed))
    branch_attn = low_back(matmul(mixed, out_w) + shifts[3])
    middle = start_rows + norm_gains[2] * branch_attn
    normed_two = low(layer_norm(middle, norm_gains[1], shifts[4]))
    up_bias = shifts[7:].reshape(-1)
    hidden = low(jax.nn.gelu(low_back(matmul(normed_two, up_w) + up_bias), approximate=False))
    branch_mlp = low_back(matmul(hidden, down_w) + shifts[5])
    return middle + norm_gains[3] * branch_mlp

def adamw_step(master, first, second, gradient, rate, decay, correction):
    first_new = 0.5 * first + 0.5 * gradient
    second_new = 0.5 * second + 0.5 * gradient * gradient
    update = first_new / correction / (jnp.sqrt(second_new / correction) + ADAM_EPS)
    master_new = master - rate * (update + decay * master)
    return (master_new, first_new, second_new, master_new.astype(jnp.bfloat16))

def reference(patches, cotangent, mask_rows, count_big, pos_big, pos_small, step_count, qkv_master, qkv_first, qkv_second, out_master, out_first, out_second, up_master, up_first, up_second, down_master, down_first, down_second, norm_gains, gain_first, gain_second, shifts, shift_first, shift_second):
    weights = tuple((lax.optimization_barrier(master.astype(jnp.bfloat16)).astype(jnp.float32) for master in (qkv_master, out_master, up_master, down_master)))
    patch_groups = patches.astype(jnp.float32).reshape(N_DP, ROWS, D)
    mask_groups = mask_rows.reshape(N_DP, ROWS)
    table_big = pos_big.astype(jnp.float32)
    table_small = pos_small.astype(jnp.float32)
    group_step = jax.checkpoint(group_forward)

    def forward(weight_set, gain_set, shift_set, patch_set):

        def one_group(item):
            return group_step(weight_set, gain_set, shift_set, item[0], item[1], item[2], table_big, table_small)
        return lax.map(one_group, (patch_set, mask_groups, count_big))
    outputs, backward = jax.vjp(forward, weights, norm_gains, shifts, patch_groups)
    valid_rows = jax.vmap(row_layout)(count_big)[4]
    grad_out = cotangent.astype(jnp.float32).reshape(N_DP, ROWS, D) * valid_rows[..., None].astype(jnp.float32)
    weight_grads, gain_grads, shift_grads, patch_grads = backward(grad_out)
    correction = 1.0 - jnp.power(jnp.float32(0.5), step_count[0].astype(jnp.float32))
    qkv_res = adamw_step(qkv_master, qkv_first, qkv_second, weight_grads[0], D ** (-0.5), DECAY, correction)
    out_res = adamw_step(out_master, out_first, out_second, weight_grads[1], (D // 16) ** (-0.5), DECAY, correction)
    up_res = adamw_step(up_master, up_first, up_second, weight_grads[2], D ** (-0.5), DECAY, correction)
    down_res = adamw_step(down_master, down_first, down_second, weight_grads[3], FF ** (-0.5), DECAY, correction)
    gain_res = adamw_step(norm_gains, gain_first, gain_second, gain_grads, 0.1, 0.0, correction)
    shift_res = adamw_step(shifts, shift_first, shift_second, shift_grads, 0.3, 0.0, correction)
    layer_out = outputs.reshape(N_DP * ROWS, D).astype(jnp.bfloat16)
    patch_grad = patch_grads.reshape(N_DP * ROWS, D)
    return (layer_out, patch_grad, qkv_res[0], qkv_res[1], qkv_res[2], qkv_res[3], out_res[0], out_res[1], out_res[2], out_res[3], up_res[0], up_res[1], up_res[2], up_res[3], down_res[0], down_res[1], down_res[2], down_res[3], gain_res[0], gain_res[1], gain_res[2], gain_res[3], shift_res[0], shift_res[1], shift_res[2], shift_res[3])
```

```python
import functools

import jax
import jax.numpy as jnp
from jax import lax
from jax.experimental import pallas as pl
from jax.experimental.pallas import tpu as pltpu
from jax.sharding import PartitionSpec as P

D = 768
HEAD_DIM = 64
FF = 3072
BIG_LEN = 197
SMALL_LEN = 101
HALO = 208
ALIGN = 16
BIG_Q, BIG_K = 224, 256
SMALL_W = 128

EPS_NORM = 1e-06
ADAM_EPS = 1e-08
DECAY = 0.05
NEGATIVE = -1e30
FACTOR = HEAD_DIM ** (-0.5)
BF = jnp.bfloat16
F32 = jnp.float32


def send_dp(value, target):
    count = lax.axis_size("dp")
    return lax.ppermute(value, "dp", [(i, target(i)) for i in range(count)])


def send_x(value):
    return send_dp(value, lambda i: i ^ 1)


def send_tensor(value, mask):
    return lax.ppermute(value, "tensor", [(i, i ^ mask) for i in range(4)])


def send_y(value):
    return send_tensor(value, 2)


def send_core(value):
    return send_tensor(value, 1)


def z_digits():
    left = lax.axis_size("dp") // 2
    stride, digits = 1, []
    while left > 1:
        radix = 4 if left % 4 == 0 else 2
        digits.append((stride, radix))
        stride, left = stride * radix, left // radix
    return digits


def send_digit(value, stride, radix, step):
    def target(i):
        z, x = i // 2, i % 2
        digit = z // stride % radix
        return 2 * (z + ((digit + step) % radix - digit) * stride) + x

    return send_dp(value, target)


def gather_z(block):
    z = lax.axis_index("dp") // 2
    block = block[None]
    for stride, radix in z_digits():
        digit = z // stride % radix
        out = jnp.zeros((radix,) + block.shape, block.dtype)
        out = lax.dynamic_update_slice(out, block[None], (digit, 0, 0, 0))
        pieces = [send_digit(block, stride, radix, step) for step in range(1, radix)]
        for step, piece in enumerate(pieces, 1):
            out = lax.dynamic_update_slice(
                out, piece[None], ((digit + radix - step) % radix, 0, 0, 0)
            )
        block = out.reshape((-1,) + block.shape[1:])
    return block


def scatter_z(partial):
    z = lax.axis_index("dp") // 2
    for stride, radix in reversed(z_digits()):
        digit = z // stride % radix
        parts = partial.reshape((radix, -1) + partial.shape[1:])
        own = lax.dynamic_index_in_dim(parts, digit, 0, keepdims=False)
        pieces = [
            send_digit(
                lax.dynamic_index_in_dim(
                    parts, (digit + step) % radix, 0, keepdims=False
                ).astype(BF),
                stride,
                radix,
                step,
            )
            for step in range(1, radix)
        ]
        for piece in pieces:
            own = own + piece.astype(F32)
        partial = own
    return partial[0]


def interleave(mine, other):
    x = lax.axis_index("dp") % 2
    low = jnp.where(x == 0, mine, other)
    high = jnp.where(x == 0, other, mine)
    return jnp.stack([low, high], axis=1).reshape(-1, mine.shape[-1])


def gather_chunk(z_all):
    half = z_all.shape[-1] // 2
    from_x = send_x(z_all)
    from_y = send_y(z_all[..., half:])
    from_xy = send_x(from_y)
    own = interleave(z_all, from_x)
    across = send_y(own[:, :half])
    own_core = send_core(own)
    across = jnp.concatenate([across, interleave(from_y, from_xy)], axis=1)
    return own, own_core, across, send_core(across)


def scatter_chunk(own, across):
    count, n = lax.axis_size("dp"), own.shape[-1]
    half = n // 2
    x = lax.axis_index("dp") % 2

    def at_x(value, which):
        return lax.dynamic_index_in_dim(value, which, 1, keepdims=False)

    own = own.reshape(count // 2, 2, -1, n)
    across = across.reshape(count // 2, 2, -1, n)
    over_y = send_y(across[..., :half].astype(BF))
    far = jnp.stack([at_x(own[..., half:], 1 - x), at_x(across[..., half:], 1 - x)])
    over_x = send_x(far.astype(BF))
    low = own[..., :half] + over_y.astype(F32)
    high_across = at_x(across[..., half:], x) + over_x[1].astype(F32)
    low_x = send_x(at_x(low, 1 - x).astype(BF))
    high_y = send_y(high_across.astype(BF))
    low = at_x(low, x) + low_x.astype(F32)
    high = at_x(own[..., half:], x) + over_x[0].astype(F32) + high_y.astype(F32)
    return scatter_z(jnp.concatenate([low, high], axis=-1))


def sum_everywhere(value):
    value = value + send_core(value)
    across = send_y(value), send_x(value), send_x(send_y(value))
    value = (value + across[1]) + (across[0] + across[2])
    count = lax.axis_size("dp")
    bit = 2
    while bit < count:
        value = value + send_dp(value, lambda i, b=bit: i ^ b)
        bit *= 2
    return value


def image_loops(bounds, window_loop):
    big_rows, total = bounds[4], bounds[6]

    def big(index, carry):
        window_loop(index * BIG_LEN, index * BIG_LEN + BIG_LEN, BIG_Q, BIG_K)
        return carry

    def small(index, carry):
        start = big_rows + index * SMALL_LEN
        window_loop(start, jnp.minimum(start + SMALL_LEN, total), SMALL_W, SMALL_W)
        return carry

    lax.fori_loop(bounds[0], bounds[1], big, 0)
    lax.fori_loop(bounds[2], bounds[3], small, 0)


def image_bounds(count_big, first_row, local_rows, total_rows):
    big_rows = count_big * BIG_LEN
    last_row = first_row + local_rows - 1
    big_from = jnp.minimum(first_row // BIG_LEN, count_big)
    big_to = jnp.minimum(last_row // BIG_LEN + 1, count_big)
    small_from = jnp.maximum(first_row - big_rows, 0) // SMALL_LEN
    small_to = jnp.where(last_row >= big_rows, (last_row - big_rows) // SMALL_LEN + 1, small_from)
    base = first_row - HALO
    return jnp.stack(
        [big_from, big_to, small_from, small_to, big_rows, base, jnp.int32(total_rows), base]
    ).astype(jnp.int32)


def masks(start, stop, base, ext_rows, rows, keys):
    aligned = (start - base) // ALIGN * ALIGN
    at_q = pl.multiple_of(jnp.minimum(aligned, ext_rows - rows), ALIGN)
    at_k = pl.multiple_of(jnp.minimum(aligned, ext_rows - keys), ALIGN)

    def inside(offset, shape, axis):
        ids = lax.broadcasted_iota(jnp.int32, shape, axis) + (offset + base)
        return (ids >= start) & (ids < stop)

    return (
        at_q,
        at_k,
        inside(at_q, (rows, 1), 0),
        inside(at_k, (1, keys), 1),
        inside(at_k, (keys, 1), 0),
    )


def dot_nt(left, right):
    return lax.dot_general(left, right, (((1,), (1,)), ((), ())), preferred_element_type=F32)


def dot_tn(left, right):
    return lax.dot_general(left, right, (((0,), (0,)), ((), ())), preferred_element_type=F32)


def dot_nn(left, right):
    return jnp.dot(left, right, preferred_element_type=F32)


def attention_forward_kernel(bounds, *refs):
    qkv, outs = refs[:4], refs[4:]
    ext_rows = qkv[0].shape[0]

    def window(start, stop, rows, keys):
        at_q, at_k, row_in, key_in, _ = masks(start, stop, bounds[5], ext_rows, rows, keys)
        for source, out in zip(qkv, outs):
            width = out.shape[1]
            parts = []
            for at in range(0, width, HEAD_DIM):
                query = source[pl.ds(at_q, rows), at : at + HEAD_DIM]
                key = source[pl.ds(at_k, keys), width + at : width + at + HEAD_DIM]
                value = source[pl.ds(at_k, keys), 2 * width + at : 2 * width + at + HEAD_DIM]
                scores = jnp.where(key_in, dot_nt(query, key) * FACTOR, NEGATIVE)
                exps = jnp.exp(scores - jnp.max(scores, axis=-1, keepdims=True))
                probs = exps * (1.0 / jnp.sum(exps, axis=-1, keepdims=True))
                parts.append(dot_nn(probs.astype(BF), value))
            mixed = jnp.concatenate(parts, axis=1).astype(BF)
            old = out[pl.ds(at_q, rows), :]
            out[pl.ds(at_q, rows), :] = jnp.where(row_in, mixed, old)

    image_loops(bounds, window)


def attention_backward_kernel(bounds, *refs):
    qkv, grads, outs = refs[:4], refs[4:8], refs[8:]
    ext_rows = qkv[0].shape[0]

    def window(start, stop, rows, keys):
        at_q, at_k, row_in, key_in, key_row_in = masks(
            start, stop, bounds[5], ext_rows, rows, keys
        )
        both = row_in & key_in
        for source, grad, out in zip(qkv, grads, outs):
            width = grad.shape[1]
            query_parts, key_parts, value_parts = [], [], []
            for at in range(0, width, HEAD_DIM):
                query = source[pl.ds(at_q, rows), at : at + HEAD_DIM]
                key = source[pl.ds(at_k, keys), width + at : width + at + HEAD_DIM]
                value = source[pl.ds(at_k, keys), 2 * width + at : 2 * width + at + HEAD_DIM]
                grad_rows = grad[pl.ds(at_q, rows), at : at + HEAD_DIM]
                scores = jnp.where(key_in, dot_nt(query, key) * FACTOR, NEGATIVE)
                exps = jnp.exp(scores - jnp.max(scores, axis=-1, keepdims=True))
                probs = exps * (1.0 / jnp.sum(exps, axis=-1, keepdims=True))
                probs = jnp.where(both, probs, 0.0)
                weighted = probs * dot_nt(grad_rows, value)
                inner = jnp.sum(weighted, axis=-1, keepdims=True)
                grad_scores = (weighted - probs * inner).astype(BF)
                query_parts.append(dot_nn(grad_scores, key) * FACTOR)
                key_parts.append(dot_tn(grad_scores, query) * FACTOR)
                value_parts.append(dot_tn(probs.astype(BF), grad_rows))
            grad_query = jnp.concatenate(query_parts, axis=1).astype(BF)
            old = out[pl.ds(at_q, rows), :width]
            out[pl.ds(at_q, rows), :width] = jnp.where(row_in, grad_query, old)
            grad_kv = jnp.concatenate(key_parts + value_parts, axis=1).astype(BF)
            old = out[pl.ds(at_k, keys), width:]
            out[pl.ds(at_k, keys), width:] = jnp.where(key_row_in, grad_kv, old)

    image_loops(bounds, window)


def run_attention(kernel, name, bounds, inputs, out_width):
    ext_rows = inputs[0].shape[0]
    in_vmem = pl.BlockSpec(memory_space=pltpu.VMEM)
    return pl.pallas_call(
        kernel,
        name=name,
        in_specs=[pl.BlockSpec(memory_space=pltpu.SMEM)] + [in_vmem] * len(inputs),
        out_specs=[in_vmem] * 4,
        out_shape=[jax.ShapeDtypeStruct((ext_rows, out_width), BF)] * 4,
        compiler_params=pltpu.CompilerParams(vmem_limit_bytes=40 << 20),
    )(bounds, *inputs)


def exact_gelu(values):
    return jax.nn.gelu(values, approximate=False)


def norm_parts(values, gain, shift):
    average = jnp.mean(values, axis=-1, keepdims=True)
    centered = values - average
    inverse = lax.rsqrt(jnp.mean(centered * centered, axis=-1, keepdims=True) + EPS_NORM)
    normal_rows = centered * inverse
    return (normal_rows * gain + shift, normal_rows, inverse)


def norm_back(grad_rows, normal_rows, inverse, gain):
    scaled = grad_rows * gain
    return inverse * (
        scaled
        - jnp.mean(scaled, axis=-1, keepdims=True)
        - normal_rows * jnp.mean(scaled * normal_rows, axis=-1, keepdims=True)
    )


def adamw_step(master, first, second, gradient, rate, decay, correction):
    first_new = 0.5 * first + 0.5 * gradient
    second_new = 0.5 * second + 0.5 * gradient * gradient
    update = first_new / correction / (jnp.sqrt(second_new / correction) + ADAM_EPS)
    master_new = master - rate * (update + decay * master)
    return (master_new, first_new, second_new, master_new.astype(BF))


def to_absolute(parts):
    index = lax.axis_index("tensor")
    stacked = jnp.stack(parts).reshape(2, 2, -1)
    stacked = jnp.where(index // 2 == 1, stacked[::-1], stacked)
    return jnp.where(index % 2 == 1, stacked[:, ::-1], stacked).reshape(4, -1)


def on_device(
    patches,
    cotangent,
    mask_rows,
    count_big,
    pos_big,
    pos_small,
    step_count,
    qkv_master,
    qkv_first,
    qkv_second,
    out_master,
    out_first,
    out_second,
    up_master,
    up_first,
    up_second,
    down_master,
    down_first,
    down_second,
    norm_gains,
    gain_first,
    gain_second,
    shifts,
    shift_first,
    shift_second,
):
    tensor_id = lax.axis_index("tensor")
    local_rows = patches.shape[0]
    total_rows = 4 * local_rows
    lanes = qkv_master.shape[2]
    hidden_lanes = up_master.shape[1]
    big_rows = count_big[0] * BIG_LEN
    used_rows = big_rows + (total_rows - big_rows) // SMALL_LEN * SMALL_LEN
    first_row = tensor_id * local_rows

    payload = jnp.concatenate(
        [patches, jnp.broadcast_to(mask_rows[:, None].astype(BF), (local_rows, 128))], axis=1
    )
    up_hops, down_hops = [(0, 1), (1, 2), (2, 3)], [(1, 0), (2, 1), (3, 2)]
    before = lax.ppermute(payload[-HALO:], "tensor", up_hops)
    after = lax.ppermute(payload[:HALO], "tensor", down_hops)

    local_a = jnp.concatenate(
        [qkv_master[0], qkv_master[1], qkv_master[2], out_master.T], axis=1
    ).astype(BF)
    z_a = gather_z(local_a)
    local_b, local_c, z_a = lax.optimization_barrier(
        (up_master.astype(BF), down_master.astype(BF).T, z_a)
    )
    z_b = gather_z(local_b)
    a_all = gather_chunk(z_a)
    local_c, z_b = lax.optimization_barrier((local_c, z_b))
    z_c = gather_z(local_c)
    b_all = gather_chunk(z_b)
    c_all = gather_chunk(z_c)

    payload = jnp.concatenate([before, payload, after], axis=0)
    ext_rows = payload.shape[0]
    row_ids = first_row - HALO + jnp.arange(ext_rows, dtype=jnp.int32)
    remainder = row_ids - big_rows
    is_big = (row_ids >= 0) & (row_ids < big_rows)
    is_valid = (row_ids >= 0) & (row_ids < used_rows)
    is_small = is_valid & jnp.logical_not(is_big)
    position = jnp.where(is_big, row_ids % BIG_LEN, remainder % SMALL_LEN)
    masked_ext = (payload[:, D] == 1) & is_valid
    pick_big = (
        (position[:, None] == jnp.arange(BIG_LEN, dtype=jnp.int32)[None, :]) & is_big[:, None]
    ).astype(BF)
    pick_small = (
        (position[:, None] == jnp.arange(SMALL_LEN, dtype=jnp.int32)[None, :]) & is_small[:, None]
    ).astype(BF)
    placed = dot_nn(pick_big, pos_big) + dot_nn(pick_small, pos_small)
    start_ext = (
        jnp.where(masked_ext[:, None], shifts[6][None, :], payload[:, :D].astype(F32)) + placed
    )
    own = slice(HALO, HALO + local_rows)
    normed_ext, normal_ext, inverse_ext = norm_parts(start_ext, norm_gains[0], shifts[0])
    normed_ext = normed_ext.astype(BF)
    start_rows, masked, valid_local = start_ext[own], masked_ext[own], is_valid[own]
    normed, normal_one, inverse_one = normed_ext[own], normal_ext[own], inverse_ext[own]

    bounds = image_bounds(count_big[0], first_row, local_rows, total_rows)
    zero_bias = jnp.zeros((lanes,), F32)
    qkv_ext = []
    for step, weight in enumerate(a_all):
        at = (tensor_id ^ step) * lanes
        bias = jnp.concatenate(
            [
                lax.dynamic_slice_in_dim(shifts[1], at, lanes),
                zero_bias,
                lax.dynamic_slice_in_dim(shifts[2], at, lanes),
                zero_bias,
            ]
        )
        qkv_ext.append((dot_nn(normed_ext, weight) + bias).astype(BF))
    mixed = run_attention(attention_forward_kernel, "attention_forward", bounds, qkv_ext, lanes)
    mixed = [part[own] for part in mixed]
    out_w = [weight[:, 3 * lanes :] for weight in a_all]
    branch_attn = sum(dot_nt(part, weight) for part, weight in zip(mixed, out_w)) + shifts[3]
    middle = start_rows + norm_gains[2] * branch_attn
    normed_two, normal_two, inverse_two = norm_parts(middle, norm_gains[1], shifts[4])
    normed_two = normed_two.astype(BF)

    grad_out = cotangent.astype(F32) * valid_local[:, None].astype(F32)
    grad_branch = (norm_gains[3] * grad_out).astype(BF)
    up_bias = shifts[7:].reshape(-1)
    hidden, pre_grad = [], []
    for step in range(4):
        bias = lax.dynamic_slice_in_dim(up_bias, (tensor_id ^ step) * hidden_lanes, hidden_lanes)
        pre = dot_nn(normed_two, b_all[step]) + bias
        value, pull = jax.vjp(exact_gelu, pre)
        hidden.append(value.astype(BF))
        pre_grad.append(pull(dot_nn(grad_branch, c_all[step]))[0].astype(BF))

    def with_partner(rows, parts):
        sent = send_core(jnp.concatenate([rows, parts[1], parts[3]], axis=1))
        split = rows.shape[1], rows.shape[1] + parts[1].shape[1]
        other_rows = sent[:, : split[0]]
        return (
            dot_tn(rows, parts[0]) + dot_tn(other_rows, sent[:, split[0] : split[1]]),
            dot_tn(rows, parts[2]) + dot_tn(other_rows, sent[:, split[1] :]),
        )

    down_grad = scatter_chunk(*with_partner(grad_branch, hidden))
    grad_normed_two = sum(dot_nt(part, weight) for part, weight in zip(pre_grad, b_all))
    up_grad = scatter_chunk(*with_partner(normed_two, pre_grad))

    grad_middle = grad_out + norm_back(grad_normed_two, normal_two, inverse_two, norm_gains[1])
    grad_attn = (norm_gains[2] * grad_middle).astype(BF)
    before = lax.ppermute(grad_attn[-HALO:], "tensor", up_hops)
    after = lax.ppermute(grad_attn[:HALO], "tensor", down_hops)
    grad_attn_ext = jnp.concatenate([before, grad_attn, after], axis=0)
    grad_mixed = [dot_nn(grad_attn_ext, weight).astype(BF) for weight in out_w]
    grad_qkv = run_attention(
        attention_backward_kernel, "attention_backward", bounds, qkv_ext + grad_mixed, 3 * lanes
    )
    grad_qkv = [part[own] for part in grad_qkv]
    grad_normed = sum(
        dot_nt(part, weight[:, : 3 * lanes]) for part, weight in zip(grad_qkv, a_all)
    )
    qkv_pair = with_partner(normed, grad_qkv)
    out_pair = with_partner(grad_attn, mixed)
    a_grad = scatter_chunk(
        *(jnp.concatenate(pair, axis=1) for pair in zip(qkv_pair, out_pair))
    )

    branch_mlp = sum(dot_nt(part, weight) for part, weight in zip(hidden, c_all)) + shifts[5]
    layer_out = (middle + norm_gains[3] * branch_mlp).astype(BF)

    grad_start = grad_middle + norm_back(grad_normed, normal_one, inverse_one, norm_gains[0])
    patch_grad = jnp.where(masked[:, None], 0.0, grad_start)
    token_grad = jnp.sum(jnp.where(masked[:, None], grad_start, 0.0), axis=0)

    def column_sums(parts, at, width):
        return to_absolute([jnp.sum(part[:, at : at + width].astype(F32), axis=0) for part in parts])

    small = jnp.stack(
        [
            jnp.sum(grad_normed * normal_one, axis=0),
            jnp.sum(grad_normed_two * normal_two, axis=0),
            jnp.sum(grad_middle * branch_attn, axis=0),
            jnp.sum(grad_out * branch_mlp, axis=0),
            jnp.sum(grad_normed, axis=0),
            column_sums(grad_qkv, 0, lanes).reshape(-1),
            column_sums(grad_qkv, 2 * lanes, lanes).reshape(-1),
            jnp.sum(grad_attn.astype(F32), axis=0),
            jnp.sum(grad_normed_two, axis=0),
            jnp.sum(grad_branch.astype(F32), axis=0),
            token_grad,
        ]
    )
    small = jnp.concatenate([small, column_sums(pre_grad, 0, hidden_lanes)], axis=0)
    small = sum_everywhere(small)
    gain_total, shift_total = small[:4], small[4:]

    correction = 1.0 - jnp.power(jnp.float32(0.5), step_count[0].astype(F32))
    qkv_owned = jnp.stack([a_grad[:, i * lanes : (i + 1) * lanes] for i in range(3)])
    qkv_res = adamw_step(
        qkv_master, qkv_first, qkv_second, qkv_owned, D ** (-0.5), DECAY, correction
    )
    out_res = adamw_step(
        out_master, out_first, out_second, a_grad[:, 3 * lanes :].T, (D // 16) ** (-0.5), DECAY, correction
    )
    up_res = adamw_step(up_master, up_first, up_second, up_grad, D ** (-0.5), DECAY, correction)
    down_res = adamw_step(
        down_master, down_first, down_second, down_grad.T, FF ** (-0.5), DECAY, correction
    )
    gain_res = adamw_step(norm_gains, gain_first, gain_second, gain_total, 0.1, 0.0, correction)
    shift_res = adamw_step(shifts, shift_first, shift_second, shift_total, 0.3, 0.0, correction)
    return (
        (layer_out, patch_grad) + qkv_res + out_res + up_res + down_res + gain_res + shift_res
    )


def solution(mesh):
    rows = P(("dp", "tensor"), None)
    qkv = (P(None, "dp", "tensor"),)
    tensor_first, dp_first, whole = (P("tensor", "dp"),), (P("dp", "tensor"),), (P(),)
    weights = tuple(
        spec * 3 for spec in (qkv, tensor_first, dp_first, tensor_first)
    )
    results = tuple(
        spec * 4 for spec in (qkv, tensor_first, dp_first, tensor_first)
    )
    return jax.shard_map(
        on_device,
        mesh=mesh,
        in_specs=(rows, rows, P(("dp", "tensor")), P("dp")) + whole * 3 + sum(weights, ()) + whole * 6,
        out_specs=(rows, rows) + sum(results, ()) + whole * 8,
        check_vma=False,
    )
```

```python
import functools

import jax
import jax.numpy as jnp
from jax import lax
from jax.experimental import pallas as pl
from jax.experimental.pallas import tpu as pltpu
from jax.sharding import PartitionSpec as P

D = 768
HEAD_DIM = 64
FF = 3072
BIG_LEN = 197
SMALL_LEN = 101
HALO = 208
ALIGN = 16
BIG_Q, BIG_K = 224, 256
SMALL_W = 128
ROW_BLOCK = 256

EPS_NORM = 1e-06
ADAM_EPS = 1e-08
DECAY = 0.05
NEGATIVE = -1e30
FACTOR = HEAD_DIM ** (-0.5)
BF = jnp.bfloat16
F32 = jnp.float32


def send_dp(value, target):
    count = lax.axis_size("dp")
    return lax.ppermute(value, "dp", [(i, target(i)) for i in range(count)])


def send_x(value):
    return send_dp(value, lambda i: i ^ 1)


def send_tensor(value, mask):
    return lax.ppermute(value, "tensor", [(i, i ^ mask) for i in range(4)])


def send_y(value):
    return send_tensor(value, 2)


def send_core(value):
    return send_tensor(value, 1)


def z_digits():
    left = lax.axis_size("dp") // 2
    stride, digits = 1, []
    while left > 1:
        radix = 4 if left % 4 == 0 else 2
        digits.append((stride, radix))
        stride, left = stride * radix, left // radix
    return digits


def send_digit(value, stride, radix, step):
    def target(i):
        z, x = i // 2, i % 2
        digit = z // stride % radix
        return 2 * (z + ((digit + step) % radix - digit) * stride) + x

    return send_dp(value, target)


def gather_z(block):
    z = lax.axis_index("dp") // 2
    block = block[None]
    for stride, radix in z_digits():
        digit = z // stride % radix
        out = jnp.zeros((radix,) + block.shape, block.dtype)
        out = lax.dynamic_update_slice(out, block[None], (digit, 0, 0, 0))
        pieces = [send_digit(block, stride, radix, step) for step in range(1, radix)]
        for step, piece in enumerate(pieces, 1):
            out = lax.dynamic_update_slice(
                out, piece[None], ((digit + radix - step) % radix, 0, 0, 0)
            )
        block = out.reshape((-1,) + block.shape[1:])
    return block


def scatter_z(partial):
    z = lax.axis_index("dp") // 2
    for stride, radix in reversed(z_digits()):
        digit = z // stride % radix
        parts = partial.reshape((radix, -1) + partial.shape[1:])
        own = lax.dynamic_index_in_dim(parts, digit, 0, keepdims=False)
        pieces = [
            send_digit(
                lax.dynamic_index_in_dim(
                    parts, (digit + step) % radix, 0, keepdims=False
                ).astype(BF),
                stride,
                radix,
                step,
            )
            for step in range(1, radix)
        ]
        for piece in pieces:
            own = own + piece.astype(F32)
        partial = own
    return partial[0]


def interleave(mine, other):
    x = lax.axis_index("dp") % 2
    low = jnp.where(x == 0, mine, other)
    high = jnp.where(x == 0, other, mine)
    return jnp.stack([low, high], axis=1).reshape(-1, mine.shape[-1])


def after(value, *others):
    return lax.optimization_barrier((value, others))[0]


def plane_first(z_all):
    with jax.named_scope("x"):
        from_x = send_x(z_all)
    with jax.named_scope("y1"):
        from_y = send_y(z_all[..., z_all.shape[-1] // 2 :])
    with jax.named_scope("yx"):
        return from_x, from_y, send_x(from_y)


def plane_second(own):
    with jax.named_scope("xy"):
        across = send_y(own[:, : own.shape[1] // 2])
    with jax.named_scope("core0"):
        return across, send_core(own)


def at_x(value, which):
    return lax.dynamic_index_in_dim(value, which, 1, keepdims=False)


def scatter_first(own, across):
    count, n = lax.axis_size("dp"), own.shape[-1]
    half = n // 2
    x = lax.axis_index("dp") % 2
    own = own.reshape(count // 2, 2, -1, n)
    across = across.reshape(count // 2, 2, -1, n)
    far = jnp.stack([at_x(own[..., half:], 1 - x), at_x(across[..., half:], 1 - x)])
    sent = across[..., :half].astype(BF), far.astype(BF)
    kept = own[..., :half], at_x(across[..., half:], x), at_x(own[..., half:], x)
    return sent, kept


def sum_everywhere(value):
    value = value + send_core(value)
    across = send_y(value), send_x(value), send_x(send_y(value))
    value = (value + across[1]) + (across[0] + across[2])
    count = lax.axis_size("dp")
    bit = 2
    while bit < count:
        value = value + send_dp(value, lambda i, b=bit: i ^ b)
        bit *= 2
    return value


def dot_nt(left, right):
    return lax.dot_general(left, right, (((1,), (1,)), ((), ())), preferred_element_type=F32)


def dot_tn(left, right):
    return lax.dot_general(left, right, (((0,), (0,)), ((), ())), preferred_element_type=F32)


def dot_nn(left, right):
    return jnp.dot(left, right, preferred_element_type=F32)


def array(shape, dtype):
    return jax.ShapeDtypeStruct(shape, dtype)


def column_sum(values):
    return jnp.sum(values, axis=0, keepdims=True)


class Fetched:
    def __init__(self, copies, held):
        self.copies, self.held = copies, held

    def __call__(self):
        for copy in self.copies:
            copy.wait()
        self.copies = ()
        return self.held


class Sent:
    def __init__(self, held, target, sem):
        self.held, self.copy, self.started = held, pltpu.make_async_copy(held, target, sem), False

    def done(self):
        if not self.started:
            self.copy.start()
        self.started = True


def call(body, name, scalars, inputs, outputs, scratch=(), temporaries=8):
    groups = [value if isinstance(value, (list, tuple)) else [value] for value in inputs]
    flat = [value for group in groups for value in group]
    held = [
        array((sum(v.shape[0] for v in group),) + group[0].shape[1:], group[0].dtype)
        for group in groups
    ]
    boxes = [pltpu.VMEM(v.shape, v.dtype) for v in held + list(outputs)]
    total = sum(v.size * v.dtype.itemsize for v in held + list(outputs))
    total += sum(v.size * v.dtype.itemsize for v in (array(b[0], b[1]) for b in scratch))

    def kernel(scalar_ref, *refs):
        sources, refs = refs[: len(flat)], refs[len(flat) :]
        targets, refs = refs[: len(outputs)], refs[len(outputs) :]
        in_boxes, refs = refs[: len(groups)], refs[len(groups) :]
        out_boxes, refs = refs[: len(outputs)], refs[len(outputs) :]
        extra, sems = refs[: len(scratch)], refs[-1]
        fetched, at = [], 0
        for group, box in zip(groups, in_boxes):
            row, copies = 0, []
            for value in group:
                rows = value.shape[0]
                part = box if len(group) == 1 else box.at[pl.ds(row, rows)]
                copies.append(pltpu.make_async_copy(sources[at], part, sems.at[at]))
                copies[-1].start()
                row, at = row + rows, at + 1
            fetched.append(Fetched(copies, box))
        sent = [
            Sent(box, target, sems.at[at + i])
            for i, (box, target) in enumerate(zip(out_boxes, targets))
        ]
        body(scalar_ref, fetched, sent, extra)
        for item in fetched:
            item()
        for item in sent:
            item.done()
        for item in sent:
            item.copy.wait()

    return pl.pallas_call(
        kernel,
        name=name,
        in_specs=[pl.BlockSpec(memory_space=pltpu.SMEM)]
        + [pl.BlockSpec(memory_space=pl.ANY)] * len(flat),
        out_specs=[pl.BlockSpec(memory_space=pl.ANY)] * len(outputs),
        out_shape=list(outputs),
        scratch_shapes=boxes
        + [pltpu.VMEM(*box) for box in scratch]
        + [pltpu.SemaphoreType.DMA((len(flat) + len(outputs),))],
        compiler_params=pltpu.CompilerParams(vmem_limit_bytes=total + (temporaries << 20)),
        cost_estimate=pl.CostEstimate(flops=0, transcendentals=0, bytes_accessed=0),
    )(scalars, *flat)


def image_loops(bounds, window):
    big_rows, total = bounds[4], bounds[6]

    def big(index, carry):
        window(index * BIG_LEN, index * BIG_LEN + BIG_LEN, BIG_K, BIG_Q)
        return carry

    def small(index, carry):
        start = big_rows + index * SMALL_LEN
        window(start, jnp.minimum(start + SMALL_LEN, total), SMALL_W, SMALL_W)
        return carry

    lax.fori_loop(bounds[0], bounds[1], big, 0)
    lax.fori_loop(bounds[2], bounds[3], small, 0)


def image_bounds(count_big, first_row, local_rows, total_rows):
    big_rows = count_big * BIG_LEN
    last_row = first_row + local_rows - 1
    big_from = jnp.minimum(first_row // BIG_LEN, count_big)
    big_to = jnp.minimum(last_row // BIG_LEN + 1, count_big)
    small_from = jnp.maximum(first_row - big_rows, 0) // SMALL_LEN
    small_to = jnp.where(last_row >= big_rows, (last_row - big_rows) // SMALL_LEN + 1, small_from)
    base = first_row - HALO
    return jnp.stack(
        [big_from, big_to, small_from, small_to, big_rows, base, jnp.int32(total_rows), base]
    ).astype(jnp.int32)


class Window:
    def __init__(self, start, stop, base, ext_rows, rows, keys):
        aligned = (start - base) // ALIGN * ALIGN
        at_q = pl.multiple_of(jnp.minimum(aligned, ext_rows - rows), ALIGN)
        at_k = pl.multiple_of(jnp.minimum(aligned, ext_rows - keys), ALIGN)

        def inside(offset, shape, axis):
            ids = lax.broadcasted_iota(jnp.int32, shape, axis) + (offset + base)
            return (ids >= start) & (ids < stop)

        self.queries, self.keys = pl.ds(at_q, rows), pl.ds(at_k, keys)
        self.query_across = inside(at_q, (1, rows), 1)
        self.query_down = inside(at_q, (rows, 1), 0)
        self.key_down = inside(at_k, (keys, 1), 0)


def softmax_down(key, query, key_in):
    scores = jnp.where(key_in, dot_nt(key, query), NEGATIVE)
    exps = jnp.exp(scores - jnp.max(scores, axis=0, keepdims=True))
    return exps * (1.0 / jnp.sum(exps, axis=0, keepdims=True))


def attention_forward(bounds, qkv, local_rows, lanes):
    ext_rows = qkv[0].shape[0]

    def body(bounds, ins, outs, mixed_ext):
        qkv = [item() for item in ins]

        def window(start, stop, rows, keys):
            at = Window(start, stop, bounds[5], ext_rows, rows, keys)
            for source, out in zip(qkv, mixed_ext):
                parts = []
                for lane in range(0, lanes, HEAD_DIM):
                    query = source[at.queries, lane : lane + HEAD_DIM] * BF(FACTOR)
                    key = source[at.keys, lanes + lane : lanes + lane + HEAD_DIM]
                    value = source[at.keys, 2 * lanes + lane : 2 * lanes + lane + HEAD_DIM]
                    probs = softmax_down(key, query, at.key_down)
                    parts.append(dot_nn(value.T, probs.astype(BF)))
                mixed = jnp.concatenate(parts, axis=0).T.astype(BF)
                out[at.queries, :] = jnp.where(at.query_down, mixed, out[at.queries, :])

        image_loops(bounds, window)
        for source, out in zip(mixed_ext, outs):
            out.held[...] = source[HALO : HALO + local_rows, :]
            out.done()

    return call(
        body,
        "attention_forward",
        bounds,
        qkv,
        [array((local_rows, lanes), BF)] * 2,
        [((ext_rows, lanes), BF)] * 2,
    )


def attention_backward(bounds, grad_attn, qkv, weights, mixed):
    ext_rows = qkv[0].shape[0]
    local_rows, lanes = mixed[0].shape

    def body(bounds, ins, outs, scratch):
        ext, grads = scratch[:2], scratch[2:]
        grad_attn, weights = ins[0](), [item() for item in ins[1:3]]
        for weight, grad in zip(weights, grads):
            grad[...] = dot_nn(grad_attn[...], weight[:, 3 * lanes :]).astype(BF)
        qkv, mixed = [item() for item in ins[3:5]], [item() for item in ins[5:7]]

        def window(start, stop, rows, keys):
            at = Window(start, stop, bounds[5], ext_rows, rows, keys)
            both = at.key_down & at.query_across
            for source, grad, out in zip(qkv, grads, ext):
                query_parts, key_parts, value_parts = [], [], []
                for lane in range(0, lanes, HEAD_DIM):
                    query = source[at.queries, lane : lane + HEAD_DIM] * BF(FACTOR)
                    key = source[at.keys, lanes + lane : lanes + lane + HEAD_DIM]
                    value = source[at.keys, 2 * lanes + lane : 2 * lanes + lane + HEAD_DIM]
                    grad_rows = grad[at.queries, lane : lane + HEAD_DIM]
                    probs = jnp.where(both, softmax_down(key, query, at.key_down), 0.0)
                    weighted = probs * dot_nt(value, grad_rows)
                    inner = jnp.sum(weighted, axis=0, keepdims=True)
                    grad_scores = (weighted - probs * inner).astype(BF)
                    query_parts.append(dot_nn((key * BF(FACTOR)).T, grad_scores))
                    key_parts.append(dot_nn(grad_scores, query))
                    value_parts.append(dot_nn(probs.astype(BF), grad_rows))
                grad_query = jnp.concatenate(query_parts, axis=0).T.astype(BF)
                old = out[at.queries, :lanes]
                out[at.queries, :lanes] = jnp.where(at.query_down, grad_query, old)
                grad_kv = jnp.concatenate(key_parts + value_parts, axis=1).astype(BF)
                old = out[at.keys, lanes:]
                out[at.keys, lanes:] = jnp.where(at.key_down, grad_kv, old)

        image_loops(bounds, window)
        for source, rows, out in zip(ext, mixed, outs):
            out.held[:, : 3 * lanes] = source[HALO : HALO + local_rows, :]
            out.held[:, 3 * lanes :] = rows[...]
            out.done()

    return call(
        body,
        "attention_backward",
        bounds,
        [grad_attn, *weights, *qkv, *mixed],
        [array((local_rows, 4 * lanes), BF)] * 2,
        [((ext_rows, 3 * lanes), BF)] * 2 + [((ext_rows, lanes), BF)] * 2,
    )


def mlp_up(ids, rows, shifts, weights, first):
    count = len(weights)

    def body(ids, ins, outs, _):
        rows, shifts = ins[0](), ins[1]()
        for i in range(count):
            weight, hidden, slope = ins[2 + i](), outs[i], outs[count + i]

            def block(index, carry):
                at = pl.ds(index * 128, 128)
                pre = dot_nn(rows[at, :], weight[...])
                pre = pre + shifts[pl.ds(7 + (ids[0] ^ (first + i)), 1), :]
                share = 0.5 * (1.0 + lax.erf(pre * 0.5**0.5))
                hidden.held[at, :] = (pre * share).astype(BF)
                density = jnp.exp(-0.5 * pre * pre) * (2.0 * jnp.pi) ** -0.5
                slope.held[at, :] = share + pre * density
                return carry

            lax.fori_loop(0, rows.shape[0] // 128, block, 0)
            hidden.done()
            slope.done()

    shape = (rows.shape[0], weights[0].shape[1])
    outs = call(
        body,
        "mlp_up",
        ids,
        [rows, shifts, *weights],
        [array(shape, BF)] * count + [array(shape, F32)] * count,
    )
    return outs[:count], outs[count:]


def norm_back_rows(grad, rows, gain):
    average = jnp.mean(rows, axis=-1, keepdims=True)
    centered = rows - average
    inverse = lax.rsqrt(jnp.mean(centered * centered, axis=-1, keepdims=True) + EPS_NORM)
    normal = centered * inverse
    scaled = grad * gain
    back = inverse * (
        scaled
        - jnp.mean(scaled, axis=-1, keepdims=True)
        - normal * jnp.mean(scaled * normal, axis=-1, keepdims=True)
    )
    return normal, back


def mlp_back(ids, grad_branch, gains, down, up, slopes, grad_out, middle, branch):
    rows, width = grad_branch.shape
    hidden = up[0].shape[1]

    def body(ids, ins, outs, scratch):
        total, sums = scratch[0], outs[6].held
        grad_branch = ins[0]()
        for i in range(4):
            down, slope, up = ins[5 + i](), ins[9 + i](), ins[13 + i]()
            pre_grads = outs[i]

            def block(index, carry):
                at = pl.ds(index * ROW_BLOCK, ROW_BLOCK)
                back = dot_nn(grad_branch[at, :], down[...])
                pre_grad = (slope[at, :] * back).astype(BF)
                pre_grads.held[at, :] = pre_grad
                product = dot_nt(pre_grad, up[...])
                total[at, :] = product if i == 0 else total[at, :] + product
                return carry + column_sum(pre_grad.astype(F32))

            start = jnp.zeros((1, hidden), F32)
            found = lax.fori_loop(0, rows // ROW_BLOCK, block, start)
            sums[pl.ds(4 + (ids[0] ^ i), 1), :] = found
            pre_grads.done()
        gains, grad_out, middle, branch = (item() for item in ins[1:5])

        def finish(index, carry):
            at = pl.ds(index * 128, 128)
            grad = total[at, :]
            normal, back = norm_back_rows(grad, middle[at, :], gains[1:2, :])
            found = grad_out[at, :] + back
            scaled = (gains[2:3, :] * found).astype(BF)
            outs[4].held[at, :] = found
            outs[5].held[at, :] = scaled
            return (
                carry[0] + column_sum(grad * normal),
                carry[1] + column_sum(grad),
                carry[2] + column_sum(found * branch[at, :]),
                carry[3] + column_sum(scaled.astype(F32)),
            )

        zero = jnp.zeros((1, width), F32)
        found = lax.fori_loop(0, rows // 128, finish, (zero,) * 4)
        for i in range(4):
            sums[i : i + 1, :] = found[i]

    outs = call(
        body,
        "mlp_back",
        ids,
        [grad_branch, gains, grad_out, middle, branch, *down, *slopes, *up],
        [array((rows, hidden), BF)] * 4
        + [array((rows, width), F32), array((rows, width), BF), array((8, width), F32)],
        [((rows, width), F32)],
    )
    return (outs[:4], *outs[4:])


def qkv_back(ids, masked, gains, grads, weights, start, grad_middle, mlp_sums, extra_sums):
    rows, width = start.shape
    lanes = width // 4

    def body(ids, ins, outs, scratch):
        total, sides = scratch
        small = outs[1].held
        grads = [item() for item in ins[2:6]]
        for i in range(4):
            sides[i : i + 1, :] = column_sum(grads[i][:, :lanes].astype(F32))
            sides[4 + i : 5 + i, :] = column_sum(grads[i][:, 2 * lanes : 3 * lanes].astype(F32))
        for i in range(4):
            at = slice(i * lanes, (i + 1) * lanes)
            small[5:6, at] = sides[pl.ds(ids[0] ^ i, 1), :]
            small[6:7, at] = sides[pl.ds(4 + (ids[0] ^ i), 1), :]
        for i in range(4):
            weight = ins[6 + i]()

            def block(index, carry):
                at = pl.ds(index * ROW_BLOCK, ROW_BLOCK)
                product = dot_nt(grads[i][at, : 3 * lanes], weight[:, : 3 * lanes])
                total[at, :] = product if i == 0 else total[at, :] + product
                return carry

            lax.fori_loop(0, rows // ROW_BLOCK, block, 0)
        masked, gains = ins[0](), ins[1]()
        start, grad_middle, mlp_sums, extra_sums = (item() for item in ins[10:14])

        def finish(index, carry):
            at = pl.ds(index * 128, 128)
            grad = total[at, :]
            normal, back = norm_back_rows(grad, start[at, :], gains[0:1, :])
            found = grad_middle[at, :] + back
            hidden = masked[at, 0:1] > 0.5
            outs[0].held[at, :] = jnp.where(hidden, 0.0, found)
            return (
                carry[0] + column_sum(grad * normal),
                carry[1] + column_sum(grad),
                carry[2] + column_sum(jnp.where(hidden, found, 0.0)),
            )

        zero = jnp.zeros((1, width), F32)
        found = lax.fori_loop(0, rows // 128, finish, (zero,) * 3)
        small[0:1, :], small[4:5, :], small[10:11, :] = found
        small[1:2, :], small[2:3, :] = mlp_sums[0:1, :], mlp_sums[2:3, :]
        small[7:8, :], small[8:9, :] = mlp_sums[3:4, :], mlp_sums[1:2, :]
        small[3:4, :], small[9:10, :] = extra_sums[0:1, :], extra_sums[1:2, :]
        small[11:15, :] = mlp_sums[4:8, :]
        small[15:16, :] = zero

    return call(
        body,
        "qkv_back",
        ids,
        [masked, gains, *grads, *weights, start, grad_middle, mlp_sums, extra_sums],
        [array((rows, width), F32), array((16, width), F32)],
        [((rows, width), F32), ((8, lanes), F32)],
    )


def first_hop(ids, lefts, rights, others, segments, count):
    rows, width = lefts[0].shape
    z_count, block = count // 2, width // count
    half = sum(segment[3] for segment in segments[0])
    if block % ALIGN:
        found = []
        for which in range(2):
            parts = [
                dot_tn(lefts[2 * left], rights[2 * right + which][:, lane : lane + n])
                + dot_tn(lefts[2 * left + 1], others[2 * right + which][:, lane : lane + n])
                for color in segments
                for left, right, lane, n in color
            ]
            found.append(jnp.concatenate(parts, axis=1))
        return scatter_first(*found)

    def body(ids, ins, outs, scratch):
        turned, product = scratch
        for i in range(len(lefts)):
            turned[i] = ins[i]()[...].T
        mine = ins[len(lefts) : len(lefts) + len(rights)]
        theirs = ins[len(lefts) + len(rights) :]

        def compute(color, which):
            parts = []
            for left, right, lane, n in segments[color]:
                lanes, pair = slice(lane, lane + n), 2 * right + which
                parts.append(
                    dot_nn(turned[2 * left], mine[pair]()[:, lanes])
                    + dot_nn(turned[2 * left + 1], theirs[pair]()[:, lanes])
                )
            return parts[0] if len(parts) == 1 else jnp.concatenate(parts, axis=1)

        over_y, over_x, low = outs[:3]
        over_y.held[...] = compute(0, 1).astype(BF)
        over_y.done()
        low.held[...] = compute(0, 0)
        low.done()
        for which, kept in ((1, outs[3]), (0, outs[4])):
            product[...] = compute(1, which)
            for z in range(z_count):
                far = pl.multiple_of((2 * z + 1 - ids[1]) * block, ALIGN)
                near = pl.multiple_of((2 * z + ids[1]) * block, ALIGN)
                over_x.held[which, z] = product[pl.ds(far, block), :].astype(BF)
                kept.held[z] = product[pl.ds(near, block), :]
            kept.done()

    high = (z_count, block, half)
    outs = call(
        body,
        "weight_grad",
        ids,
        [*lefts, *rights, *others],
        [
            array((width, half), BF),
            array((2,) + high, BF),
            array((width, half), F32),
            array(high, F32),
            array(high, F32),
        ],
        [((len(lefts), width, rows), BF), ((width, half), F32)],
    )
    return tuple(outs[:2]), tuple(outs[2:])


def second_hop(ids, chunks):
    received = []
    for sent, _ in chunks:
        with jax.named_scope("g1y"):
            over_y = send_y(sent[0])
        with jax.named_scope("g1x"):
            received.append((over_y, send_x(sent[1])))
    shape = chunks[0][1][2].shape
    if len(shape) == 3 and shape[1] % ALIGN == 0:
        z_count, block, half = shape

        def body(ids, ins, outs, _):
            sent_x, kept_low, sent_y, kept_high = outs
            for i in range(len(chunks)):
                low, across_high, own_high, over_y, over_x = (
                    item() for item in ins[5 * i : 5 * i + 5]
                )
                lanes = slice(i * half, (i + 1) * half)
                for z in range(z_count):
                    far = pl.multiple_of((2 * z + 1 - ids[1]) * block, ALIGN)
                    near = pl.multiple_of((2 * z + ids[1]) * block, ALIGN)
                    far, near = pl.ds(far, block), pl.ds(near, block)
                    found = low[far, :] + over_y[far, :].astype(F32)
                    sent_x.held[z, :, lanes] = found.astype(BF)
                    kept_low.held[z, :, lanes] = low[near, :] + over_y[near, :].astype(F32)
                    found = across_high[z] + over_x[1, z].astype(F32)
                    sent_y.held[z, :, lanes] = found.astype(BF)
                    kept_high.held[z, :, lanes] = own_high[z] + over_x[0, z].astype(F32)

        ins = []
        for (_, kept), (over_y, over_x) in zip(chunks, received):
            ins += [*kept, over_y, over_x]
        out = (z_count, block, half * len(chunks))
        outs = call(
            body, "second_hop", ids, ins, [array(out, BF), array(out, F32)] * 2
        )
        return (outs[0], outs[2]), (outs[1], outs[3])
    x = ids[1]
    results = []
    for (_, (low, across_high, own_high)), (over_y, over_x) in zip(chunks, received):
        low = low + over_y.reshape(low.shape).astype(F32)
        high_across = across_high + over_x[1].astype(F32)
        high = own_high + over_x[0].astype(F32)
        results.append((at_x(low, 1 - x).astype(BF), high_across.astype(BF), at_x(low, x), high))
    joined = [jnp.concatenate(parts, axis=-1) for parts in zip(*results)]
    return tuple(joined[:2]), tuple(joined[2:])


def third_hop(ids, sent, kept):
    with jax.named_scope("g2x"):
        over_x = send_x(sent[0])
    with jax.named_scope("g2y"):
        over_y = send_y(sent[1])
    z_count, block, half = kept[0].shape
    if z_count == 4 and block % ALIGN == 0:

        def body(ids, ins, outs, _):
            low, over_x, high, over_y = (item() for item in ins)
            for step, out in enumerate(outs):
                at = lax.rem(ids[2] + step, z_count)
                kind = out.held.dtype
                out.held[:, :half] = (low[at] + over_x[at].astype(F32)).astype(kind)
                out.held[:, half:] = (high[at] + over_y[at].astype(F32)).astype(kind)
                out.done()

        own, *sent = call(
            body,
            "third_hop",
            ids,
            (kept[0], over_x, kept[1], over_y),
            [array((block, 2 * half), F32)] + [array((block, 2 * half), BF)] * 3,
        )
        return tuple(sent), own
    low = kept[0] + over_x.astype(F32)
    high = kept[1] + over_y.astype(F32)
    return (), jnp.concatenate([low, high], axis=-1)


def last_hop(sent, own):
    if not sent:
        return scatter_z(own)
    for step, value in enumerate(sent, 1):
        with jax.named_scope("g3z"):
            own = own + send_digit(value, 1, 4, step).astype(F32)
    return own


def norm_rows(values, gain, shift):
    average = jnp.mean(values, axis=-1, keepdims=True)
    centered = values - average
    inverse = lax.rsqrt(jnp.mean(centered * centered, axis=-1, keepdims=True) + EPS_NORM)
    return centered * inverse * gain + shift


def adamw_step(master, first, second, gradient, rate, decay, correction):
    first_new = 0.5 * first + 0.5 * gradient
    second_new = 0.5 * second + 0.5 * gradient * gradient
    update = first_new / correction / (jnp.sqrt(second_new / correction) + ADAM_EPS)
    master_new = master - rate * (update + decay * master)
    return (master_new, first_new, second_new, master_new.astype(BF))


def on_device(
    patches,
    cotangent,
    mask_rows,
    count_big,
    pos_big,
    pos_small,
    step_count,
    qkv_master,
    qkv_first,
    qkv_second,
    out_master,
    out_first,
    out_second,
    up_master,
    up_first,
    up_second,
    down_master,
    down_first,
    down_second,
    norm_gains,
    gain_first,
    gain_second,
    shifts,
    shift_first,
    shift_second,
):
    tensor_id = lax.axis_index("tensor")
    local_rows = patches.shape[0]
    total_rows = 4 * local_rows
    lanes = qkv_master.shape[2]
    hidden_lanes = up_master.shape[1]
    big_rows = count_big[0] * BIG_LEN
    used_rows = big_rows + (total_rows - big_rows) // SMALL_LEN * SMALL_LEN
    first_row = tensor_id * local_rows

    half = hidden_lanes // 2
    bounds = image_bounds(count_big[0], first_row, local_rows, total_rows)
    dp_id = lax.axis_index("dp")
    ids = jnp.stack([tensor_id, dp_id % 2, dp_id // 2]).astype(jnp.int32)
    own = slice(HALO, HALO + local_rows)

    local_a = jnp.concatenate(
        [qkv_master[0], qkv_master[1], qkv_master[2], out_master.T], axis=1
    ).astype(BF)
    with jax.named_scope("wa"):
        z_a = gather_z(local_a)
    payload = jnp.concatenate(
        [patches, jnp.broadcast_to(mask_rows[:, None].astype(BF), (local_rows, 128))], axis=1
    )
    up_hops, down_hops = [(0, 1), (1, 2), (2, 3)], [(1, 0), (2, 1), (3, 2)]
    with jax.named_scope("halo"):
        halo_before = lax.ppermute(payload[-HALO:], "tensor", up_hops)
        halo_after = lax.ppermute(payload[:HALO], "tensor", down_hops)

    with jax.named_scope("wa"):
        x_a, y_a, yx_a = plane_first(z_a)
    payload = jnp.concatenate([halo_before, payload, halo_after], axis=0)
    ext_rows = payload.shape[0]
    row_ids = first_row - HALO + jnp.arange(ext_rows, dtype=jnp.int32)
    remainder = row_ids - big_rows
    is_big = (row_ids >= 0) & (row_ids < big_rows)
    is_valid = (row_ids >= 0) & (row_ids < used_rows)
    is_small = is_valid & jnp.logical_not(is_big)
    position = jnp.where(is_big, row_ids % BIG_LEN, remainder % SMALL_LEN)
    masked_ext = (payload[:, D] == 1) & is_valid
    pick_big = (
        (position[:, None] == jnp.arange(BIG_LEN, dtype=jnp.int32)[None, :]) & is_big[:, None]
    ).astype(BF)
    pick_small = (
        (position[:, None] == jnp.arange(SMALL_LEN, dtype=jnp.int32)[None, :]) & is_small[:, None]
    ).astype(BF)
    placed = dot_nn(pick_big, pos_big) + dot_nn(pick_small, pos_small)
    start_ext = (
        jnp.where(masked_ext[:, None], shifts[6][None, :], payload[:, :D].astype(F32)) + placed
    )
    normed_ext = norm_rows(start_ext, norm_gains[0], shifts[0]).astype(BF)
    start_rows, masked, valid_local = start_ext[own], masked_ext[own], is_valid[own]
    normed = normed_ext[own]
    grad_out = cotangent.astype(F32) * valid_local[:, None].astype(F32)
    grad_branch = (norm_gains[3] * grad_out).astype(BF)
    local_b, local_c = up_master.astype(BF), down_master.astype(BF).T
    zero_bias = jnp.zeros((lanes,), F32)

    def project(step, weight):
        at = (tensor_id ^ step) * lanes
        bias = jnp.concatenate(
            [
                lax.dynamic_slice_in_dim(shifts[1], at, lanes),
                zero_bias,
                lax.dynamic_slice_in_dim(shifts[2], at, lanes),
                zero_bias,
            ]
        )
        return (dot_nn(normed_ext, weight) + bias).astype(BF)

    own_a = interleave(z_a, x_a)
    xy_a, core_a = plane_second(own_a)
    with jax.named_scope("wb"):
        z_b = gather_z(after(local_b, own_a))
    qkv_ext = [project(0, own_a), project(1, core_a)]
    mixed = attention_forward(bounds, qkv_ext, local_rows, lanes)

    across_a = jnp.concatenate([xy_a, interleave(y_a, yx_a)], axis=1)
    with jax.named_scope("wa/core1"):
        across_core_a = send_core(across_a)
    with jax.named_scope("wb"):
        x_b, y_b, yx_b = plane_first(after(z_b, across_a, mixed))
    with jax.named_scope("wc"):
        z_c = gather_z(after(local_c, z_b, across_a, mixed))
    qkv_ext += [project(2, across_a), project(3, across_core_a)]
    mixed += attention_forward(bounds, qkv_ext[2:], local_rows, lanes)
    a_all = [own_a, core_a, across_a, across_core_a]
    branch_attn = shifts[3] + sum(
        dot_nt(part, weight[:, 3 * lanes :]) for part, weight in zip(mixed, a_all)
    )
    middle = start_rows + norm_gains[2] * branch_attn
    normed_two = norm_rows(middle, norm_gains[1], shifts[4]).astype(BF)

    own_b = interleave(z_b, after(x_b, normed_two))
    with jax.named_scope("wb"):
        xy_b, core_b = plane_second(own_b)
    with jax.named_scope("wc"):
        x_c, y_c, yx_c = plane_first(after(z_c, own_b))
    with jax.named_scope("pair"):
        grad_branch_other = send_core(after(grad_branch, own_b))
        normed_other = send_core(after(normed, own_b))
        normed_two_other = send_core(after(normed_two, own_b))
    hidden, slopes = mlp_up(ids, normed_two, shifts, [own_b, core_b], 0)

    across_b = jnp.concatenate([after(xy_b, hidden), interleave(y_b, yx_b)], axis=1)
    with jax.named_scope("wb/core1"):
        across_core_b = send_core(across_b)
    own_c = interleave(z_c, after(x_c, hidden))
    with jax.named_scope("wc"):
        xy_c, core_c = plane_second(own_c)
    found = mlp_up(ids, normed_two, shifts, [across_b, across_core_b], 2)
    hidden, slopes = hidden + found[0], slopes + found[1]
    b_all = [own_b, core_b, across_b, across_core_b]

    def hop_one(name, lefts, rights, segments):
        with jax.named_scope(name):
            others = [send_core(parts[i + 1]) for parts in rights for i in (0, 2)]
            mine = [parts[i] for parts in rights for i in (0, 2)]
            return first_hop(ids, lefts, mine, others, segments, lax.axis_size("dp"))

    mlp_segments = (((0, 0, 0, half),), ((0, 0, half, half),))
    chunk_c = hop_one("gc", (grad_branch, grad_branch_other), (hidden,), mlp_segments)

    across_c = jnp.concatenate([after(xy_c, chunk_c[0]), interleave(y_c, yx_c)], axis=1)
    with jax.named_scope("wc/core1"):
        across_core_c = send_core(across_c)
    c_all = [own_c, core_c, across_c, across_core_c]

    pre_grad, grad_middle, grad_attn, mlp_sums = mlp_back(
        ids, grad_branch, norm_gains, c_all, b_all, slopes, grad_out, middle, branch_attn
    )
    with jax.named_scope("halo"):
        halo_before = lax.ppermute(grad_attn[-HALO:], "tensor", up_hops)
        halo_after = lax.ppermute(grad_attn[:HALO], "tensor", down_hops)
    with jax.named_scope("pair"):
        grad_attn_other = send_core(grad_attn)
    chunk_b = hop_one("gb", (normed_two, normed_two_other), (pre_grad,), mlp_segments)
    grad_qkv = attention_backward(
        after(bounds, chunk_b[0]),
        (halo_before, grad_attn, halo_after),
        qkv_ext[2:],
        a_all[2:],
        mixed[2:],
    )
    with jax.named_scope("gbc"):
        sent, kept = second_hop(ids, (chunk_c, chunk_b))
    grad_qkv = (
        attention_backward(
            after(bounds, grad_qkv, sent),
            (halo_before, grad_attn, halo_after),
            qkv_ext[:2],
            a_all[:2],
            mixed[:2],
        )
        + grad_qkv
    )
    with jax.named_scope("gbc"):
        sent, sum_bc = third_hop(ids, sent, kept)
    chunk_a = hop_one(
        "ga",
        (normed, normed_other, grad_attn, grad_attn_other),
        (grad_qkv,),
        (((0, 0, 0, 2 * lanes),), ((0, 0, 2 * lanes, lanes), (1, 0, 3 * lanes, lanes))),
    )
    with jax.named_scope("gbc"):
        bc_grad = last_hop(sent, sum_bc)
    width = bc_grad.shape[1] // 4
    down_grad = jnp.concatenate([bc_grad[:, :width], bc_grad[:, 2 * width : 3 * width]], axis=1)
    up_grad = jnp.concatenate([bc_grad[:, width : 2 * width], bc_grad[:, 3 * width :]], axis=1)

    branch_mlp = shifts[5] + sum(dot_nt(part, weight) for part, weight in zip(hidden, c_all))
    layer_out = (middle + norm_gains[3] * branch_mlp).astype(BF)
    extra_sums = jnp.stack(
        [jnp.sum(grad_out * branch_mlp, axis=0), jnp.sum(grad_branch.astype(F32), axis=0)]
    )
    patch_grad, small = qkv_back(
        after(ids, chunk_a[0], sent),
        jnp.broadcast_to(masked[:, None].astype(F32), (local_rows, 128)),
        norm_gains,
        grad_qkv,
        a_all,
        start_rows,
        grad_middle,
        mlp_sums,
        extra_sums,
    )
    with jax.named_scope("ga"):
        sent, kept = second_hop(ids, (chunk_a,))
        last, sum_a = third_hop(ids, sent, kept)
        a_grad = last_hop(last, sum_a)
    with jax.named_scope("small"):
        small = sum_everywhere(after(small, sent))
    gain_total, shift_total = small[:4], small[4:15]

    correction = 1.0 - jnp.power(jnp.float32(0.5), step_count[0].astype(F32))
    qkv_owned = jnp.stack([a_grad[:, i * lanes : (i + 1) * lanes] for i in range(3)])
    qkv_res = adamw_step(
        qkv_master, qkv_first, qkv_second, qkv_owned, D ** (-0.5), DECAY, correction
    )
    out_res = adamw_step(
        out_master, out_first, out_second, after(a_grad[:, 3 * lanes :].T), (D // 16) ** (-0.5), DECAY, correction
    )
    up_res = adamw_step(up_master, up_first, up_second, up_grad, D ** (-0.5), DECAY, correction)
    down_res = adamw_step(
        down_master, down_first, down_second, after(down_grad.T), FF ** (-0.5), DECAY, correction
    )
    gain_res = adamw_step(norm_gains, gain_first, gain_second, gain_total, 0.1, 0.0, correction)
    shift_res = adamw_step(shifts, shift_first, shift_second, shift_total, 0.3, 0.0, correction)
    return (
        (layer_out, patch_grad) + qkv_res + out_res + up_res + down_res + gain_res + shift_res
    )


def solution(mesh):
    rows = P(("dp", "tensor"), None)
    qkv = (P(None, "dp", "tensor"),)
    tensor_first, dp_first, whole = (P("tensor", "dp"),), (P("dp", "tensor"),), (P(),)
    weights = tuple(
        spec * 3 for spec in (qkv, tensor_first, dp_first, tensor_first)
    )
    results = tuple(
        spec * 4 for spec in (qkv, tensor_first, dp_first, tensor_first)
    )
    return jax.shard_map(
        on_device,
        mesh=mesh,
        in_specs=(rows, rows, P(("dp", "tensor")), P("dp")) + whole * 3 + sum(weights, ()) + whole * 6,
        out_specs=(rows, rows) + sum(results, ()) + whole * 8,
        check_vma=False,
    )
```

```python
import functools

import jax
import jax.numpy as jnp
import numpy as np
from jax import lax
from jax.experimental import pallas as pl
from jax.experimental.pallas import tpu as pltpu
from jax.sharding import PartitionSpec as P

D = 768
HEAD_DIM = 64
FF = 3072
BIG_LEN = 197
SMALL_LEN = 101
HALO = 208
ALIGN = 16
PARTS = (0, 2, 1, 3)
BIG_Q, BIG_K = 224, 256
SMALL_W = 128
ROW_BLOCK = 256

EPS_NORM = 1e-06
ADAM_EPS = 1e-08
DECAY = 0.05
NEGATIVE = -1e30
FACTOR = HEAD_DIM ** (-0.5)
BF = jnp.bfloat16
F32 = jnp.float32


def send_dp(value, target):
    count = lax.axis_size("dp")
    return lax.ppermute(value, "dp", [(i, target(i)) for i in range(count)])


def send_x(value):
    return send_dp(value, lambda i: i ^ 1)


def send_tensor(value, mask):
    return lax.ppermute(value, "tensor", [(i, i ^ mask) for i in range(4)])


def send_y(value):
    return send_tensor(value, 2)


def send_core(value):
    return send_tensor(value, 1)


def z_digits():
    left = lax.axis_size("dp") // 2
    stride, digits = 1, []
    while left > 1:
        radix = 4 if left % 4 == 0 else 2
        digits.append((stride, radix))
        stride, left = stride * radix, left // radix
    return digits


def send_digit(value, stride, radix, step):
    def target(i):
        z, x = i // 2, i % 2
        digit = z // stride % radix
        return 2 * (z + ((digit + step) % radix - digit) * stride) + x

    return send_dp(value, target)


def gather_z(block):
    block = block[None]
    digits = z_digits()
    for stride, radix in digits[:-1]:
        pieces = [send_digit(block, stride, radix, step) for step in range(1, radix)]
        block = place([block] + pieces, stride, radix)
    stride, radix = digits[-1]
    return [block] + [send_digit(block, stride, radix, step) for step in range(1, radix)]


def place(parts, stride, radix):
    z = lax.shift_right_logical(lax.axis_index("dp"), 1)
    digit = lax.bitwise_and(lax.div(z, stride), radix - 1)
    out = jnp.zeros((radix,) + parts[0].shape, parts[0].dtype)
    for step, piece in enumerate(parts):
        at = lax.bitwise_and(digit - step, radix - 1)
        out = lax.dynamic_update_slice(out, piece[None], (at, 0, 0, 0))
    return out.reshape((-1,) + parts[0].shape[1:])


def scatter_z(partial):
    z = lax.axis_index("dp") // 2
    for stride, radix in reversed(z_digits()):
        digit = z // stride % radix
        parts = partial.reshape((radix, -1) + partial.shape[1:])
        own = lax.dynamic_index_in_dim(parts, digit, 0, keepdims=False)
        pieces = [
            send_digit(
                lax.dynamic_index_in_dim(
                    parts, (digit + step) % radix, 0, keepdims=False
                ).astype(BF),
                stride,
                radix,
                step,
            )
            for step in range(1, radix)
        ]
        for piece in pieces:
            own = own + piece.astype(F32)
        partial = own
    return partial[0]


def after(value, *others):
    return lax.optimization_barrier((value, others))[0]


def gate(*values):
    return lax.optimization_barrier(values)


def send_far(value):
    count = lax.axis_size("dp")
    pairs = [(4 * i + j, 4 * (i ^ 1) + (j ^ 2)) for i in range(count) for j in range(4)]
    return lax.ppermute(value, ("dp", "tensor"), pairs)


def send_near(to_x, to_y):
    with jax.named_scope("x"):
        from_x = send_x(to_x)
    with jax.named_scope("y"):
        return from_x, send_y(to_y)


def send_plane(to_x, to_y, to_far):
    near = send_near(to_x, to_y)
    with jax.named_scope("far"):
        return (*near, send_far(to_far))


def sum_everywhere(value):
    value = value + send_core(value)
    value = value + send_y(value)
    bit = 1
    while bit < lax.axis_size("dp"):
        value = value + send_dp(value, lambda i, b=bit: i ^ b)
        bit *= 2
    return value


def dot_nt(left, right):
    return lax.dot_general(left, right, (((1,), (1,)), ((), ())), preferred_element_type=F32)


def dot_tn(left, right):
    return lax.dot_general(left, right, (((0,), (0,)), ((), ())), preferred_element_type=F32)


def dot_nn(left, right):
    return jnp.dot(left, right, preferred_element_type=F32)


def array(shape, dtype):
    return jax.ShapeDtypeStruct(shape, dtype)


def column_sum(values):
    return jnp.sum(values, axis=0, keepdims=True)


class Held:
    def __init__(self, held):
        self.held = held

    def __call__(self):
        return self.held

    def done(self, first=None):
        pass


def call(body, name, scalars, inputs, outputs, scratch=(), grant=8, cover=10):
    flat, places = [], []
    for value in inputs:
        group = value if isinstance(value, list) else [value[0] if isinstance(value, tuple) else value]
        places.append([])
        for item in group:
            found = [i for i, other in enumerate(flat) if other is item]
            places[-1].append(found[0] if found else len(flat))
            if not found:
                flat.append(item)
    boxes = [
        pltpu.VMEM((sum(v.shape[0] for v in value),) + value[0].shape[1:], value[0].dtype)
        for value in inputs
        if isinstance(value, list)
    ]

    def kernel(scalar_ref, *refs):
        sources, refs = refs[: len(flat)], refs[len(flat) :]
        targets, refs = refs[: len(outputs)], refs[len(outputs) :]
        joined, extra = iter(refs[: len(boxes)]), refs[len(boxes) :]
        ins = []
        for value, place in zip(inputs, places):
            if isinstance(value, list):
                box, row = next(joined), 0
                for at in place:
                    rows = sources[at].shape[0]
                    box[row : row + rows] = sources[at][...]
                    row += rows
                ins.append(Held(box))
            elif isinstance(value, tuple):
                ins.append(Held(sources[place[0]].at[value[1]]))
            else:
                ins.append(Held(sources[place[0]]))
        body(scalar_ref, ins, [Held(target) for target in targets], extra)

    in_vmem = pl.BlockSpec(memory_space=pltpu.VMEM)
    return pl.pallas_call(
        kernel,
        name=name,
        in_specs=[pl.BlockSpec(memory_space=pltpu.SMEM)] + [in_vmem] * len(flat),
        out_specs=[in_vmem] * len(outputs),
        out_shape=list(outputs),
        scratch_shapes=boxes + [pltpu.VMEM(*box) for box in scratch],
        compiler_params=pltpu.CompilerParams(vmem_limit_bytes=grant << 20),
        cost_estimate=pl.CostEstimate(
            flops=0, transcendentals=0, bytes_accessed=cover * 3 * 10**6
        ),
    )(scalars, *flat)


def move(name, scalars, inputs, outputs, plan):
    def kernel(scalar_ref, *refs):
        pairs = plan(scalar_ref, refs[: len(inputs)], refs[len(inputs) : -1])
        copies = [
            pltpu.make_async_copy(source, target, refs[-1].at[i])
            for i, (source, target) in enumerate(pairs)
        ]
        for copy in copies:
            copy.start()
        for copy in copies:
            copy.wait()

    return pl.pallas_call(
        kernel,
        name=name,
        in_specs=[pl.BlockSpec(memory_space=pltpu.SMEM)]
        + [pl.BlockSpec(memory_space=pl.ANY)] * len(inputs),
        out_specs=[pl.BlockSpec(memory_space=pltpu.VMEM)] * len(outputs),
        out_shape=list(outputs),
        scratch_shapes=[pltpu.SemaphoreType.DMA((len(inputs) * len(outputs),))],
        compiler_params=pltpu.CompilerParams(vmem_limit_bytes=1 << 20),
        cost_estimate=pl.CostEstimate(flops=0, transcendentals=0, bytes_accessed=6 * 10**6),
    )(scalars, *inputs)


def place_z(ids, parts, split=1):
    stride, radix = z_digits()[-1]
    _, rows, n = parts[0].shape
    each = n // split
    if rows % ALIGN or stride != 1:
        whole = place(parts, stride, radix)
        return [whole[..., i * each : (i + 1) * each] for i in range(split)]

    def plan(ids, ins, outs):
        return [
            (
                piece.at[0, :, pl.ds(i * each, each)],
                outs[i].at[lax.bitwise_and(ids[2] - step, radix - 1)],
            )
            for i in range(split)
            for step, piece in enumerate(ins)
        ]

    return move("place_z", ids, parts, [array((radix, rows, each), BF)] * split, plan)


def place_x(ids, mine, from_x, from_y, from_far):
    count, rows, n = mine.shape
    if rows % ALIGN:
        x = ids[1]

        def merge(near, far):
            pair = [jnp.where(x == 0, near, far), jnp.where(x == 0, far, near)]
            return jnp.stack(pair, axis=1).reshape(-1, n)

        return jnp.stack([merge(mine, from_x), merge(from_y, from_far)])

    def plan(ids, ins, outs):
        x = ids[1]
        return [
            (ins[0], outs[0].at[0, :, x]),
            (ins[1], outs[0].at[0, :, 1 - x]),
            (ins[2], outs[0].at[1, :, x]),
            (ins[3], outs[0].at[1, :, 1 - x]),
        ]

    shape = (2, count, 2, rows, n)
    out = move("place_x", ids, [mine, from_x, from_y, from_far], [array(shape, BF)], plan)[0]
    return out.reshape(2, -1, n)


def image_loops(bounds, window):
    big_rows, total = bounds[4], bounds[6]

    def big(index, carry):
        window(index * BIG_LEN, index * BIG_LEN + BIG_LEN, BIG_K, BIG_Q)
        return carry

    def small(index, carry):
        start = big_rows + index * SMALL_LEN
        window(start, jnp.minimum(start + SMALL_LEN, total), SMALL_W, SMALL_W)
        return carry

    lax.fori_loop(bounds[0], bounds[1], big, 0)
    lax.fori_loop(bounds[2], bounds[3], small, 0)


def image_bounds(count_big, first_row, local_rows, total_rows):
    big_rows = count_big * BIG_LEN
    last_row = first_row + local_rows - 1
    big_from = jnp.minimum(first_row // BIG_LEN, count_big)
    big_to = jnp.minimum(last_row // BIG_LEN + 1, count_big)
    small_from = jnp.maximum(first_row - big_rows, 0) // SMALL_LEN
    small_to = jnp.where(last_row >= big_rows, (last_row - big_rows) // SMALL_LEN + 1, small_from)
    base = first_row - HALO
    return jnp.stack(
        [big_from, big_to, small_from, small_to, big_rows, base, jnp.int32(total_rows), base]
    ).astype(jnp.int32)


class Window:
    def __init__(self, start, stop, base, ext_rows, rows, keys):
        aligned = (start - base) // ALIGN * ALIGN
        at_q = pl.multiple_of(jnp.minimum(aligned, ext_rows - rows), ALIGN)
        at_k = pl.multiple_of(jnp.minimum(aligned, ext_rows - keys), ALIGN)

        def inside(offset, shape, axis):
            ids = lax.broadcasted_iota(jnp.int32, shape, axis) + (offset + base)
            return (ids >= start) & (ids < stop)

        self.queries, self.keys = pl.ds(at_q, rows), pl.ds(at_k, keys)
        self.query_across = inside(at_q, (1, rows), 1)
        self.query_down = inside(at_q, (rows, 1), 0)
        self.key_down = inside(at_k, (keys, 1), 0)


def softmax_down(key, query, key_in):
    scores = jnp.where(key_in, dot_nt(key, query), NEGATIVE)
    exps = jnp.exp(scores - jnp.max(scores, axis=0, keepdims=True))
    return exps * (1.0 / jnp.sum(exps, axis=0, keepdims=True))


def attention_block(bounds, rows, weights, biases, start, gains, shifts):
    ext_rows, width = rows.shape
    lanes = width // 4
    local_rows = start.shape[0]

    def body(bounds, ins, outs, _):
        rows, biases = ins[0](), ins[1]()
        held = outs[0].held
        weights = []
        for i, part in enumerate(PARTS):
            weights.append(ins[2 + i // 2]().at[i % 2])

            def project(index, carry):
                at = pl.ds(index * (ext_rows // 2), ext_rows // 2)
                found = dot_nn(rows[at, :], weights[i][:, : 3 * lanes])
                found = found + biases[part : part + 1, : 3 * lanes]
                held[i, at, : 3 * lanes] = found.astype(BF)
                return carry

            lax.fori_loop(0, 2, project, 0)

        def window(start, stop, rows, keys):
            at = Window(start, stop, bounds[5], ext_rows, rows, keys)

            def pair(index, carry):
                for source in (held.at[2 * index], held.at[2 * index + 1]):
                    parts = []
                    for lane in range(0, lanes, HEAD_DIM):
                        query = source[at.queries, lane : lane + HEAD_DIM] * BF(FACTOR)
                        key = source[at.keys, lanes + lane : lanes + lane + HEAD_DIM]
                        value = source[at.keys, 2 * lanes + lane : 2 * lanes + lane + HEAD_DIM]
                        probs = softmax_down(key, query, at.key_down)
                        parts.append(dot_nn(value.T, probs.astype(BF)))
                    mixed = jnp.concatenate(parts, axis=0).T.astype(BF)
                    old = source[at.queries, 3 * lanes :]
                    source[at.queries, 3 * lanes :] = jnp.where(at.query_down, mixed, old)
                return carry

            lax.fori_loop(0, 2, pair, 0)

        image_loops(bounds, window)
        outs[0].done()
        start, gains, shifts = (item() for item in ins[4:7])

        def finish(index, carry):
            at = pl.ds(index * 128, 128)
            ext = pl.ds(HALO + index * 128, 128)
            found = shifts[3:4, :]
            for i in range(4):
                found = found + dot_nt(held[i, ext, 3 * lanes :], weights[i][:, 3 * lanes :])
            outs[1].held[at, :] = found
            found = start[at, :] + gains[2:3, :] * found
            outs[2].held[at, :] = found
            outs[3].held[at, :] = norm_rows(found, gains[1:2, :], shifts[4:5, :]).astype(BF)
            return carry

        lax.fori_loop(0, local_rows // 128, finish, 0)

    return call(
        body,
        "attention_block",
        bounds,
        [rows, biases, *weights, start, gains, shifts],
        [array((4, ext_rows, width), BF)]
        + [array((local_rows, width), F32)] * 2
        + [array((local_rows, width), BF)],
        cover=40,
    )


def attention_backward(bounds, grad_attn, qkv, weights):
    _, ext_rows, width = qkv.shape
    lanes = width // 4
    local_rows = ext_rows - 2 * HALO

    def body(bounds, ins, outs, scratch):
        ext, grads = scratch
        grad_attn = ins[0]()
        for i in range(4):
            weight = ins[1 + i // 2]()
            grads[i] = dot_nn(grad_attn[...], weight[i % 2, :, 3 * lanes :]).astype(BF)
        held = ins[3]()

        def window(start, stop, rows, keys):
            at = Window(start, stop, bounds[5], ext_rows, rows, keys)
            both = at.key_down & at.query_across

            def pair(index, carry):
                for part in (2 * index, 2 * index + 1):
                    source, grad, out = held.at[part], grads.at[part], ext.at[part]
                    query_parts, key_parts, value_parts = [], [], []
                    for lane in range(0, lanes, HEAD_DIM):
                        query = source[at.queries, lane : lane + HEAD_DIM] * BF(FACTOR)
                        key = source[at.keys, lanes + lane : lanes + lane + HEAD_DIM]
                        value = source[at.keys, 2 * lanes + lane : 2 * lanes + lane + HEAD_DIM]
                        grad_rows = grad[at.queries, lane : lane + HEAD_DIM]
                        probs = jnp.where(both, softmax_down(key, query, at.key_down), 0.0)
                        weighted = probs * dot_nt(value, grad_rows)
                        inner = jnp.sum(weighted, axis=0, keepdims=True)
                        grad_scores = (weighted - probs * inner).astype(BF)
                        query_parts.append(dot_nn((key * BF(FACTOR)).T, grad_scores))
                        key_parts.append(dot_nn(grad_scores, query))
                        value_parts.append(dot_nn(probs.astype(BF), grad_rows))
                    grad_query = jnp.concatenate(query_parts, axis=0).T.astype(BF)
                    old = out[at.queries, :lanes]
                    out[at.queries, :lanes] = jnp.where(at.query_down, grad_query, old)
                    grad_kv = jnp.concatenate(key_parts + value_parts, axis=1).astype(BF)
                    old = out[at.keys, lanes:]
                    out[at.keys, lanes:] = jnp.where(at.key_down, grad_kv, old)
                return carry

            lax.fori_loop(0, 2, pair, 0)

        image_loops(bounds, window)
        at = slice(HALO, HALO + local_rows)
        for i in (2, 3, 0, 1):
            out = outs[i // 2]
            out.held[i % 2, :, : 3 * lanes] = ext[i, at, :]
            out.held[i % 2, :, 3 * lanes :] = held[i, at, 3 * lanes :]
            if i % 2:
                out.done()

    return call(
        body,
        "attention_backward",
        bounds,
        [grad_attn, *weights, qkv],
        [array((2, local_rows, width), BF)] * 2,
        [((4, ext_rows, 3 * lanes), BF), ((4, ext_rows, lanes), BF)],
        grant=16,
        cover=40,
    )


def mlp_up(ids, rows, shifts, weights, pair, cover):
    def body(ids, ins, outs, _):
        rows, shifts = ins[0](), ins[1]()
        for i in range(2):
            weight, (hidden, slope) = ins[2 + i](), outs

            def block(index, carry):
                at = pl.ds(index * 128, 128)
                pre = dot_nn(rows[at, :], weight[...])
                pre = pre + shifts[pl.ds(7 + (ids[0] ^ PARTS[2 * pair + i]), 1), :]
                share = 0.5 * (1.0 + lax.erf(pre * 0.5**0.5))
                hidden.held[i, at, :] = (pre * share).astype(BF)
                density = jnp.exp(-0.5 * pre * pre) * (2.0 * jnp.pi) ** -0.5
                slope.held[i, at, :] = share + pre * density
                return carry

            lax.fori_loop(0, rows.shape[0] // 128, block, 0)

    shape = (2, rows.shape[0], weights.shape[2])
    return call(
        body,
        "mlp_up",
        ids,
        [rows, shifts, (weights, 0), (weights, 1)],
        [array(shape, BF), array(shape, F32)],
        cover=cover,
    )


def norm_back_rows(grad, rows, gain):
    average = jnp.mean(rows, axis=-1, keepdims=True)
    centered = rows - average
    inverse = lax.rsqrt(jnp.mean(centered * centered, axis=-1, keepdims=True) + EPS_NORM)
    normal = centered * inverse
    scaled = grad * gain
    back = inverse * (
        scaled
        - jnp.mean(scaled, axis=-1, keepdims=True)
        - normal * jnp.mean(scaled * normal, axis=-1, keepdims=True)
    )
    return normal, back


def mlp_back(ids, grad_branch, gains, down, up, slopes, grad_out, middle, branch):
    rows, width = grad_branch.shape
    hidden = up[0].shape[2]

    def body(ids, ins, outs, scratch):
        total, sums = scratch[0], outs[4].held
        grad_branch = ins[0]()
        for i in range(4):
            down, slope, up = (item() for item in ins[1 + 3 * i : 4 + 3 * i])
            pre_grads = outs[i // 2]

            def block(index, carry):
                at = pl.ds(index * ROW_BLOCK, ROW_BLOCK)
                back = dot_nn(grad_branch[at, :], down[...])
                pre_grad = (slope[at, :] * back).astype(BF)
                pre_grads.held[i % 2, at, :] = pre_grad
                product = dot_nt(pre_grad, up[...])
                total[at, :] = product if i == 0 else total[at, :] + product
                return carry + column_sum(pre_grad.astype(F32))

            start = jnp.zeros((1, hidden), F32)
            found = lax.fori_loop(0, rows // ROW_BLOCK, block, start)
            sums[pl.ds(4 + (ids[0] ^ PARTS[i]), 1), :] = found
            if i % 2:
                pre_grads.done()
        gains, grad_out, middle, branch = (item() for item in ins[13:])

        def finish(index, carry):
            at = pl.ds(index * 128, 128)
            grad = total[at, :]
            normal, back = norm_back_rows(grad, middle[at, :], gains[1:2, :])
            found = grad_out[at, :] + back
            scaled = (gains[2:3, :] * found).astype(BF)
            outs[2].held[at, :] = found
            outs[3].held[at, :] = scaled
            return (
                carry[0] + column_sum(grad * normal),
                carry[1] + column_sum(grad),
                carry[2] + column_sum(found * branch[at, :]),
                carry[3] + column_sum(scaled.astype(F32)),
            )

        zero = jnp.zeros((1, width), F32)
        found = lax.fori_loop(0, rows // 128, finish, (zero,) * 4)
        for i in range(4):
            sums[i : i + 1, :] = found[i]

    outs = call(
        body,
        "mlp_back",
        ids,
        [grad_branch]
        + [(kind[i // 2], i % 2) for i in range(4) for kind in (down, slopes, up)]
        + [gains, grad_out, middle, branch],
        [array((2, rows, hidden), BF)] * 2
        + [array((rows, width), F32), array((rows, width), BF), array((8, width), F32)],
        [((rows, width), F32)],
        grant=10,
        cover=40,
    )
    return (list(outs[:2]), *outs[2:])


def qkv_back(ids, masked, gains, grads, weights, start, grad_middle, mlp_sums):
    rows, width = start.shape
    lanes = width // 4

    def body(ids, ins, outs, scratch):
        total, sides = scratch
        small = outs[1].held
        grads = [ins[2 + i // 2]().at[i % 2] for i in range(4)]
        for i, part in enumerate(PARTS):
            sides[part : part + 1, :] = column_sum(grads[i][:, :lanes].astype(F32))
            found = column_sum(grads[i][:, 2 * lanes : 3 * lanes].astype(F32))
            sides[4 + part : 5 + part, :] = found
        for i in range(4):
            at = slice(i * lanes, (i + 1) * lanes)
            small[5:6, at] = sides[pl.ds(ids[0] ^ i, 1), :]
            small[6:7, at] = sides[pl.ds(4 + (ids[0] ^ i), 1), :]
        for i in range(4):
            weight = ins[4 + i // 2]().at[i % 2]

            def block(index, carry):
                at = pl.ds(index * ROW_BLOCK, ROW_BLOCK)
                product = dot_nt(grads[i][at, : 3 * lanes], weight[:, : 3 * lanes])
                total[at, :] = product if i == 0 else total[at, :] + product
                return carry

            lax.fori_loop(0, rows // ROW_BLOCK, block, 0)
        masked, gains = ins[0](), ins[1]()
        start, grad_middle, mlp_sums = (item() for item in ins[6:9])

        def finish(index, carry):
            at = pl.ds(index * 128, 128)
            grad = total[at, :]
            normal, back = norm_back_rows(grad, start[at, :], gains[0:1, :])
            found = grad_middle[at, :] + back
            hidden = masked[at, 0:1] > 0.5
            outs[0].held[at, :] = jnp.where(hidden, 0.0, found)
            return (
                carry[0] + column_sum(grad * normal),
                carry[1] + column_sum(grad),
                carry[2] + column_sum(jnp.where(hidden, found, 0.0)),
            )

        zero = jnp.zeros((1, width), F32)
        found = lax.fori_loop(0, rows // 128, finish, (zero,) * 3)
        small[0:1, :], small[4:5, :], small[10:11, :] = found
        small[1:2, :], small[2:3, :] = mlp_sums[0:1, :], mlp_sums[2:3, :]
        small[7:8, :], small[8:9, :] = mlp_sums[3:4, :], mlp_sums[1:2, :]
        small[3:4, :], small[9:10, :] = zero, zero
        small[11:15, :] = mlp_sums[4:8, :]
        small[15:16, :] = zero

    return call(
        body,
        "qkv_back",
        ids,
        [masked, gains, *grads, *weights, start, grad_middle, mlp_sums],
        [array((rows, width), F32), array((16, width), F32)],
        [((rows, width), F32), ((8, lanes), F32)],
        grant=10,
        cover=40,
    )


def weight_grad(ids, lefts, right, other, segments):
    rows, width = lefts[0].shape
    count = lax.axis_size("dp")
    z_count, block = count // 2, width // count
    total = right.shape[2]
    if block % ALIGN:
        found = []
        for which in range(2):
            parts = [
                dot_tn(lefts[2 * left], right[which, :, lane : lane + n])
                + dot_tn(lefts[2 * left + 1], other[which, :, lane : lane + n])
                for left, lane, n in segments
            ]
            found.append(jnp.concatenate(parts, axis=1).reshape(z_count, 2, block, total))
        x = ids[1]

        def at_x(value, which):
            return lax.dynamic_index_in_dim(value, which, 1, keepdims=False)

        own, across = found
        sent = at_x(own, 1 - x), at_x(across, x), at_x(across, 1 - x)
        return tuple(value.astype(BF) for value in sent), at_x(own, x)

    def body(ids, ins, outs, scratch):
        turned, product = scratch
        for i in range(len(lefts)):
            turned[i] = ins[i]()[...].T
        right, other = ins[-2](), ins[-1]()
        to_x, to_y, to_far, kept = outs
        for which, near_out, far_out in ((1, to_y, to_far), (0, kept, to_x)):
            for left, lane, n in segments:
                lanes = slice(lane, lane + n)
                product[:, lanes] = dot_nn(
                    turned[2 * left], right[which, :, lanes]
                ) + dot_nn(turned[2 * left + 1], other[which, :, lanes])
            for z in range(z_count):
                far = pl.multiple_of((2 * z + 1 - ids[1]) * block, ALIGN)
                near = pl.multiple_of((2 * z + ids[1]) * block, ALIGN)
                far_out.held[z] = product[pl.ds(far, block), :].astype(BF)
                near_out.held[z] = product[pl.ds(near, block), :].astype(near_out.held.dtype)
            near_out.done()
            far_out.done()

    shape = (z_count, block, total)
    *sent, kept = call(
        body,
        "weight_grad",
        ids,
        [*lefts, right, other],
        [array(shape, BF)] * 3 + [array(shape, F32)],
        [((len(lefts), width, rows), BF), ((width, total), F32)],
        grant=12,
    )
    return tuple(sent), kept


def plane_sum(ids, chunks):
    z_count, block, n = chunks[0][1].shape
    if z_count == 4 and block % ALIGN == 0:

        def body(ids, ins, outs, _):
            for step in (1, 2, 3, 0):
                at = lax.rem(ids[2] + step, z_count)
                for i in range(len(chunks)):
                    found = ins[4 * i]()[at]
                    for item in ins[4 * i + 1 : 4 * i + 4]:
                        found = found + item()[at].astype(F32)
                    out = outs[step].held
                    out[:, i * n : (i + 1) * n] = found.astype(out.dtype)
                outs[step].done()

        shape = (block, n * len(chunks))
        own, *sent = call(
            body,
            "plane_sum",
            ids,
            [value for received, kept in chunks for value in (kept, *received)],
            [array(shape, F32)] + [array(shape, BF)] * 3,
        )
        return tuple(sent), own
    sums = [
        kept + (received[0].astype(F32) + received[1].astype(F32) + received[2].astype(F32))
        for received, kept in chunks
    ]
    return (), jnp.concatenate(sums, axis=-1)


def last_hop(sent, own):
    if not sent:
        return [], scatter_z(own)
    with jax.named_scope("g3z"):
        return [send_digit(value, 1, 4, step) for step, value in enumerate(sent, 1)], own


def adamw_step(master, first, second, gradient, rate, decay, correction):
    first_new = 0.5 * first + 0.5 * gradient
    second_new = 0.5 * second + 0.5 * gradient * gradient
    update = first_new / correction / (jnp.sqrt(second_new / correction) + ADAM_EPS)
    master_new = master - rate * (update + decay * master)
    return (master_new, first_new, second_new, master_new.astype(BF))


def update_weights(ids, correction, received, own, states, rates, pick):
    if own.shape[0] % ALIGN:
        results = []
        for i, (state, rate) in enumerate(zip(states, rates)):
            results += adamw_step(*state, pick(own, i), rate, DECAY, correction[0, 0])
        return results

    def body(ids, ins, outs, scratch):
        correction, total = ins[0]()[0:1, 0:1], scratch[0]
        found = ins[1]()[...]
        for item in ins[2 : 2 + len(received)]:
            found = found + item()[...].astype(F32)
        total[...] = found
        at = 2 + len(received)
        for i, rate in enumerate(rates):
            master, first, second = (item()[...] for item in ins[at + 3 * i : at + 3 * i + 3])
            results = adamw_step(
                master, first, second, pick(total, i), rate, DECAY, correction
            )
            for out, value in zip(outs[4 * i : 4 * i + 4], results):
                out.held[...] = value
                out.done()

    outputs = []
    for state in states:
        outputs += [array(state[0].shape, F32)] * 3 + [array(state[0].shape, BF)]
    flat = [value for state in states for value in state]
    return call(
        body,
        "update_weights",
        ids,
        [correction, own, *received, *flat],
        outputs,
        [(own.shape, F32)],
    )


def pack_weights(ids, qkv_master, out_master):
    count, rows, lanes = qkv_master.shape
    if rows % ALIGN:
        parts = [qkv_master[i] for i in range(count)] + [out_master.T]
        return jnp.concatenate(parts, axis=1).astype(BF)

    def body(ids, ins, outs, _):
        qkv = ins[0]()
        for i in range(count):
            outs[0].held[:, i * lanes : (i + 1) * lanes] = qkv[i].astype(BF)
        outs[0].held[:, count * lanes :] = ins[1]()[...].T.astype(BF)

    return call(
        body,
        "pack_weights",
        ids,
        [qkv_master, out_master],
        [array((rows, (count + 1) * lanes), BF)],
    )[0]


def pack_down(ids, up_master, down_turned):
    rows, width = up_master.shape
    if rows % ALIGN:
        return jnp.concatenate([up_master, down_turned], axis=1).astype(BF)

    def body(ids, ins, outs, _):
        outs[0].held[:, :width] = ins[0]()[...].astype(BF)
        outs[0].held[:, width:] = ins[1]()[...].astype(BF)

    return call(
        body, "pack_down", ids, [up_master, down_turned], [array((rows, 2 * width), BF)]
    )[0]


def norm_rows(values, gain, shift):
    average = jnp.mean(values, axis=-1, keepdims=True)
    centered = values - average
    inverse = lax.rsqrt(jnp.mean(centered * centered, axis=-1, keepdims=True) + EPS_NORM)
    return centered * inverse * gain + shift


def on_device(
    patches,
    cotangent,
    mask_rows,
    count_big,
    pos_big,
    pos_small,
    step_count,
    qkv_master,
    qkv_first,
    qkv_second,
    out_master,
    out_first,
    out_second,
    up_master,
    up_first,
    up_second,
    down_master,
    down_first,
    down_second,
    norm_gains,
    gain_first,
    gain_second,
    shifts,
    shift_first,
    shift_second,
):
    tensor_id = lax.axis_index("tensor")
    local_rows = patches.shape[0]
    total_rows = 4 * local_rows
    lanes = qkv_master.shape[2]
    hidden_lanes = up_master.shape[1]
    big_rows = count_big[0] * BIG_LEN
    used_rows = big_rows + (total_rows - big_rows) // SMALL_LEN * SMALL_LEN
    first_row = tensor_id * local_rows

    half = hidden_lanes // 2
    bounds = image_bounds(count_big[0], first_row, local_rows, total_rows)
    dp_id = lax.axis_index("dp")
    ids = jnp.stack(
        [tensor_id, lax.bitwise_and(dp_id, 1), lax.shift_right_logical(dp_id, 1)]
    ).astype(jnp.int32)
    own = slice(HALO, HALO + local_rows)
    correction = 1.0 - jnp.power(jnp.float32(0.5), step_count[0].astype(F32))

    down_state = (down_master.T, down_first.T, down_second.T)

    local_a = pack_weights(ids, qkv_master, out_master)
    with jax.named_scope("wa"):
        z_a = gather_z(local_a)
    payload = jnp.concatenate(
        [patches, jnp.broadcast_to(mask_rows[:, None].astype(BF), (local_rows, 128))], axis=1
    )
    up_hops, down_hops = [(0, 1), (1, 2), (2, 3)], [(1, 0), (2, 1), (3, 2)]
    with jax.named_scope("halo"):
        halo_before = lax.ppermute(payload[-HALO:], "tensor", up_hops)
        halo_after = lax.ppermute(payload[:HALO], "tensor", down_hops)
    local_bc = pack_down(after(ids, local_a), up_master, down_state[0])

    z_a, halo_before, halo_after, local_bc = gate(z_a, halo_before, halo_after, local_bc)
    (z_a,) = place_z(ids, z_a)
    with jax.named_scope("wa"):
        plane_a = send_plane(z_a, z_a, z_a)
    with jax.named_scope("wbc"):
        z_bc = gather_z(after(local_bc, z_a))
    payload = jnp.concatenate([halo_before, payload, halo_after], axis=0)
    ext_rows = payload.shape[0]
    row_ids = first_row - HALO + jnp.arange(ext_rows, dtype=jnp.int32)
    remainder = row_ids - big_rows
    is_big = (row_ids >= 0) & (row_ids < big_rows)
    is_valid = (row_ids >= 0) & (row_ids < used_rows)
    is_small = is_valid & jnp.logical_not(is_big)
    position = jnp.where(is_big, row_ids % BIG_LEN, remainder % SMALL_LEN)
    masked_ext = (payload[:, D] == 1) & is_valid
    pick_big = (
        (position[:, None] == jnp.arange(BIG_LEN, dtype=jnp.int32)[None, :]) & is_big[:, None]
    ).astype(BF)
    pick_small = (
        (position[:, None] == jnp.arange(SMALL_LEN, dtype=jnp.int32)[None, :]) & is_small[:, None]
    ).astype(BF)
    placed = dot_nn(pick_big, pos_big) + dot_nn(pick_small, pos_small)
    start_ext = (
        jnp.where(masked_ext[:, None], shifts[6][None, :], payload[:, :D].astype(F32)) + placed
    )
    normed_ext = norm_rows(start_ext, norm_gains[0], shifts[0]).astype(BF)
    start_rows, masked, valid_local = start_ext[own], masked_ext[own], is_valid[own]
    normed = normed_ext[own]
    masked = jnp.broadcast_to(masked[:, None].astype(F32), (local_rows, 128))
    grad_out = cotangent.astype(F32) * valid_local[:, None].astype(F32)
    grad_branch = (norm_gains[3] * grad_out).astype(BF)
    biases = jnp.stack(
        [
            jnp.concatenate(
                [
                    lax.dynamic_slice_in_dim(shifts[1], (tensor_id ^ i) * lanes, lanes),
                    jnp.zeros((lanes,), F32),
                    lax.dynamic_slice_in_dim(shifts[2], (tensor_id ^ i) * lanes, lanes),
                    jnp.zeros((lanes,), F32),
                ]
            )
            for i in range(4)
        ]
    )

    z_a, plane_a, z_bc, normed_ext, start_rows, grad_branch, normed, biases = gate(
        z_a, plane_a, z_bc, normed_ext, start_rows, grad_branch, normed, biases
    )
    z_b, z_c = place_z(ids, z_bc, 2)
    with jax.named_scope("wb"):
        plane_b = send_plane(z_b, z_b, z_b)
    own_a = place_x(ids, z_a, *plane_a)
    with jax.named_scope("wa/core"):
        a_all = [own_a, send_core(own_a)]
    with jax.named_scope("pair"):
        grad_branch_other = send_core(grad_branch)
    qkv, branch_attn, middle, normed_two = attention_block(
        after(bounds, z_b), normed_ext, a_all, biases, start_rows, norm_gains, shifts
    )

    plane_b, z_b, z_c, normed_two, grad_branch_other = gate(
        plane_b, z_b, z_c, normed_two, grad_branch_other
    )
    with jax.named_scope("wc"):
        plane_c = send_plane(z_c, z_c, z_c)
    own_b = place_x(ids, z_b, *plane_b)
    with jax.named_scope("wb/core"):
        b_all = [own_b, send_core(own_b)]
    hidden, slopes = zip(
        mlp_up(ids, normed_two, shifts, b_all[0], 0, 40),
        mlp_up(ids, normed_two, shifts, b_all[1], 1, 0),
    )
    with jax.named_scope("gc"):
        hidden_other = send_core(hidden[1])
    plane_c, normed_two, hidden, hidden_other = gate(plane_c, normed_two, hidden, hidden_other)
    own_c = place_x(ids, z_c, *plane_c)
    with jax.named_scope("wc/core"):
        c_all = [own_c, send_core(own_c)]
    with jax.named_scope("pair"):
        normed_two_other = send_core(normed_two)
    chunk_c = weight_grad(
        ids,
        (grad_branch, grad_branch_other),
        hidden[0],
        hidden_other,
        ((0, 0, half), (0, half, half)),
    )

    chunk_c, c_all, grad_branch, normed_two_other = gate(
        chunk_c, c_all, grad_branch, normed_two_other
    )
    with jax.named_scope("gc"):
        near_c = send_near(*chunk_c[0][:2])
    pre_grad, grad_middle, grad_attn, mlp_sums = mlp_back(
        ids, grad_branch, norm_gains, c_all, b_all, slopes, grad_out, middle, branch_attn
    )
    near_c, pre_grad, grad_attn = gate(near_c, pre_grad, grad_attn)
    with jax.named_scope("gb"):
        pre_grad_other = send_core(pre_grad[1])
    with jax.named_scope("halo"):
        halo_before = lax.ppermute(grad_attn[-HALO:], "tensor", up_hops)
        halo_after = lax.ppermute(grad_attn[:HALO], "tensor", down_hops)
    chunk_b = weight_grad(
        ids,
        (normed_two, normed_two_other),
        pre_grad[0],
        pre_grad_other,
        ((0, 0, half), (0, half, half)),
    )
    halo_before, halo_after, chunk_b, grad_attn, normed = gate(
        halo_before, halo_after, chunk_b, grad_attn, normed
    )
    with jax.named_scope("gc/far"):
        far_c = send_far(chunk_c[0][2])
    with jax.named_scope("gb"):
        near_b = send_near(*chunk_b[0][:2])
    with jax.named_scope("pair"):
        grad_attn_other, normed_other = send_core(grad_attn), send_core(normed)
    grad_qkv = attention_backward(
        after(bounds, chunk_b[0]), [halo_before, grad_attn, halo_after], qkv, a_all
    )
    far_c, near_b, grad_qkv, grad_attn_other, normed_other = gate(
        far_c, near_b, grad_qkv, grad_attn_other, normed_other
    )
    with jax.named_scope("ga"):
        grad_qkv_other = send_core(grad_qkv[1])
    with jax.named_scope("gb/far"):
        far_b = send_far(chunk_b[0][2])
    chunk_a = weight_grad(
        ids,
        (normed, normed_other, grad_attn, grad_attn_other),
        grad_qkv[0],
        grad_qkv_other,
        ((0, 0, 2 * lanes), (0, 2 * lanes, lanes), (1, 3 * lanes, lanes)),
    )
    chunk_a, grad_qkv = gate(chunk_a, grad_qkv)
    with jax.named_scope("ga"):
        plane_a = send_plane(*chunk_a[0])
    with jax.named_scope("gbc"):
        sent, sum_bc = plane_sum(
            after(ids, chunk_a[0]),
            (((*near_c, far_c), chunk_c[1]), ((*near_b, far_b), chunk_b[1])),
        )
        last_bc, sum_bc = last_hop(sent, sum_bc)
    patch_grad, small = qkv_back(
        after(ids, sent), masked, norm_gains, grad_qkv, a_all, start_rows, grad_middle, mlp_sums
    )
    hidden = after(hidden, sent)
    branch_mlp = shifts[5] + sum(
        dot_nt(hidden[i // 2][i % 2], c_all[i // 2][i % 2]) for i in range(4)
    )
    layer_out = (middle + norm_gains[3] * branch_mlp).astype(BF)
    extra = [jnp.sum(grad_out * branch_mlp, axis=0), jnp.sum(grad_branch.astype(F32), axis=0)]
    plane_a, small, layer_out, extra, early = gate(
        plane_a, small, layer_out, extra, last_bc[:2]
    )
    last_bc = list(early) + list(last_bc[2:])
    with jax.named_scope("ga"):
        sent, sum_a = plane_sum(ids, ((plane_a, chunk_a[1]),))
        last_a, sum_a = last_hop(sent, sum_a)
    is_row = [lax.broadcasted_iota(jnp.int32, small.shape, 0) == row for row in (3, 9)]
    small = jnp.where(is_row[0], extra[0], jnp.where(is_row[1], extra[1], small))
    with jax.named_scope("small"):
        small = sum_everywhere(after(small, sent))
    gain_res = adamw_step(norm_gains, gain_first, gain_second, small[:4], 0.1, 0.0, correction)
    shift_res = adamw_step(shifts, shift_first, shift_second, small[4:15], 0.3, 0.0, correction)
    correction = jnp.broadcast_to(correction, (8, 128))
    middle_lane = sum_bc.shape[1] // 2

    def pick_bc(total, i):
        return total[:, middle_lane:] if i == 0 else total[:, :middle_lane]

    def pick_a(total, i):
        if i == 1:
            return total[:, 3 * lanes :].T
        return jnp.stack([total[:, at * lanes : (at + 1) * lanes] for at in range(3)])

    up_down = update_weights(
        after(ids, sent, sum_a),
        correction,
        last_bc,
        sum_bc,
        ((up_master, up_first, up_second), down_state),
        (D ** (-0.5), FF ** (-0.5)),
        pick_bc,
    )
    qkv_out = update_weights(
        after(ids, up_down),
        correction,
        last_a,
        sum_a,
        ((qkv_master, qkv_first, qkv_second), (out_master, out_first, out_second)),
        (D ** (-0.5), (D // 16) ** (-0.5)),
        pick_a,
    )
    down_out = [value.T for value in up_down[4:]]
    return (layer_out, patch_grad, *qkv_out, *up_down[:4], *down_out, *gain_res, *shift_res)


def solution(mesh):
    rows = P(("dp", "tensor"), None)
    qkv = (P(None, "dp", "tensor"),)
    tensor_first, dp_first, whole = (P("tensor", "dp"),), (P("dp", "tensor"),), (P(),)
    weights = tuple(
        spec * 3 for spec in (qkv, tensor_first, dp_first, tensor_first)
    )
    results = tuple(
        spec * 4 for spec in (qkv, tensor_first, dp_first, tensor_first)
    )
    return jax.shard_map(
        on_device,
        mesh=mesh,
        in_specs=(rows, rows, P(("dp", "tensor")), P("dp")) + whole * 3 + sum(weights, ()) + whole * 6,
        out_specs=(rows, rows) + sum(results, ()) + whole * 8,
        check_vma=False,
    )
```

```python
import functools

import jax
import jax.numpy as jnp
import numpy as np
from jax import lax
from jax.experimental import pallas as pl
from jax.experimental.pallas import tpu as pltpu
from jax.sharding import PartitionSpec as P

D = 768
HEAD_DIM = 64
FF = 3072
BIG_LEN = 197
SMALL_LEN = 101
HALO = 208
ALIGN = 16
PARTS = (0, 2, 1, 3)
BIG_Q, BIG_K = 224, 256
SMALL_W = 128
ROW_BLOCK = 256

EPS_NORM = 1e-06
ADAM_EPS = 1e-08
DECAY = 0.05
NEGATIVE = -1e30
FACTOR = HEAD_DIM ** (-0.5)
BF = jnp.bfloat16
F32 = jnp.float32


def send_dp(value, target):
    count = lax.axis_size("dp")
    return lax.ppermute(value, "dp", [(i, target(i)) for i in range(count)])


def send_x(value):
    return send_dp(value, lambda i: i ^ 1)


def send_tensor(value, mask):
    return lax.ppermute(value, "tensor", [(i, i ^ mask) for i in range(4)])


def send_y(value):
    return send_tensor(value, 2)


def send_core(value):
    return send_tensor(value, 1)


def z_digits():
    left = lax.axis_size("dp") // 2
    stride, digits = 1, []
    while left > 1:
        radix = 4 if left % 4 == 0 else 2
        digits.append((stride, radix))
        stride, left = stride * radix, left // radix
    return digits


def send_digit(value, stride, radix, step):
    def target(i):
        z, x = i // 2, i % 2
        digit = z // stride % radix
        return 2 * (z + ((digit + step) % radix - digit) * stride) + x

    return send_dp(value, target)


def gather_z(block):
    block = block[None]
    digits = z_digits()
    for stride, radix in digits[:-1]:
        pieces = [send_digit(block, stride, radix, step) for step in range(1, radix)]
        block = place([block] + pieces, stride, radix)
    stride, radix = digits[-1]
    return [block] + [send_digit(block, stride, radix, step) for step in range(1, radix)]


def place(parts, stride, radix):
    z = lax.shift_right_logical(lax.axis_index("dp"), 1)
    digit = lax.bitwise_and(lax.div(z, stride), radix - 1)
    out = jnp.zeros((radix,) + parts[0].shape, parts[0].dtype)
    for step, piece in enumerate(parts):
        at = lax.bitwise_and(digit - step, radix - 1)
        out = lax.dynamic_update_slice(out, piece[None], (at, 0, 0, 0))
    return out.reshape((-1,) + parts[0].shape[1:])


def scatter_z(partial):
    z = lax.axis_index("dp") // 2
    for stride, radix in reversed(z_digits()):
        digit = z // stride % radix
        parts = partial.reshape((radix, -1) + partial.shape[1:])
        own = lax.dynamic_index_in_dim(parts, digit, 0, keepdims=False)
        pieces = [
            send_digit(
                lax.dynamic_index_in_dim(
                    parts, (digit + step) % radix, 0, keepdims=False
                ).astype(BF),
                stride,
                radix,
                step,
            )
            for step in range(1, radix)
        ]
        for piece in pieces:
            own = own + piece.astype(F32)
        partial = own
    return partial[0]


def after(value, *others):
    return lax.optimization_barrier((value, others))[0]


def gate(*values):
    return lax.optimization_barrier(values)


def send_far(value):
    count = lax.axis_size("dp")
    pairs = [(4 * i + j, 4 * (i ^ 1) + (j ^ 2)) for i in range(count) for j in range(4)]
    return lax.ppermute(value, ("dp", "tensor"), pairs)


def send_near(to_x, to_y):
    with jax.named_scope("x"):
        from_x = send_x(to_x)
    with jax.named_scope("y"):
        return from_x, send_y(to_y)


def send_first(to_y, to_x):
    with jax.named_scope("g1y"):
        from_y = send_y(to_y)
    with jax.named_scope("g1x"):
        return from_y, send_x(to_x)


def send_second(to_x, to_y):
    with jax.named_scope("g2x"):
        from_x = send_x(to_x)
    with jax.named_scope("g2y"):
        return from_x, send_y(to_y)


def send_plane(to_x, to_y, to_far):
    near = send_near(to_x, to_y)
    with jax.named_scope("far"):
        return (*near, send_far(to_far))


def sum_over_z(value):
    bit = 2
    while bit < lax.axis_size("dp"):
        value = value + send_dp(value, lambda i, b=bit: i ^ b)
        bit *= 2
    return value


def sum_over_plane(value):
    for send in (send_core, send_y, send_x):
        value = value + send(value)
    return value


def dot_nt(left, right):
    return lax.dot_general(left, right, (((1,), (1,)), ((), ())), preferred_element_type=F32)


def dot_tn(left, right):
    return lax.dot_general(left, right, (((0,), (0,)), ((), ())), preferred_element_type=F32)


def dot_nn(left, right):
    return jnp.dot(left, right, preferred_element_type=F32)


def array(shape, dtype):
    return jax.ShapeDtypeStruct(shape, dtype)


def column_sum(values):
    return jnp.sum(values, axis=0, keepdims=True)


class Held:
    def __init__(self, held):
        self.held = held

    def __call__(self):
        return self.held

    def done(self, first=None):
        pass


def call(body, name, scalars, inputs, outputs, scratch=(), grant=8, cover=10):
    flat, places = [], []
    for value in inputs:
        group = value if isinstance(value, list) else [value[0] if isinstance(value, tuple) else value]
        places.append([])
        for item in group:
            found = [i for i, other in enumerate(flat) if other is item]
            places[-1].append(found[0] if found else len(flat))
            if not found:
                flat.append(item)
    boxes = [
        pltpu.VMEM((sum(v.shape[0] for v in value),) + value[0].shape[1:], value[0].dtype)
        for value in inputs
        if isinstance(value, list)
    ]

    def kernel(scalar_ref, *refs):
        sources, refs = refs[: len(flat)], refs[len(flat) :]
        targets, refs = refs[: len(outputs)], refs[len(outputs) :]
        joined, extra = iter(refs[: len(boxes)]), refs[len(boxes) :]
        ins = []
        for value, place in zip(inputs, places):
            if isinstance(value, list):
                box, row = next(joined), 0
                for at in place:
                    rows = sources[at].shape[0]
                    box[row : row + rows] = sources[at][...]
                    row += rows
                ins.append(Held(box))
            elif isinstance(value, tuple):
                ins.append(Held(sources[place[0]].at[value[1]]))
            else:
                ins.append(Held(sources[place[0]]))
        body(scalar_ref, ins, [Held(target) for target in targets], extra)

    in_vmem = pl.BlockSpec(memory_space=pltpu.VMEM)
    return pl.pallas_call(
        kernel,
        name=name,
        in_specs=[pl.BlockSpec(memory_space=pltpu.SMEM)] + [in_vmem] * len(flat),
        out_specs=[in_vmem] * len(outputs),
        out_shape=list(outputs),
        scratch_shapes=boxes + [pltpu.VMEM(*box) for box in scratch],
        compiler_params=pltpu.CompilerParams(vmem_limit_bytes=grant << 20),
        cost_estimate=pl.CostEstimate(
            flops=0, transcendentals=0, bytes_accessed=cover * 3 * 10**6
        ),
    )(scalars, *flat)


def move(name, scalars, inputs, outputs, plan, cover=2):
    def kernel(scalar_ref, *refs):
        pairs = plan(scalar_ref, refs[: len(inputs)], refs[len(inputs) : -1])
        copies = [
            pltpu.make_async_copy(source, target, refs[-1].at[i])
            for i, (source, target) in enumerate(pairs)
        ]
        for copy in copies:
            copy.start()
        for copy in copies:
            copy.wait()

    return pl.pallas_call(
        kernel,
        name=name,
        in_specs=[pl.BlockSpec(memory_space=pltpu.SMEM)]
        + [pl.BlockSpec(memory_space=pl.ANY)] * len(inputs),
        out_specs=[pl.BlockSpec(memory_space=pltpu.VMEM)] * len(outputs),
        out_shape=list(outputs),
        scratch_shapes=[pltpu.SemaphoreType.DMA((len(inputs) * len(outputs),))],
        compiler_params=pltpu.CompilerParams(vmem_limit_bytes=1 << 20),
        cost_estimate=pl.CostEstimate(flops=0, transcendentals=0, bytes_accessed=cover * 3 * 10**6),
    )(scalars, *inputs)


def place_z(ids, parts, split=1):
    stride, radix = z_digits()[-1]
    _, rows, n = parts[0].shape
    each = n // split
    if rows % ALIGN or stride != 1:
        whole = place(parts, stride, radix)
        return [whole[..., i * each : (i + 1) * each] for i in range(split)]

    def plan(ids, ins, outs):
        return [
            (
                piece.at[0, :, pl.ds(i * each, each)],
                outs[i].at[lax.bitwise_and(ids[2] - step, radix - 1)],
            )
            for i in range(split)
            for step, piece in enumerate(ins)
        ]

    return move("place_z", ids, parts, [array((radix, rows, each), BF)] * split, plan)


def place_x(ids, mine, from_x, from_y, from_far, cover=2):
    count, rows, n = mine.shape
    if rows % ALIGN:
        x = ids[1]

        def merge(near, far):
            pair = [jnp.where(x == 0, near, far), jnp.where(x == 0, far, near)]
            return jnp.stack(pair, axis=1).reshape(-1, n)

        return jnp.stack([merge(mine, from_x), merge(from_y, from_far)])

    def plan(ids, ins, outs):
        x = ids[1]
        return [
            (ins[0], outs[0].at[0, :, x]),
            (ins[1], outs[0].at[0, :, 1 - x]),
            (ins[2], outs[0].at[1, :, x]),
            (ins[3], outs[0].at[1, :, 1 - x]),
        ]

    shape = (2, count, 2, rows, n)
    inputs = [mine, from_x, from_y, from_far]
    out = move("place_x", ids, inputs, [array(shape, BF)], plan, cover)[0]
    return out.reshape(2, -1, n)


def image_loops(bounds, window):
    big_rows, total = bounds[4], bounds[6]

    def big(index, carry):
        window(index * BIG_LEN, index * BIG_LEN + BIG_LEN, BIG_K, BIG_Q)
        return carry

    def small(index, carry):
        start = big_rows + index * SMALL_LEN
        window(start, jnp.minimum(start + SMALL_LEN, total), SMALL_W, SMALL_W)
        return carry

    lax.fori_loop(bounds[0], bounds[1], big, 0)
    lax.fori_loop(bounds[2], bounds[3], small, 0)


def image_bounds(count_big, first_row, local_rows, total_rows):
    big_rows = count_big * BIG_LEN
    last_row = first_row + local_rows - 1
    big_from = jnp.minimum(first_row // BIG_LEN, count_big)
    big_to = jnp.minimum(last_row // BIG_LEN + 1, count_big)
    small_from = jnp.maximum(first_row - big_rows, 0) // SMALL_LEN
    small_to = jnp.where(last_row >= big_rows, (last_row - big_rows) // SMALL_LEN + 1, small_from)
    base = first_row - HALO
    return jnp.stack(
        [big_from, big_to, small_from, small_to, big_rows, base, jnp.int32(total_rows), base]
    ).astype(jnp.int32)


class Window:
    def __init__(self, start, stop, base, ext_rows, rows, keys):
        aligned = (start - base) // ALIGN * ALIGN
        at_q = pl.multiple_of(jnp.minimum(aligned, ext_rows - rows), ALIGN)
        at_k = pl.multiple_of(jnp.minimum(aligned, ext_rows - keys), ALIGN)

        def inside(offset, shape, axis):
            ids = lax.broadcasted_iota(jnp.int32, shape, axis) + (offset + base)
            return (ids >= start) & (ids < stop)

        self.queries, self.keys = pl.ds(at_q, rows), pl.ds(at_k, keys)
        self.query_across = inside(at_q, (1, rows), 1)
        self.query_down = inside(at_q, (rows, 1), 0)
        self.key_down = inside(at_k, (keys, 1), 0)


def softmax_down(key, query, key_in):
    scores = jnp.where(key_in, dot_nt(key, query), NEGATIVE)
    exps = jnp.exp(scores - jnp.max(scores, axis=0, keepdims=True))
    return exps * (1.0 / jnp.sum(exps, axis=0, keepdims=True))


def attention_block(bounds, rows, weights, biases, start, gains, shifts):
    ext_rows, width = rows.shape
    lanes = width // 4
    local_rows = start.shape[0]

    def body(bounds, ins, outs, _):
        rows, biases = ins[0](), ins[1]()
        held = outs[0].held
        weights = []
        for i, part in enumerate(PARTS):
            weights.append(ins[2 + i // 2]().at[i % 2])

            def project(index, carry):
                at = pl.ds(index * (ext_rows // 2), ext_rows // 2)
                found = dot_nn(rows[at, :], weights[i][:, : 3 * lanes])
                found = found + biases[part : part + 1, : 3 * lanes]
                held[i, at, : 3 * lanes] = found.astype(BF)
                return carry

            lax.fori_loop(0, 2, project, 0)

        def window(start, stop, rows, keys):
            at = Window(start, stop, bounds[5], ext_rows, rows, keys)

            def pair(index, carry):
                for source in (held.at[2 * index], held.at[2 * index + 1]):
                    parts = []
                    for lane in range(0, lanes, HEAD_DIM):
                        query = source[at.queries, lane : lane + HEAD_DIM] * BF(FACTOR)
                        key = source[at.keys, lanes + lane : lanes + lane + HEAD_DIM]
                        value = source[at.keys, 2 * lanes + lane : 2 * lanes + lane + HEAD_DIM]
                        probs = softmax_down(key, query, at.key_down)
                        parts.append(dot_nn(value.T, probs.astype(BF)))
                    mixed = jnp.concatenate(parts, axis=0).T.astype(BF)
                    old = source[at.queries, 3 * lanes :]
                    source[at.queries, 3 * lanes :] = jnp.where(at.query_down, mixed, old)
                return carry

            lax.fori_loop(0, 2, pair, 0)

        image_loops(bounds, window)
        outs[0].done()
        start, gains, shifts = (item() for item in ins[4:7])

        def finish(index, carry):
            at = pl.ds(index * 128, 128)
            ext = pl.ds(HALO + index * 128, 128)
            found = shifts[3:4, :]
            for i in range(4):
                found = found + dot_nt(held[i, ext, 3 * lanes :], weights[i][:, 3 * lanes :])
            outs[1].held[at, :] = found
            found = start[at, :] + gains[2:3, :] * found
            outs[2].held[at, :] = found
            outs[3].held[at, :] = norm_rows(found, gains[1:2, :], shifts[4:5, :]).astype(BF)
            return carry

        lax.fori_loop(0, local_rows // 128, finish, 0)

    return call(
        body,
        "attention_block",
        bounds,
        [rows, biases, *weights, start, gains, shifts],
        [array((4, ext_rows, width), BF)]
        + [array((local_rows, width), F32)] * 2
        + [array((local_rows, width), BF)],
        cover=40,
    )


def attention_backward(bounds, grad_attn, qkv, weights):
    _, ext_rows, width = qkv.shape
    lanes = width // 4
    local_rows = ext_rows - 2 * HALO

    def body(bounds, ins, outs, scratch):
        ext, grads = scratch
        grad_attn = ins[0]()
        for i in range(4):
            weight = ins[1 + i // 2]()
            grads[i] = dot_nn(grad_attn[...], weight[i % 2, :, 3 * lanes :]).astype(BF)
        held = ins[3]()

        def window(start, stop, rows, keys):
            at = Window(start, stop, bounds[5], ext_rows, rows, keys)
            both = at.key_down & at.query_across

            def pair(index, carry):
                for part in (2 * index, 2 * index + 1):
                    source, grad, out = held.at[part], grads.at[part], ext.at[part]
                    query_parts, key_parts, value_parts = [], [], []
                    for lane in range(0, lanes, HEAD_DIM):
                        query = source[at.queries, lane : lane + HEAD_DIM] * BF(FACTOR)
                        key = source[at.keys, lanes + lane : lanes + lane + HEAD_DIM]
                        value = source[at.keys, 2 * lanes + lane : 2 * lanes + lane + HEAD_DIM]
                        grad_rows = grad[at.queries, lane : lane + HEAD_DIM]
                        probs = jnp.where(both, softmax_down(key, query, at.key_down), 0.0)
                        weighted = probs * dot_nt(value, grad_rows)
                        inner = jnp.sum(weighted, axis=0, keepdims=True)
                        grad_scores = (weighted - probs * inner).astype(BF)
                        query_parts.append(dot_nn((key * BF(FACTOR)).T, grad_scores))
                        key_parts.append(dot_nn(grad_scores, query))
                        value_parts.append(dot_nn(probs.astype(BF), grad_rows))
                    grad_query = jnp.concatenate(query_parts, axis=0).T.astype(BF)
                    old = out[at.queries, :lanes]
                    out[at.queries, :lanes] = jnp.where(at.query_down, grad_query, old)
                    grad_kv = jnp.concatenate(key_parts + value_parts, axis=1).astype(BF)
                    old = out[at.keys, lanes:]
                    out[at.keys, lanes:] = jnp.where(at.key_down, grad_kv, old)
                return carry

            lax.fori_loop(0, 2, pair, 0)

        image_loops(bounds, window)
        at = slice(HALO, HALO + local_rows)
        for i in (2, 3, 0, 1):
            out = outs[i // 2]
            out.held[i % 2, :, : 3 * lanes] = ext[i, at, :]
            out.held[i % 2, :, 3 * lanes :] = held[i, at, 3 * lanes :]
            if i % 2:
                out.done()

    return call(
        body,
        "attention_backward",
        bounds,
        [grad_attn, *weights, qkv],
        [array((2, local_rows, width), BF)] * 2,
        [((4, ext_rows, 3 * lanes), BF), ((4, ext_rows, lanes), BF)],
        grant=16,
        cover=40,
    )


def mlp_up(ids, rows, shifts, weights, pair, cover):
    def body(ids, ins, outs, _):
        rows, shifts = ins[0](), ins[1]()
        for i in range(2):
            weight, (hidden, slope) = ins[2 + i](), outs

            def block(index, carry):
                at = pl.ds(index * 128, 128)
                pre = dot_nn(rows[at, :], weight[...])
                pre = pre + shifts[pl.ds(7 + (ids[0] ^ PARTS[2 * pair + i]), 1), :]
                share = 0.5 * (1.0 + lax.erf(pre * 0.5**0.5))
                hidden.held[i, at, :] = (pre * share).astype(BF)
                density = jnp.exp(-0.5 * pre * pre) * (2.0 * jnp.pi) ** -0.5
                slope.held[i, at, :] = share + pre * density
                return carry

            lax.fori_loop(0, rows.shape[0] // 128, block, 0)

    shape = (2, rows.shape[0], weights.shape[2])
    return call(
        body,
        "mlp_up",
        ids,
        [rows, shifts, (weights, 0), (weights, 1)],
        [array(shape, BF), array(shape, F32)],
        cover=cover,
    )


def norm_back_rows(grad, rows, gain):
    average = jnp.mean(rows, axis=-1, keepdims=True)
    centered = rows - average
    inverse = lax.rsqrt(jnp.mean(centered * centered, axis=-1, keepdims=True) + EPS_NORM)
    normal = centered * inverse
    scaled = grad * gain
    back = inverse * (
        scaled
        - jnp.mean(scaled, axis=-1, keepdims=True)
        - normal * jnp.mean(scaled * normal, axis=-1, keepdims=True)
    )
    return normal, back


def mlp_back(ids, grad_branch, gains, down, up, slopes, grad_out, middle, branch):
    rows, width = grad_branch.shape
    hidden = up[0].shape[2]

    def body(ids, ins, outs, scratch):
        total, sums = scratch[0], outs[4].held
        grad_branch = ins[0]()
        for i in range(4):
            down, slope, up = (item() for item in ins[1 + 3 * i : 4 + 3 * i])
            pre_grads = outs[i // 2]

            def block(index, carry):
                at = pl.ds(index * ROW_BLOCK, ROW_BLOCK)
                back = dot_nn(grad_branch[at, :], down[...])
                pre_grad = (slope[at, :] * back).astype(BF)
                pre_grads.held[i % 2, at, :] = pre_grad
                product = dot_nt(pre_grad, up[...])
                total[at, :] = product if i == 0 else total[at, :] + product
                return carry + column_sum(pre_grad.astype(F32))

            start = jnp.zeros((1, hidden), F32)
            found = lax.fori_loop(0, rows // ROW_BLOCK, block, start)
            sums[pl.ds(4 + (ids[0] ^ PARTS[i]), 1), :] = found
            if i % 2:
                pre_grads.done()
        gains, grad_out, middle, branch = (item() for item in ins[13:])

        def finish(index, carry):
            at = pl.ds(index * 128, 128)
            grad = total[at, :]
            normal, back = norm_back_rows(grad, middle[at, :], gains[1:2, :])
            found = grad_out[at, :] + back
            scaled = (gains[2:3, :] * found).astype(BF)
            outs[2].held[at, :] = found
            outs[3].held[at, :] = scaled
            return (
                carry[0] + column_sum(grad * normal),
                carry[1] + column_sum(grad),
                carry[2] + column_sum(found * branch[at, :]),
                carry[3] + column_sum(scaled.astype(F32)),
            )

        zero = jnp.zeros((1, width), F32)
        found = lax.fori_loop(0, rows // 128, finish, (zero,) * 4)
        for i in range(4):
            sums[i : i + 1, :] = found[i]

    outs = call(
        body,
        "mlp_back",
        ids,
        [grad_branch]
        + [(kind[i // 2], i % 2) for i in range(4) for kind in (down, slopes, up)]
        + [gains, grad_out, middle, branch],
        [array((2, rows, hidden), BF)] * 2
        + [array((rows, width), F32), array((rows, width), BF), array((8, width), F32)],
        [((rows, width), F32)],
        grant=10,
        cover=40,
    )
    return (list(outs[:2]), *outs[2:])


def qkv_back(ids, masked, gains, grads, weights, start, grad_middle, mlp_sums):
    rows, width = start.shape
    lanes = width // 4

    def body(ids, ins, outs, scratch):
        total, sides = scratch
        small = outs[1].held
        grads = [ins[2 + i // 2]().at[i % 2] for i in range(4)]
        for i, part in enumerate(PARTS):
            sides[part : part + 1, :] = column_sum(grads[i][:, :lanes].astype(F32))
            found = column_sum(grads[i][:, 2 * lanes : 3 * lanes].astype(F32))
            sides[4 + part : 5 + part, :] = found
        for i in range(4):
            at = slice(i * lanes, (i + 1) * lanes)
            small[5:6, at] = sides[pl.ds(ids[0] ^ i, 1), :]
            small[6:7, at] = sides[pl.ds(4 + (ids[0] ^ i), 1), :]
        for i in range(4):
            weight = ins[4 + i // 2]().at[i % 2]

            def block(index, carry):
                at = pl.ds(index * ROW_BLOCK, ROW_BLOCK)
                product = dot_nt(grads[i][at, : 3 * lanes], weight[:, : 3 * lanes])
                total[at, :] = product if i == 0 else total[at, :] + product
                return carry

            lax.fori_loop(0, rows // ROW_BLOCK, block, 0)
        masked, gains = ins[0](), ins[1]()
        start, grad_middle, mlp_sums = (item() for item in ins[6:9])

        def finish(index, carry):
            at = pl.ds(index * 128, 128)
            grad = total[at, :]
            normal, back = norm_back_rows(grad, start[at, :], gains[0:1, :])
            found = grad_middle[at, :] + back
            hidden = masked[at, 0:1] > 0.5
            outs[0].held[at, :] = jnp.where(hidden, 0.0, found)
            return (
                carry[0] + column_sum(grad * normal),
                carry[1] + column_sum(grad),
                carry[2] + column_sum(jnp.where(hidden, found, 0.0)),
            )

        zero = jnp.zeros((1, width), F32)
        found = lax.fori_loop(0, rows // 128, finish, (zero,) * 3)
        small[0:1, :], small[4:5, :], small[10:11, :] = found
        small[1:2, :], small[2:3, :] = mlp_sums[0:1, :], mlp_sums[2:3, :]
        small[7:8, :], small[8:9, :] = mlp_sums[3:4, :], mlp_sums[1:2, :]
        small[3:4, :], small[9:10, :] = zero, zero
        small[11:15, :] = mlp_sums[4:8, :]
        small[15:16, :] = zero

    return call(
        body,
        "qkv_back",
        ids,
        [masked, gains, *grads, *weights, start, grad_middle, mlp_sums],
        [array((rows, width), F32), array((16, width), F32)],
        [((rows, width), F32), ((8, lanes), F32)],
        grant=10,
        cover=40,
    )


def weight_grad(ids, lefts, right, other, segments):
    rows, width = lefts[0].shape
    count = lax.axis_size("dp")
    z_count, block = count // 2, width // count
    total = right.shape[2]
    if block % ALIGN:
        found = []
        for which in range(2):
            parts = [
                dot_tn(lefts[2 * left], right[which, :, lane : lane + n])
                + dot_tn(lefts[2 * left + 1], other[which, :, lane : lane + n])
                for left, lane, n in segments
            ]
            found.append(jnp.concatenate(parts, axis=1).reshape(z_count, 2, block, total))
        x = ids[1]

        def at_x(value, which):
            return lax.dynamic_index_in_dim(value, which, 1, keepdims=False)

        own, across = found
        sent = at_x(own, 1 - x), at_x(across, x), at_x(across, 1 - x)
        return tuple(value.astype(BF) for value in sent), at_x(own, x)

    def body(ids, ins, outs, scratch):
        turned, product = scratch
        for i in range(len(lefts)):
            turned[i] = ins[i]()[...].T
        right, other = ins[-2](), ins[-1]()
        to_x, to_y, to_far, kept = outs
        for which, near_out, far_out in ((1, to_y, to_far), (0, kept, to_x)):
            for left, lane, n in segments:
                lanes = slice(lane, lane + n)
                product[:, lanes] = dot_nn(
                    turned[2 * left], right[which, :, lanes]
                ) + dot_nn(turned[2 * left + 1], other[which, :, lanes])
            for z in range(z_count):
                far = pl.multiple_of((2 * z + 1 - ids[1]) * block, ALIGN)
                near = pl.multiple_of((2 * z + ids[1]) * block, ALIGN)
                far_out.held[z] = product[pl.ds(far, block), :].astype(BF)
                near_out.held[z] = product[pl.ds(near, block), :].astype(near_out.held.dtype)
            near_out.done()
            far_out.done()

    shape = (z_count, block, total)
    *sent, kept = call(
        body,
        "weight_grad",
        ids,
        [*lefts, right, other],
        [array(shape, BF)] * 3 + [array(shape, F32)],
        [((len(lefts), width, rows), BF), ((width, total), F32)],
        grant=12,
    )
    return tuple(sent), kept


def first_hop(ids, lefts, right, other):
    rows, width = lefts[0].shape
    count, total = lax.axis_size("dp"), right.shape[2]
    z_count, block, half = count // 2, width // count, total // 2
    if block % ALIGN:
        own, across = (
            (dot_tn(lefts[0], right[which]) + dot_tn(lefts[1], other[which])).reshape(
                z_count, 2, block, total
            )
            for which in range(2)
        )
        x = ids[1]

        def at_x(value, which):
            return lax.dynamic_index_in_dim(value[..., half:], which, 1, keepdims=False)

        over_x = jnp.stack([at_x(own, 1 - x), at_x(across, 1 - x)])
        kept = own[..., :half], at_x(across, x), at_x(own, x)
        return (across[..., :half].astype(BF), over_x.astype(BF)), kept

    def body(ids, ins, outs, scratch):
        turned, product = scratch
        for i in range(2):
            turned[i] = ins[i]()[...].T
        right, other = ins[2](), ins[3]()
        over_y, over_x, low, across_high, own_high = (out.held for out in outs)

        def compute(which, lanes):
            return dot_nn(turned[0], right[which, :, lanes]) + dot_nn(
                turned[1], other[which, :, lanes]
            )

        over_y[...] = compute(1, slice(0, half)).astype(BF)
        low[...] = compute(0, slice(0, half))
        for which, kept in ((1, across_high), (0, own_high)):
            product[...] = compute(which, slice(half, total))
            for z in range(z_count):
                far = pl.multiple_of((2 * z + 1 - ids[1]) * block, ALIGN)
                near = pl.multiple_of((2 * z + ids[1]) * block, ALIGN)
                over_x[which, z] = product[pl.ds(far, block), :].astype(BF)
                kept[z] = product[pl.ds(near, block), :]

    high = (z_count, block, half)
    outs = call(
        body,
        "first_hop",
        ids,
        [*lefts, right, other],
        [
            array((width, half), BF),
            array((2,) + high, BF),
            array((width, half), F32),
            array(high, F32),
            array(high, F32),
        ],
        [((2, width, rows), BF), ((width, half), F32)],
        grant=12,
    )
    return tuple(outs[:2]), tuple(outs[2:])


def second_hop(ids, chunks):
    z_count, block, half = chunks[0][1][2].shape
    if block % ALIGN:
        x, results = ids[1], []
        for (over_y, over_x), (low, across_high, own_high) in chunks:
            low = low + over_y.astype(F32)
            far, near = (
                lax.dynamic_index_in_dim(low, which, 1, keepdims=False) for which in (1 - x, x)
            )
            high = across_high + over_x[1].astype(F32)
            results.append(
                (far.astype(BF), high.astype(BF), near, own_high + over_x[0].astype(F32))
            )
        joined = [jnp.concatenate(parts, axis=-1) for parts in zip(*results)]
        return tuple(joined[:2]), tuple(joined[2:])

    def body(ids, ins, outs, _):
        sent_x, sent_y, kept_low, kept_high = (out.held for out in outs)
        for i in range(len(chunks)):
            lanes = slice(i * half, (i + 1) * half)
            low, across_high, own_high, over_y, over_x = (
                item() for item in ins[5 * i : 5 * i + 5]
            )
            for z in range(z_count):
                far = pl.ds(pl.multiple_of((2 * z + 1 - ids[1]) * block, ALIGN), block)
                near = pl.ds(pl.multiple_of((2 * z + ids[1]) * block, ALIGN), block)
                sent_x[z, :, lanes] = (low[far, :] + over_y[far, :].astype(F32)).astype(BF)
                kept_low[z, :, lanes] = low[near, :] + over_y[near, :].astype(F32)
                sent_y[z, :, lanes] = (across_high[z] + over_x[1, z].astype(F32)).astype(BF)
                kept_high[z, :, lanes] = own_high[z] + over_x[0, z].astype(F32)

    high = (z_count, block, half * len(chunks))
    outs = call(
        body,
        "second_hop",
        ids,
        [value for received, kept in chunks for value in (*kept, *received)],
        [array(high, BF)] * 2 + [array(high, F32)] * 2,
        cover=2,
    )
    return tuple(outs[:2]), tuple(outs[2:])


def in_thirds(value):
    high = value.astype(BF)
    rest = value - high.astype(F32)
    middle = rest.astype(BF)
    return high, middle, (rest - middle.astype(F32)).astype(BF)


def plane_sum(ids, parts, vectors=None):
    z_count, block, _ = parts[0][0].shape
    widths = [kept.shape[2] for kept, _ in parts]
    if z_count == 4 and block % ALIGN == 0:

        def body(ids, ins, outs, _):
            for step in (1, 2, 3, 0):
                at, place, lane = lax.rem(ids[2] + step, z_count), 0, 0
                out = outs[step].held
                for (_, received), n in zip(parts, widths):
                    found = ins[place]()[at]
                    for item in ins[place + 1 : place + 1 + len(received)]:
                        found = found + item()[at].astype(F32)
                    out[:block, lane : lane + n] = found.astype(out.dtype)
                    place, lane = place + 1 + len(received), lane + n
                if step and vectors is not None:
                    for i, third in enumerate(in_thirds(ins[-1]()[...])):
                        out[block + 16 * i : block + 16 * (i + 1), :] = third

        below = [] if vectors is None else [vectors]
        shape = (block, sum(widths))
        longer = (block + 48 * len(below), sum(widths))
        own, *sent = call(
            body,
            "plane_sum",
            ids,
            [value for kept, received in parts for value in (kept, *received)] + below,
            [array(shape, F32)] + [array(longer, BF)] * 3,
            cover=2,
        )
        return tuple(sent), own
    sums = [sum((value.astype(F32) for value in received), kept) for kept, received in parts]
    return (), jnp.concatenate(sums, axis=-1)


def last_hop(sent, own, steps):
    if not sent:
        return [], own if own.ndim == 2 else scatter_z(own)
    with jax.named_scope("g3z"):
        return [send_digit(sent[step - 1], 1, 4, step) for step in steps], own


def adamw_step(master, first, second, gradient, rate, decay, correction):
    first_new = 0.5 * first + 0.5 * gradient
    second_new = 0.5 * second + 0.5 * gradient * gradient
    update = first_new / correction / (jnp.sqrt(second_new / correction) + ADAM_EPS)
    master_new = master - rate * (update + decay * master)
    return (master_new, first_new, second_new, master_new.astype(BF))


def update_weights(ids, correction, received, own, states, rates, pick, vectors=None, others=()):
    block = own.shape[0]
    if block % ALIGN:
        results = []
        for i, (state, rate) in enumerate(zip(states, rates)):
            results += adamw_step(*state, pick(own, i), rate, DECAY, correction[0, 0])
        return results
    places = list(states) + list(others)

    def body(ids, ins, outs, scratch):
        correction, total = ins[0]()[0:1, 0:1], scratch[0]
        received_refs = [item() for item in ins[2 : 2 + len(received)]]
        found = ins[1]()[...]
        for item in received_refs:
            found = found + item[:block, :].astype(F32)
        total[...] = found
        grads = [(pick, i, rate, DECAY) for i, rate in enumerate(rates)]
        if vectors is not None:
            by_z = scratch[1]
            by_z[ids[2]] = sum(third.astype(F32) for third in in_thirds(ins[-1]()[...]))
            for step, item in enumerate(received_refs, 1):
                thirds = (item[block + 16 * i : block + 16 * (i + 1), :] for i in range(3))
                at = lax.bitwise_and(ids[2] - step, 3)
                by_z[at] = sum(third.astype(F32) for third in thirds)
            sums = (by_z[0] + by_z[1]) + (by_z[2] + by_z[3])
            grads += [
                (lambda _, i: sums[0:4, :], 0, 0.1, 0.0),
                (lambda _, i: sums[4:15, :], 0, 0.3, 0.0),
            ]
        at = 2 + len(received)
        for i, (choose, which, rate, decay) in enumerate(grads):
            master, first, second = (item()[...] for item in ins[at + 3 * i : at + 3 * i + 3])
            results = adamw_step(
                master, first, second, choose(total, which), rate, decay, correction
            )
            for out, value in zip(outs[4 * i : 4 * i + 4], results):
                out.held[...] = value

    outputs = []
    for state in places:
        outputs += [array(state[0].shape, F32)] * 3 + [array(state[0].shape, BF)]
    flat = [value for state in places for value in state]
    scratch = [(own.shape, F32)]
    if vectors is not None:
        flat.append(vectors)
        scratch.append(((4,) + vectors.shape, F32))
    return call(
        body,
        "update_weights",
        ids,
        [correction, own, *received, *flat],
        outputs,
        scratch,
    )


def pack_weights(ids, qkv_master, out_master):
    count, rows, lanes = qkv_master.shape
    if rows % ALIGN:
        parts = [qkv_master[i] for i in range(count)] + [out_master.T]
        return jnp.concatenate(parts, axis=1).astype(BF)

    def body(ids, ins, outs, _):
        qkv = ins[0]()
        for i in range(count):
            outs[0].held[:, i * lanes : (i + 1) * lanes] = qkv[i].astype(BF)
        outs[0].held[:, count * lanes :] = ins[1]()[...].T.astype(BF)

    return call(
        body,
        "pack_weights",
        ids,
        [qkv_master, out_master],
        [array((rows, (count + 1) * lanes), BF)],
    )[0]


def pack_down(ids, up_master, down_turned):
    rows, width = up_master.shape
    if rows % ALIGN:
        return jnp.concatenate([up_master, down_turned], axis=1).astype(BF)

    def body(ids, ins, outs, _):
        outs[0].held[:, :width] = ins[0]()[...].astype(BF)
        outs[0].held[:, width:] = ins[1]()[...].astype(BF)

    return call(
        body, "pack_down", ids, [up_master, down_turned], [array((rows, 2 * width), BF)]
    )[0]


def norm_rows(values, gain, shift):
    average = jnp.mean(values, axis=-1, keepdims=True)
    centered = values - average
    inverse = lax.rsqrt(jnp.mean(centered * centered, axis=-1, keepdims=True) + EPS_NORM)
    return centered * inverse * gain + shift


def on_device(
    patches,
    cotangent,
    mask_rows,
    count_big,
    pos_big,
    pos_small,
    step_count,
    qkv_master,
    qkv_first,
    qkv_second,
    out_master,
    out_first,
    out_second,
    up_master,
    up_first,
    up_second,
    down_master,
    down_first,
    down_second,
    norm_gains,
    gain_first,
    gain_second,
    shifts,
    shift_first,
    shift_second,
):
    tensor_id = lax.axis_index("tensor")
    local_rows = patches.shape[0]
    total_rows = 4 * local_rows
    lanes = qkv_master.shape[2]
    hidden_lanes = up_master.shape[1]
    big_rows = count_big[0] * BIG_LEN
    used_rows = big_rows + (total_rows - big_rows) // SMALL_LEN * SMALL_LEN
    first_row = tensor_id * local_rows

    in_kernels = up_master.shape[0] % ALIGN == 0 and lax.axis_size("dp") == 8
    bounds = image_bounds(count_big[0], first_row, local_rows, total_rows)
    dp_id = lax.axis_index("dp")
    ids = jnp.stack(
        [tensor_id, lax.bitwise_and(dp_id, 1), lax.shift_right_logical(dp_id, 1)]
    ).astype(jnp.int32)
    own = slice(HALO, HALO + local_rows)
    correction = 1.0 - jnp.power(jnp.float32(0.5), step_count[0].astype(F32))

    down_state = (down_master.T, down_first.T, down_second.T)

    local_a = pack_weights(ids, qkv_master, out_master)
    with jax.named_scope("wa"):
        z_a = gather_z(local_a)
    payload = jnp.concatenate(
        [patches, jnp.broadcast_to(mask_rows[:, None].astype(BF), (local_rows, 128))], axis=1
    )
    up_hops, down_hops = [(0, 1), (1, 2), (2, 3)], [(1, 0), (2, 1), (3, 2)]
    with jax.named_scope("halo"):
        halo_before = lax.ppermute(payload[-HALO:], "tensor", up_hops)
        halo_after = lax.ppermute(payload[:HALO], "tensor", down_hops)
    local_bc = pack_down(after(ids, local_a), up_master, down_state[0])

    z_a, halo_before, halo_after, local_bc = gate(z_a, halo_before, halo_after, local_bc)
    (z_a,) = place_z(ids, z_a)
    with jax.named_scope("wbc"):
        z_bc = gather_z(after(local_bc, z_a))
    with jax.named_scope("wa"):
        plane_a = send_plane(z_a, z_a, z_a)
    payload = jnp.concatenate([halo_before, payload, halo_after], axis=0)
    ext_rows = payload.shape[0]
    row_ids = first_row - HALO + jnp.arange(ext_rows, dtype=jnp.int32)
    remainder = row_ids - big_rows
    is_big = (row_ids >= 0) & (row_ids < big_rows)
    is_valid = (row_ids >= 0) & (row_ids < used_rows)
    is_small = is_valid & jnp.logical_not(is_big)
    position = jnp.where(is_big, row_ids % BIG_LEN, remainder % SMALL_LEN)
    masked_ext = (payload[:, D] == 1) & is_valid
    pick_big = (
        (position[:, None] == jnp.arange(BIG_LEN, dtype=jnp.int32)[None, :]) & is_big[:, None]
    ).astype(BF)
    pick_small = (
        (position[:, None] == jnp.arange(SMALL_LEN, dtype=jnp.int32)[None, :]) & is_small[:, None]
    ).astype(BF)
    placed = dot_nn(pick_big, pos_big) + dot_nn(pick_small, pos_small)
    start_ext = (
        jnp.where(masked_ext[:, None], shifts[6][None, :], payload[:, :D].astype(F32)) + placed
    )
    normed_ext = norm_rows(start_ext, norm_gains[0], shifts[0]).astype(BF)
    start_rows, masked, valid_local = start_ext[own], masked_ext[own], is_valid[own]
    normed = normed_ext[own]
    masked = jnp.broadcast_to(masked[:, None].astype(F32), (local_rows, 128))
    grad_out = cotangent.astype(F32) * valid_local[:, None].astype(F32)
    grad_branch = (norm_gains[3] * grad_out).astype(BF)
    biases = jnp.stack(
        [
            jnp.concatenate(
                [
                    lax.dynamic_slice_in_dim(shifts[1], (tensor_id ^ i) * lanes, lanes),
                    jnp.zeros((lanes,), F32),
                    lax.dynamic_slice_in_dim(shifts[2], (tensor_id ^ i) * lanes, lanes),
                    jnp.zeros((lanes,), F32),
                ]
            )
            for i in range(4)
        ]
    )

    z_a, plane_a, z_bc, normed_ext, start_rows, grad_branch, normed, biases = gate(
        z_a, plane_a, z_bc, normed_ext, start_rows, grad_branch, normed, biases
    )
    z_b, z_c = place_z(ids, z_bc, 2)
    with jax.named_scope("wb"):
        plane_b = send_plane(z_b, z_b, z_b)
    own_a = place_x(ids, z_a, *plane_a)
    with jax.named_scope("wa/core"):
        a_all = [own_a, send_core(own_a)]
    with jax.named_scope("pair"):
        grad_branch_other = send_core(grad_branch)
    qkv, branch_attn, middle, normed_two = attention_block(
        after(bounds, z_b), normed_ext, a_all, biases, start_rows, norm_gains, shifts
    )

    plane_b, z_b, z_c, normed_two, grad_branch_other = gate(
        plane_b, z_b, z_c, normed_two, grad_branch_other
    )
    own_b = place_x(ids, z_b, *plane_b)
    with jax.named_scope("wb/core"):
        b_all = [own_b, send_core(own_b)]
    with jax.named_scope("wc"):
        plane_c = send_plane(z_c, z_c, z_c)
    found = mlp_up(ids, normed_two, shifts, b_all[0], 0, 40)
    other = mlp_up(after(ids, found), normed_two, shifts, b_all[1], 1, 0)
    hidden, slopes = zip(found, other)
    plane_c, normed_two, normed, hidden = gate(plane_c, normed_two, normed, hidden)
    own_c = place_x(ids, z_c, *plane_c)
    with jax.named_scope("wc/core"):
        c_all = [own_c, send_core(own_c)]

    with jax.named_scope("pair"):
        hidden_other = send_core(hidden[1])
        normed_two_other, normed_other = send_core(normed_two), send_core(normed)
    pre_grad, grad_middle, grad_attn, mlp_sums = mlp_back(
        ids, grad_branch, norm_gains, c_all, b_all, slopes, grad_out, middle, branch_attn
    )
    hidden_other, normed_two_other, normed_other, pre_grad, grad_attn = gate(
        hidden_other, normed_two_other, normed_other, pre_grad, grad_attn
    )
    with jax.named_scope("gb"):
        pre_grad_other = send_core(pre_grad[1])
    with jax.named_scope("halo"):
        halo_before = lax.ppermute(grad_attn[-HALO:], "tensor", up_hops)
        halo_after = lax.ppermute(grad_attn[:HALO], "tensor", down_hops)
    with jax.named_scope("pair"):
        grad_attn_other = send_core(grad_attn)
    chunk_c = first_hop(ids, (grad_branch, grad_branch_other), hidden[0], hidden_other)
    chunk_b = first_hop(
        after(ids, chunk_c[0]), (normed_two, normed_two_other), pre_grad[0], pre_grad_other
    )
    halo_before, halo_after, chunk_b, chunk_c, grad_attn, grad_attn_other = gate(
        halo_before, halo_after, chunk_b, chunk_c, grad_attn, grad_attn_other
    )
    with jax.named_scope("gc"):
        first_c = send_first(*chunk_c[0])
    with jax.named_scope("gb"):
        first_b = send_first(*chunk_b[0])
    grad_qkv = attention_backward(
        after(bounds, chunk_b[0]), [halo_before, grad_attn, halo_after], qkv, a_all
    )
    first_c, first_b, grad_qkv = gate(first_c, first_b, grad_qkv)
    sent, kept = second_hop(ids, ((first_c, chunk_c[1]), (first_b, chunk_b[1])))
    with jax.named_scope("gbc"):
        second_bc = send_second(*sent)
    with jax.named_scope("ga"):
        grad_qkv_other = send_core(grad_qkv[1])
    chunk_a = weight_grad(
        after(ids, sent),
        (normed, normed_other, grad_attn, grad_attn_other),
        grad_qkv[0],
        grad_qkv_other,
        ((0, 0, 2 * lanes), (0, 2 * lanes, lanes), (1, 3 * lanes, lanes)),
    )
    x_bc, chunk_a, grad_qkv = gate(second_bc[0], chunk_a, grad_qkv)
    with jax.named_scope("gbc"):
        sent, sum_bc = plane_sum(ids, [(kept[0], (x_bc,)), (kept[1], (second_bc[1],))])
        early_bc, sum_bc = last_hop(sent, sum_bc, (1, 2))
    with jax.named_scope("ga"):
        plane_a = send_plane(*chunk_a[0])
    patch_grad, small = qkv_back(
        after(ids, sent), masked, norm_gains, grad_qkv, a_all, start_rows, grad_middle, mlp_sums
    )
    hidden = after(hidden, chunk_a)
    branch_mlp = shifts[5] + sum(
        dot_nt(hidden[i // 2][i % 2], c_all[i // 2][i % 2]) for i in range(4)
    )
    layer_out = (middle + norm_gains[3] * branch_mlp).astype(BF)
    extra = [jnp.sum(grad_out * branch_mlp, axis=0), jnp.sum(grad_branch.astype(F32), axis=0)]
    early_bc, sent, small, layer_out, extra, x_a = gate(
        early_bc, sent, small, layer_out, extra, plane_a[0]
    )
    is_row = [lax.broadcasted_iota(jnp.int32, small.shape, 0) == row for row in (3, 9)]
    small = jnp.where(is_row[0], extra[0], jnp.where(is_row[1], extra[1], small))
    with jax.named_scope("small"):
        if not in_kernels:
            small = sum_over_z(small)
    with jax.named_scope("gbc"):
        late_bc, sum_bc = last_hop(sent, sum_bc, (3,))
    last_bc = [*early_bc, *late_bc]
    with jax.named_scope("small"):
        small = sum_over_plane(small)
    *plane_a, small = gate(x_a, *plane_a[1:], small)
    with jax.named_scope("ga"):
        sent, sum_a = plane_sum(ids, [(chunk_a[1], plane_a)], small if in_kernels else None)
        last_a, sum_a = last_hop(sent, sum_a, (1, 2, 3))
    vectors = ((norm_gains, gain_first, gain_second), (shifts, shift_first, shift_second))
    if not in_kernels:
        gain_res = adamw_step(*vectors[0], small[:4], 0.1, 0.0, correction)
        shift_res = adamw_step(*vectors[1], small[4:15], 0.3, 0.0, correction)
    correction = jnp.broadcast_to(correction, (8, 128))
    quarter = sum_bc.shape[1] // 4

    def pick_bc(total, i):
        at = (1 - i) * quarter
        parts = total[:, at : at + quarter], total[:, at + 2 * quarter : at + 3 * quarter]
        return jnp.concatenate(parts, axis=1)

    def pick_a(total, i):
        if i == 1:
            return total[:, 3 * lanes :].T
        return jnp.stack([total[:, at * lanes : (at + 1) * lanes] for at in range(3)])

    up_down = update_weights(
        after(ids, sent, sum_a),
        correction,
        last_bc,
        sum_bc,
        ((up_master, up_first, up_second), down_state),
        (D ** (-0.5), FF ** (-0.5)),
        pick_bc,
    )
    qkv_out = update_weights(
        after(ids, up_down),
        correction,
        last_a,
        sum_a,
        ((qkv_master, qkv_first, qkv_second), (out_master, out_first, out_second)),
        (D ** (-0.5), (D // 16) ** (-0.5)),
        pick_a,
        *((small, vectors) if in_kernels else ()),
    )
    if in_kernels:
        qkv_out, gain_res, shift_res = qkv_out[:8], qkv_out[8:12], qkv_out[12:]
    down_out = [value.T for value in up_down[4:]]
    return (layer_out, patch_grad, *qkv_out, *up_down[:4], *down_out, *gain_res, *shift_res)


def solution(mesh):
    rows = P(("dp", "tensor"), None)
    qkv = (P(None, "dp", "tensor"),)
    tensor_first, dp_first, whole = (P("tensor", "dp"),), (P("dp", "tensor"),), (P(),)
    weights = tuple(
        spec * 3 for spec in (qkv, tensor_first, dp_first, tensor_first)
    )
    results = tuple(
        spec * 4 for spec in (qkv, tensor_first, dp_first, tensor_first)
    )
    return jax.shard_map(
        on_device,
        mesh=mesh,
        in_specs=(rows, rows, P(("dp", "tensor")), P("dp")) + whole * 3 + sum(weights, ()) + whole * 6,
        out_specs=(rows, rows) + sum(results, ()) + whole * 8,
        check_vma=False,
    )
```

```python
import functools

import jax
import jax.numpy as jnp
import numpy as np
from jax import lax
from jax.experimental import pallas as pl
from jax.experimental.pallas import tpu as pltpu
from jax.sharding import PartitionSpec as P

D = 768
HEAD_DIM = 64
FF = 3072
BIG_LEN = 197
SMALL_LEN = 101
HALO = 208
ALIGN = 16
PARTS = (0, 2, 1, 3)
QUERIES, KEYS = 256, 224
ROW_BLOCK = 256

EPS_NORM = 1e-06
ADAM_EPS = 1e-08
DECAY = 0.05
NEGATIVE = -1e30
FACTOR = HEAD_DIM ** (-0.5)
BF = jnp.bfloat16
F32 = jnp.float32


def send_dp(value, target):
    count = lax.axis_size("dp")
    return lax.ppermute(value, "dp", [(i, target(i)) for i in range(count)])


def send_x(value):
    return send_dp(value, lambda i: i ^ 1)


def send_tensor(value, mask):
    return lax.ppermute(value, "tensor", [(i, i ^ mask) for i in range(4)])


def send_y(value):
    return send_tensor(value, 2)


def send_core(value):
    return send_tensor(value, 1)


def z_digits():
    left = lax.axis_size("dp") // 2
    stride, digits = 1, []
    while left > 1:
        radix = 4 if left % 4 == 0 else 2
        digits.append((stride, radix))
        stride, left = stride * radix, left // radix
    return digits


def send_digit(value, stride, radix, step):
    def target(i):
        z, x = i // 2, i % 2
        digit = z // stride % radix
        return 2 * (z + ((digit + step) % radix - digit) * stride) + x

    return send_dp(value, target)


def gather_z(block):
    block = block[None]
    digits = z_digits()
    for stride, radix in digits[:-1]:
        pieces = [send_digit(block, stride, radix, step) for step in range(1, radix)]
        block = place([block] + pieces, stride, radix)
    stride, radix = digits[-1]
    return [block] + [send_digit(block, stride, radix, step) for step in range(1, radix)]


def place(parts, stride, radix):
    z = lax.shift_right_logical(lax.axis_index("dp"), 1)
    digit = lax.bitwise_and(lax.div(z, stride), radix - 1)
    out = jnp.zeros((radix,) + parts[0].shape, parts[0].dtype)
    for step, piece in enumerate(parts):
        at = lax.bitwise_and(digit - step, radix - 1)
        out = lax.dynamic_update_slice(out, piece[None], (at, 0, 0, 0))
    return out.reshape((-1,) + parts[0].shape[1:])


def scatter_z(partial):
    z = lax.axis_index("dp") // 2
    for stride, radix in reversed(z_digits()):
        digit = z // stride % radix
        parts = partial.reshape((radix, -1) + partial.shape[1:])
        own = lax.dynamic_index_in_dim(parts, digit, 0, keepdims=False)
        pieces = [
            send_digit(
                lax.dynamic_index_in_dim(
                    parts, (digit + step) % radix, 0, keepdims=False
                ).astype(BF),
                stride,
                radix,
                step,
            )
            for step in range(1, radix)
        ]
        for piece in pieces:
            own = own + piece.astype(F32)
        partial = own
    return partial[0]


def after(value, *others):
    return lax.optimization_barrier((value, others))[0]


def gate(*values):
    return lax.optimization_barrier(values)


def send_far(value):
    count = lax.axis_size("dp")
    pairs = [(4 * i + j, 4 * (i ^ 1) + (j ^ 2)) for i in range(count) for j in range(4)]
    return lax.ppermute(value, ("dp", "tensor"), pairs)


def send_near(to_x, to_y):
    with jax.named_scope("x"):
        from_x = send_x(to_x)
    with jax.named_scope("y"):
        return from_x, send_y(to_y)


def send_first(to_y, to_x):
    with jax.named_scope("g1y"):
        from_y = send_y(to_y)
    with jax.named_scope("g1x"):
        return from_y, send_x(to_x)


def send_second(to_x, to_y):
    with jax.named_scope("g2x"):
        from_x = send_x(to_x)
    with jax.named_scope("g2y"):
        return from_x, send_y(to_y)


def send_plane(to_x, to_y, to_far):
    near = send_near(to_x, to_y)
    with jax.named_scope("far"):
        return (*near, send_far(to_far))


def sum_over_z(value):
    bit = 2
    while bit < lax.axis_size("dp"):
        value = value + send_dp(value, lambda i, b=bit: i ^ b)
        bit *= 2
    return value


def sum_over_plane(value):
    for send in (send_core, send_y, send_x):
        value = value + send(value)
    return value


def dot_nt(left, right):
    return lax.dot_general(left, right, (((1,), (1,)), ((), ())), preferred_element_type=F32)


def dot_tn(left, right):
    return lax.dot_general(left, right, (((0,), (0,)), ((), ())), preferred_element_type=F32)


def dot_nn(left, right):
    return jnp.dot(left, right, preferred_element_type=F32)


def array(shape, dtype):
    return jax.ShapeDtypeStruct(shape, dtype)


def column_sum(values):
    return jnp.sum(values, axis=0, keepdims=True)


class Held:
    def __init__(self, held):
        self.held = held

    def __call__(self):
        return self.held

    def done(self, first=None):
        pass


def call(body, name, scalars, inputs, outputs, scratch=(), grant=10, cover=10):
    flat, places = [], []
    for value in inputs:
        group = value if isinstance(value, list) else [value[0] if isinstance(value, tuple) else value]
        places.append([])
        for item in group:
            found = [i for i, other in enumerate(flat) if other is item]
            places[-1].append(found[0] if found else len(flat))
            if not found:
                flat.append(item)
    boxes = [
        pltpu.VMEM((sum(v.shape[0] for v in value),) + value[0].shape[1:], value[0].dtype)
        for value in inputs
        if isinstance(value, list)
    ]

    def kernel(scalar_ref, *refs):
        sources, refs = refs[: len(flat)], refs[len(flat) :]
        targets, refs = refs[: len(outputs)], refs[len(outputs) :]
        joined, extra = iter(refs[: len(boxes)]), refs[len(boxes) :]
        ins = []
        for value, place in zip(inputs, places):
            if isinstance(value, list):
                box, row = next(joined), 0
                for at in place:
                    rows = sources[at].shape[0]
                    box[row : row + rows] = sources[at][...]
                    row += rows
                ins.append(Held(box))
            elif isinstance(value, tuple):
                ins.append(Held(sources[place[0]].at[value[1]]))
            else:
                ins.append(Held(sources[place[0]]))
        body(scalar_ref, ins, [Held(target) for target in targets], extra)

    in_vmem = pl.BlockSpec(memory_space=pltpu.VMEM)
    return pl.pallas_call(
        kernel,
        name=name,
        in_specs=[pl.BlockSpec(memory_space=pltpu.SMEM)] + [in_vmem] * len(flat),
        out_specs=[in_vmem] * len(outputs),
        out_shape=list(outputs),
        scratch_shapes=boxes + [pltpu.VMEM(*box) for box in scratch],
        compiler_params=pltpu.CompilerParams(vmem_limit_bytes=grant << 20),
        cost_estimate=pl.CostEstimate(
            flops=0, transcendentals=0, bytes_accessed=cover * 3 * 10**6
        ),
    )(scalars, *flat)


def move(name, scalars, inputs, outputs, plan, cover=2):
    def kernel(scalar_ref, *refs):
        pairs = plan(scalar_ref, refs[: len(inputs)], refs[len(inputs) : -1])
        copies = [
            pltpu.make_async_copy(source, target, refs[-1].at[i])
            for i, (source, target) in enumerate(pairs)
        ]
        for copy in copies:
            copy.start()
        for copy in copies:
            copy.wait()

    return pl.pallas_call(
        kernel,
        name=name,
        in_specs=[pl.BlockSpec(memory_space=pltpu.SMEM)]
        + [pl.BlockSpec(memory_space=pl.ANY)] * len(inputs),
        out_specs=[pl.BlockSpec(memory_space=pltpu.VMEM)] * len(outputs),
        out_shape=list(outputs),
        scratch_shapes=[pltpu.SemaphoreType.DMA((len(inputs) * len(outputs),))],
        compiler_params=pltpu.CompilerParams(vmem_limit_bytes=1 << 20),
        cost_estimate=pl.CostEstimate(flops=0, transcendentals=0, bytes_accessed=cover * 3 * 10**6),
    )(scalars, *inputs)


def place_z(ids, parts, split=1):
    stride, radix = z_digits()[-1]
    _, rows, n = parts[0].shape
    each = n // split
    if rows % ALIGN or stride != 1:
        whole = place(parts, stride, radix)
        return [whole[..., i * each : (i + 1) * each] for i in range(split)]

    def plan(ids, ins, outs):
        return [
            (
                piece.at[0, :, pl.ds(i * each, each)],
                outs[i].at[lax.bitwise_and(ids[2] - step, radix - 1)],
            )
            for i in range(split)
            for step, piece in enumerate(ins)
        ]

    return move("place_z", ids, parts, [array((radix, rows, each), BF)] * split, plan)


def place_x(ids, mine, from_x, from_y, from_far, cover=2):
    count, rows, n = mine.shape
    if rows % ALIGN:
        x = ids[1]

        def merge(near, far):
            pair = [jnp.where(x == 0, near, far), jnp.where(x == 0, far, near)]
            return jnp.stack(pair, axis=1).reshape(-1, n)

        return jnp.stack([merge(mine, from_x), merge(from_y, from_far)])

    def plan(ids, ins, outs):
        x = ids[1]
        return [
            (ins[0], outs[0].at[0, :, x]),
            (ins[1], outs[0].at[0, :, 1 - x]),
            (ins[2], outs[0].at[1, :, x]),
            (ins[3], outs[0].at[1, :, 1 - x]),
        ]

    shape = (2, count, 2, rows, n)
    inputs = [mine, from_x, from_y, from_far]
    out = move("place_x", ids, inputs, [array(shape, BF)], plan, cover)[0]
    return out.reshape(2, -1, n)


def image_loop(bounds, window):
    big_from, big_count, small_from, count, big_rows, _, total = (bounds[i] for i in range(7))

    def one(index, carry):
        is_big = index < big_count
        big_start = (big_from + index) * BIG_LEN
        small_start = big_rows + (small_from + 2 * (index - big_count)) * SMALL_LEN
        start = jnp.where(is_big, big_start, small_start)
        stop = start + jnp.where(is_big, BIG_LEN, 2 * SMALL_LEN)
        window(start, start + jnp.where(is_big, BIG_LEN, SMALL_LEN), jnp.minimum(stop, total))
        return carry

    lax.fori_loop(0, count, one, 0)


def image_bounds(count_big, first_row, local_rows, total_rows):
    big_rows = count_big * BIG_LEN
    last_row = first_row + local_rows - 1
    big_from = jnp.minimum(first_row // BIG_LEN, count_big)
    big_count = jnp.minimum(last_row // BIG_LEN + 1, count_big) - big_from
    small_from = jnp.maximum(first_row - big_rows, 0) // SMALL_LEN
    small_to = jnp.where(last_row >= big_rows, (last_row - big_rows) // SMALL_LEN + 1, small_from)
    count = big_count + (small_to - small_from + 1) // 2
    base = first_row - HALO
    return jnp.stack(
        [big_from, big_count, small_from, count, big_rows, base, jnp.int32(total_rows), base]
    ).astype(jnp.int32)


class Window:
    def __init__(self, start, middle, stop, base, ext_rows):
        aligned = (start - base) // ALIGN * ALIGN
        at_q = pl.multiple_of(jnp.minimum(aligned, ext_rows - QUERIES), ALIGN)
        at_k = pl.multiple_of(jnp.minimum(aligned, ext_rows - KEYS), ALIGN)

        def ids(offset, shape, axis):
            return lax.broadcasted_iota(jnp.int32, shape, axis) + (offset + base)

        def inside(rows):
            return (rows >= start) & (rows < stop)

        key, query = ids(at_k, (KEYS, 1), 0), ids(at_q, (1, QUERIES), 1)
        self.queries, self.keys = pl.ds(at_q, QUERIES), pl.ds(at_k, KEYS)
        self.query_down = inside(ids(at_q, (QUERIES, 1), 0))
        self.key_down = inside(key)
        key_side = jnp.where(self.key_down, (key >= middle).astype(jnp.int32), 2)
        query_side = (query >= middle).astype(jnp.int32)
        self.same = key_side == query_side
        self.both = key_side == jnp.where(inside(query), query_side, 3)


def softmax_down(key, query, same):
    scores = jnp.where(same, dot_nt(key, query), NEGATIVE)
    exps = jnp.exp(scores - jnp.max(scores, axis=0, keepdims=True))
    return exps * (1.0 / jnp.sum(exps, axis=0, keepdims=True))


def attention_block(bounds, rows, weights, biases, start, gains, shifts):
    ext_rows, width = rows.shape
    lanes = width // 4
    local_rows = start.shape[0]

    def body(bounds, ins, outs, _):
        rows, biases = ins[0](), ins[1]()
        held = outs[0].held
        weights = []
        for i, part in enumerate(PARTS):
            weights.append(ins[2 + i // 2]().at[i % 2])

            def project(index, carry):
                at = pl.ds(index * (ext_rows // 2), ext_rows // 2)
                found = dot_nn(rows[at, :], weights[i][:, : 3 * lanes])
                found = found + biases[part : part + 1, : 3 * lanes]
                held[i, at, : 3 * lanes] = found.astype(BF)
                return carry

            lax.fori_loop(0, 2, project, 0)

        def window(start, middle, stop):
            at = Window(start, middle, stop, bounds[5], ext_rows)

            def pair(index, carry):
                for source in (held.at[index],):
                    parts = []
                    for lane in range(0, lanes, HEAD_DIM):
                        query = source[at.queries, lane : lane + HEAD_DIM] * BF(FACTOR)
                        key = source[at.keys, lanes + lane : lanes + lane + HEAD_DIM]
                        value = source[at.keys, 2 * lanes + lane : 2 * lanes + lane + HEAD_DIM]
                        probs = softmax_down(key, query, at.same)
                        parts.append(dot_nn(value.T, probs.astype(BF)))
                    mixed = jnp.concatenate(parts, axis=0).T.astype(BF)
                    old = source[at.queries, 3 * lanes :]
                    source[at.queries, 3 * lanes :] = jnp.where(at.query_down, mixed, old)
                return carry

            lax.fori_loop(0, 4, pair, 0)

        image_loop(bounds, window)
        outs[0].done()
        start, gains, shifts = (item() for item in ins[4:7])

        def finish(index, carry):
            at = pl.ds(index * 128, 128)
            ext = pl.ds(HALO + index * 128, 128)
            found = shifts[3:4, :]
            for i in range(4):
                found = found + dot_nt(held[i, ext, 3 * lanes :], weights[i][:, 3 * lanes :])
            outs[1].held[at, :] = found
            found = start[at, :] + gains[2:3, :] * found
            outs[2].held[at, :] = found
            outs[3].held[at, :] = norm_rows(found, gains[1:2, :], shifts[4:5, :]).astype(BF)
            return carry

        lax.fori_loop(0, local_rows // 128, finish, 0)

    return call(
        body,
        "attention_block",
        bounds,
        [rows, biases, *weights, start, gains, shifts],
        [array((4, ext_rows, width), BF)]
        + [array((local_rows, width), F32)] * 2
        + [array((local_rows, width), BF)],
        cover=40,
    )


def attention_backward(bounds, grad_attn, qkv, weights):
    _, ext_rows, width = qkv.shape
    lanes = width // 4
    local_rows = ext_rows - 2 * HALO

    def body(bounds, ins, outs, scratch):
        ext, grads = scratch
        grad_attn = ins[0]()
        for i in range(4):
            weight = ins[1 + i // 2]()
            grads[i] = dot_nn(grad_attn[...], weight[i % 2, :, 3 * lanes :]).astype(BF)
        held = ins[3]()

        def window(start, middle, stop):
            at = Window(start, middle, stop, bounds[5], ext_rows)

            def pair(index, carry):
                for part in (2 * index, 2 * index + 1):
                    source, grad, out = held.at[part], grads.at[part], ext.at[part]
                    query_parts, key_parts, value_parts = [], [], []
                    for lane in range(0, lanes, HEAD_DIM):
                        query = source[at.queries, lane : lane + HEAD_DIM] * BF(FACTOR)
                        key = source[at.keys, lanes + lane : lanes + lane + HEAD_DIM]
                        value = source[at.keys, 2 * lanes + lane : 2 * lanes + lane + HEAD_DIM]
                        grad_rows = grad[at.queries, lane : lane + HEAD_DIM]
                        probs = jnp.where(at.both, softmax_down(key, query, at.same), 0.0)
                        weighted = probs * dot_nt(value, grad_rows)
                        inner = jnp.sum(weighted, axis=0, keepdims=True)
                        grad_scores = (weighted - probs * inner).astype(BF)
                        query_parts.append(dot_nn((key * BF(FACTOR)).T, grad_scores))
                        key_parts.append(dot_nn(grad_scores, query))
                        value_parts.append(dot_nn(probs.astype(BF), grad_rows))
                    grad_query = jnp.concatenate(query_parts, axis=0).T.astype(BF)
                    old = out[at.queries, :lanes]
                    out[at.queries, :lanes] = jnp.where(at.query_down, grad_query, old)
                    grad_kv = jnp.concatenate(key_parts + value_parts, axis=1).astype(BF)
                    old = out[at.keys, lanes:]
                    out[at.keys, lanes:] = jnp.where(at.key_down, grad_kv, old)
                return carry

            lax.fori_loop(0, 2, pair, 0)

        image_loop(bounds, window)
        at = slice(HALO, HALO + local_rows)
        for i in (2, 3, 0, 1):
            out = outs[i // 2]
            out.held[i % 2, :, : 3 * lanes] = ext[i, at, :]
            out.held[i % 2, :, 3 * lanes :] = held[i, at, 3 * lanes :]
            if i % 2:
                out.done()

    return call(
        body,
        "attention_backward",
        bounds,
        [grad_attn, *weights, qkv],
        [array((2, local_rows, width), BF)] * 2,
        [((4, ext_rows, 3 * lanes), BF), ((4, ext_rows, lanes), BF)],
        grant=16,
        cover=40,
    )


def mlp_up(ids, rows, shifts, weights, pair, cover, slopes=True):
    def body(ids, ins, outs, _):
        rows, weights, shifts = (item() for item in ins)
        for i in range(2):

            def block(index, carry):
                at = pl.ds(index * ROW_BLOCK, ROW_BLOCK)
                pre = dot_nn(rows[at, :], weights[i])
                pre = pre + shifts[pl.ds(7 + (ids[0] ^ PARTS[2 * pair + i]), 1), :]
                share = 0.5 * (1.0 + lax.erf(pre * 0.5**0.5))
                outs[0].held[i, at, :] = (pre * share).astype(BF)
                if slopes:
                    density = jnp.exp(-0.5 * pre * pre) * (2.0 * jnp.pi) ** -0.5
                    outs[1].held[i, at, :] = share + pre * density
                return carry

            lax.fori_loop(0, rows.shape[0] // ROW_BLOCK, block, 0)

    shape = (2, rows.shape[0], weights.shape[2])
    return call(
        body,
        "mlp_up",
        ids,
        [rows, weights, shifts],
        [array(shape, BF)] + [array(shape, F32)] * slopes,
        cover=cover,
    )


def norm_back_rows(grad, rows, gain):
    average = jnp.mean(rows, axis=-1, keepdims=True)
    centered = rows - average
    inverse = lax.rsqrt(jnp.mean(centered * centered, axis=-1, keepdims=True) + EPS_NORM)
    normal = centered * inverse
    scaled = grad * gain
    back = inverse * (
        scaled
        - jnp.mean(scaled, axis=-1, keepdims=True)
        - normal * jnp.mean(scaled * normal, axis=-1, keepdims=True)
    )
    return normal, back


def mlp_back(ids, grad_branch, gains, down, up, slopes, grad_out, middle, branch):
    rows, width = grad_branch.shape
    hidden = up[0].shape[2]

    def body(ids, ins, outs, scratch):
        total, sums = scratch[0], outs[4].held
        grad_branch = ins[0]()
        for i in range(4):
            down, slope, up = (item() for item in ins[1 + 3 * i : 4 + 3 * i])
            pre_grads = outs[i // 2]

            def block(index, carry):
                at = pl.ds(index * ROW_BLOCK, ROW_BLOCK)
                back = dot_nn(grad_branch[at, :], down[...])
                pre_grad = (slope[at, :] * back).astype(BF)
                pre_grads.held[i % 2, at, :] = pre_grad
                product = dot_nt(pre_grad, up[...])
                total[at, :] = product if i == 0 else total[at, :] + product
                return carry + column_sum(pre_grad.astype(F32))

            start = jnp.zeros((1, hidden), F32)
            found = lax.fori_loop(0, rows // ROW_BLOCK, block, start)
            sums[pl.ds(4 + (ids[0] ^ PARTS[i]), 1), :] = found
            if i % 2:
                pre_grads.done()
        gains, grad_out, middle, branch = (item() for item in ins[13:])

        def finish(index, carry):
            at = pl.ds(index * 128, 128)
            grad = total[at, :]
            normal, back = norm_back_rows(grad, middle[at, :], gains[1:2, :])
            found = grad_out[at, :] + back
            scaled = (gains[2:3, :] * found).astype(BF)
            outs[2].held[at, :] = found
            outs[3].held[at, :] = scaled
            return (
                carry[0] + column_sum(grad * normal),
                carry[1] + column_sum(grad),
                carry[2] + column_sum(found * branch[at, :]),
                carry[3] + column_sum(scaled.astype(F32)),
            )

        zero = jnp.zeros((1, width), F32)
        found = lax.fori_loop(0, rows // 128, finish, (zero,) * 4)
        for i in range(4):
            sums[i : i + 1, :] = found[i]

    outs = call(
        body,
        "mlp_back",
        ids,
        [grad_branch]
        + [(kind[i // 2], i % 2) for i in range(4) for kind in (down, slopes, up)]
        + [gains, grad_out, middle, branch],
        [array((2, rows, hidden), BF)] * 2
        + [array((rows, width), F32), array((rows, width), BF), array((8, width), F32)],
        [((rows, width), F32)],
        grant=10,
        cover=40,
    )
    return (list(outs[:2]), *outs[2:])


def qkv_back(ids, masked, gains, grads, weights, start, grad_middle, mlp_sums):
    rows, width = start.shape
    lanes = width // 4

    def body(ids, ins, outs, scratch):
        total, sides = scratch
        small = outs[1].held
        grads = [ins[2 + i // 2]().at[i % 2] for i in range(4)]
        for i, part in enumerate(PARTS):
            sides[part : part + 1, :] = column_sum(grads[i][:, :lanes].astype(F32))
            found = column_sum(grads[i][:, 2 * lanes : 3 * lanes].astype(F32))
            sides[4 + part : 5 + part, :] = found
        for i in range(4):
            at = slice(i * lanes, (i + 1) * lanes)
            small[5:6, at] = sides[pl.ds(ids[0] ^ i, 1), :]
            small[6:7, at] = sides[pl.ds(4 + (ids[0] ^ i), 1), :]
        for i in range(4):
            weight = ins[4 + i // 2]().at[i % 2]

            def block(index, carry):
                at = pl.ds(index * ROW_BLOCK, ROW_BLOCK)
                product = dot_nt(grads[i][at, : 3 * lanes], weight[:, : 3 * lanes])
                total[at, :] = product if i == 0 else total[at, :] + product
                return carry

            lax.fori_loop(0, rows // ROW_BLOCK, block, 0)
        masked, gains = ins[0](), ins[1]()
        start, grad_middle, mlp_sums = (item() for item in ins[6:9])

        def finish(index, carry):
            at = pl.ds(index * 128, 128)
            grad = total[at, :]
            normal, back = norm_back_rows(grad, start[at, :], gains[0:1, :])
            found = grad_middle[at, :] + back
            hidden = masked[at, 0:1] > 0.5
            outs[0].held[at, :] = jnp.where(hidden, 0.0, found)
            return (
                carry[0] + column_sum(grad * normal),
                carry[1] + column_sum(grad),
                carry[2] + column_sum(jnp.where(hidden, found, 0.0)),
            )

        zero = jnp.zeros((1, width), F32)
        found = lax.fori_loop(0, rows // 128, finish, (zero,) * 3)
        small[0:1, :], small[4:5, :], small[10:11, :] = found
        small[1:2, :], small[2:3, :] = mlp_sums[0:1, :], mlp_sums[2:3, :]
        small[7:8, :], small[8:9, :] = mlp_sums[3:4, :], mlp_sums[1:2, :]
        small[3:4, :], small[9:10, :] = zero, zero
        small[11:15, :] = mlp_sums[4:8, :]
        small[15:16, :] = zero

    return call(
        body,
        "qkv_back",
        ids,
        [masked, gains, *grads, *weights, start, grad_middle, mlp_sums],
        [array((rows, width), F32), array((16, width), F32)],
        [((rows, width), F32), ((8, lanes), F32)],
        grant=10,
        cover=40,
    )


def weight_grad(ids, lefts, right, other, segments):
    rows, width = lefts[0].shape
    count = lax.axis_size("dp")
    z_count, block = count // 2, width // count
    total = right.shape[2]
    if block % ALIGN:
        found = []
        for which in range(2):
            parts = [
                dot_tn(lefts[2 * left], right[which, :, lane : lane + n])
                + dot_tn(lefts[2 * left + 1], other[which, :, lane : lane + n])
                for left, lane, n in segments
            ]
            found.append(jnp.concatenate(parts, axis=1).reshape(z_count, 2, block, total))
        x = ids[1]

        def at_x(value, which):
            return lax.dynamic_index_in_dim(value, which, 1, keepdims=False)

        own, across = found
        sent = at_x(own, 1 - x), at_x(across, x), at_x(across, 1 - x)
        return tuple(value.astype(BF) for value in sent), at_x(own, x)

    def body(ids, ins, outs, scratch):
        turned, product = scratch
        for i in range(len(lefts)):
            turned[i] = ins[i]()[...].T
        right, other = ins[-2](), ins[-1]()
        to_x, to_y, to_far, kept = outs
        for which, near_out, far_out in ((1, to_y, to_far), (0, kept, to_x)):
            for left, lane, n in segments:
                lanes = slice(lane, lane + n)
                product[:, lanes] = dot_nn(
                    turned[2 * left], right[which, :, lanes]
                ) + dot_nn(turned[2 * left + 1], other[which, :, lanes])
            for z in range(z_count):
                far = pl.multiple_of((2 * z + 1 - ids[1]) * block, ALIGN)
                near = pl.multiple_of((2 * z + ids[1]) * block, ALIGN)
                far_out.held[z] = product[pl.ds(far, block), :].astype(BF)
                near_out.held[z] = product[pl.ds(near, block), :].astype(near_out.held.dtype)
            near_out.done()
            far_out.done()

    shape = (z_count, block, total)
    *sent, kept = call(
        body,
        "weight_grad",
        ids,
        [*lefts, right, other],
        [array(shape, BF)] * 3 + [array(shape, F32)],
        [((len(lefts), width, rows), BF), ((width, total), F32)],
        grant=12,
    )
    return tuple(sent), kept


def first_hop(ids, lefts, right, other, cover=10):
    rows, width = lefts[0].shape
    count, total = lax.axis_size("dp"), right.shape[2]
    z_count, block, half = count // 2, width // count, total // 2
    if block % ALIGN:
        own, across = (
            (dot_tn(lefts[0], right[which]) + dot_tn(lefts[1], other[which])).reshape(
                z_count, 2, block, total
            )
            for which in range(2)
        )
        x = ids[1]

        def at_x(value, which):
            return lax.dynamic_index_in_dim(value[..., half:], which, 1, keepdims=False)

        over_x = jnp.stack([at_x(own, 1 - x), at_x(across, 1 - x)])
        kept = own[..., :half], at_x(across, x), at_x(own, x)
        return (across[..., :half].astype(BF), over_x.astype(BF)), kept

    def body(ids, ins, outs, scratch):
        turned, product = scratch
        for i in range(2):
            turned[i] = ins[i]()[...].T
        right, other = ins[2](), ins[3]()
        over_y, over_x, low, across_high, own_high = (out.held for out in outs)

        def compute(which, lanes):
            return dot_nn(turned[0], right[which, :, lanes]) + dot_nn(
                turned[1], other[which, :, lanes]
            )

        over_y[...] = compute(1, slice(0, half)).astype(BF)
        low[...] = compute(0, slice(0, half))
        for which, kept in ((1, across_high), (0, own_high)):
            product[...] = compute(which, slice(half, total))
            for z in range(z_count):
                far = pl.multiple_of((2 * z + 1 - ids[1]) * block, ALIGN)
                near = pl.multiple_of((2 * z + ids[1]) * block, ALIGN)
                over_x[which, z] = product[pl.ds(far, block), :].astype(BF)
                kept[z] = product[pl.ds(near, block), :]

    high = (z_count, block, half)
    outs = call(
        body,
        "first_hop",
        ids,
        [*lefts, right, other],
        [
            array((width, half), BF),
            array((2,) + high, BF),
            array((width, half), F32),
            array(high, F32),
            array(high, F32),
        ],
        [((2, width, rows), BF), ((width, half), F32)],
        grant=12,
        cover=cover,
    )
    return tuple(outs[:2]), tuple(outs[2:])


def second_hop(ids, chunks):
    z_count, block, half = chunks[0][1][2].shape
    if block % ALIGN:
        x, results = ids[1], []
        for (over_y, over_x), (low, across_high, own_high) in chunks:
            low = low + over_y.astype(F32)
            far, near = (
                lax.dynamic_index_in_dim(low, which, 1, keepdims=False) for which in (1 - x, x)
            )
            high = across_high + over_x[1].astype(F32)
            results.append(
                (far.astype(BF), high.astype(BF), near, own_high + over_x[0].astype(F32))
            )
        joined = [jnp.concatenate(parts, axis=-1) for parts in zip(*results)]
        return tuple(joined[:2]), tuple(joined[2:])

    def body(ids, ins, outs, _):
        sent_x, sent_y, kept_low, kept_high = (out.held for out in outs)
        for i in range(len(chunks)):
            lanes = slice(i * half, (i + 1) * half)
            low, across_high, own_high, over_y, over_x = (
                item() for item in ins[5 * i : 5 * i + 5]
            )
            for z in range(z_count):
                far = pl.ds(pl.multiple_of((2 * z + 1 - ids[1]) * block, ALIGN), block)
                near = pl.ds(pl.multiple_of((2 * z + ids[1]) * block, ALIGN), block)
                sent_x[z, :, lanes] = (low[far, :] + over_y[far, :].astype(F32)).astype(BF)
                kept_low[z, :, lanes] = low[near, :] + over_y[near, :].astype(F32)
                sent_y[z, :, lanes] = (across_high[z] + over_x[1, z].astype(F32)).astype(BF)
                kept_high[z, :, lanes] = own_high[z] + over_x[0, z].astype(F32)

    high = (z_count, block, half * len(chunks))
    outs = call(
        body,
        "second_hop",
        ids,
        [value for received, kept in chunks for value in (*kept, *received)],
        [array(high, BF)] * 2 + [array(high, F32)] * 2,
        cover=2,
    )
    return tuple(outs[:2]), tuple(outs[2:])


def in_halves(value):
    high = value.astype(BF)
    return high, (value - high.astype(F32)).astype(BF)


def plane_sum(ids, parts, vectors=None):
    z_count, block, _ = parts[0][0].shape
    widths = [kept.shape[2] for kept, _ in parts]
    if z_count == 4 and block % ALIGN == 0:

        def body(ids, ins, outs, _):
            for step in (1, 2, 3, 0):
                at, place, lane = lax.rem(ids[2] + step, z_count), 0, 0
                out = outs[step].held
                for (_, received), n in zip(parts, widths):
                    found = ins[place]()[at]
                    for item in ins[place + 1 : place + 1 + len(received)]:
                        found = found + item()[at].astype(F32)
                    out[:block, lane : lane + n] = found.astype(out.dtype)
                    place, lane = place + 1 + len(received), lane + n
                if step and vectors is not None:
                    for i, part in enumerate(in_halves(ins[-1]()[...])):
                        out[block + 16 * i : block + 16 * (i + 1), :] = part

        below = [] if vectors is None else [vectors]
        shape = (block, sum(widths))
        longer = (block + 32 * len(below), sum(widths))
        own, *sent = call(
            body,
            "plane_sum",
            ids,
            [value for kept, received in parts for value in (kept, *received)] + below,
            [array(shape, F32)] + [array(longer, BF)] * 3,
            cover=2,
        )
        return tuple(sent), own
    sums = [sum((value.astype(F32) for value in received), kept) for kept, received in parts]
    return (), jnp.concatenate(sums, axis=-1)


def last_hop(sent, own, steps):
    if not sent:
        return [], own if own.ndim == 2 else scatter_z(own)
    with jax.named_scope("g3z"):
        return [send_digit(sent[step - 1], 1, 4, step) for step in steps], own


def adamw_step(master, first, second, gradient, rate, decay, correction):
    first_new = 0.5 * first + 0.5 * gradient
    second_new = 0.5 * second + 0.5 * gradient * gradient
    update = first_new / correction / (jnp.sqrt(second_new / correction) + ADAM_EPS)
    master_new = master - rate * (update + decay * master)
    return (master_new, first_new, second_new, master_new.astype(BF))


def update_weights(ids, correction, received, own, states, rates, pick, vectors=None, others=()):
    block = own.shape[0]
    if block % ALIGN:
        results = []
        for i, (state, rate) in enumerate(zip(states, rates)):
            results += adamw_step(*state, pick(own, i), rate, DECAY, correction[0, 0])
        return results
    places = list(states) + list(others)

    def body(ids, ins, outs, scratch):
        correction, total = ins[0]()[0:1, 0:1], scratch[0]
        received_refs = [item() for item in ins[2 : 2 + len(received)]]
        found = ins[1]()[...]
        for item in received_refs:
            found = found + item[:block, :].astype(F32)
        total[...] = found
        grads = [(pick, i, rate, DECAY) for i, rate in enumerate(rates)]
        if vectors is not None:
            by_z = scratch[1]
            by_z[ids[2]] = sum(part.astype(F32) for part in in_halves(ins[-1]()[...]))
            for step, item in enumerate(received_refs, 1):
                halves = (item[block + 16 * i : block + 16 * (i + 1), :] for i in range(2))
                at = lax.bitwise_and(ids[2] - step, 3)
                by_z[at] = sum(part.astype(F32) for part in halves)
            sums = (by_z[0] + by_z[1]) + (by_z[2] + by_z[3])
            grads += [
                (lambda _, i: sums[0:4, :], 0, 0.1, 0.0),
                (lambda _, i: sums[4:15, :], 0, 0.3, 0.0),
            ]
        at = 2 + len(received)
        for i, (choose, which, rate, decay) in enumerate(grads):
            master, first, second = (item()[...] for item in ins[at + 3 * i : at + 3 * i + 3])
            results = adamw_step(
                master, first, second, choose(total, which), rate, decay, correction
            )
            for out, value in zip(outs[4 * i : 4 * i + 4], results):
                out.held[...] = value

    outputs = []
    for state in places:
        outputs += [array(state[0].shape, F32)] * 3 + [array(state[0].shape, BF)]
    flat = [value for state in places for value in state]
    scratch = [(own.shape, F32)]
    if vectors is not None:
        flat.append(vectors)
        scratch.append(((4,) + vectors.shape, F32))
    return call(
        body,
        "update_weights",
        ids,
        [correction, own, *received, *flat],
        outputs,
        scratch,
    )


def pack_weights(ids, qkv_master, out_master):
    count, rows, lanes = qkv_master.shape
    if rows % ALIGN:
        parts = [qkv_master[i] for i in range(count)] + [out_master.T]
        return jnp.concatenate(parts, axis=1).astype(BF)

    def body(ids, ins, outs, _):
        qkv = ins[0]()
        for i in range(count):
            outs[0].held[:, i * lanes : (i + 1) * lanes] = qkv[i].astype(BF)
        outs[0].held[:, count * lanes :] = ins[1]()[...].T.astype(BF)

    return call(
        body,
        "pack_weights",
        ids,
        [qkv_master, out_master],
        [array((rows, (count + 1) * lanes), BF)],
    )[0]


def pack_down(ids, up_master, down_turned):
    rows, width = up_master.shape
    if rows % ALIGN:
        return jnp.concatenate([up_master, down_turned], axis=1).astype(BF)

    def body(ids, ins, outs, _):
        outs[0].held[:, :width] = ins[0]()[...].astype(BF)
        outs[0].held[:, width:] = ins[1]()[...].astype(BF)

    return call(
        body, "pack_down", ids, [up_master, down_turned], [array((rows, 2 * width), BF)]
    )[0]


def norm_rows(values, gain, shift):
    average = jnp.mean(values, axis=-1, keepdims=True)
    centered = values - average
    inverse = lax.rsqrt(jnp.mean(centered * centered, axis=-1, keepdims=True) + EPS_NORM)
    return centered * inverse * gain + shift


def on_device(
    patches,
    cotangent,
    mask_rows,
    count_big,
    pos_big,
    pos_small,
    step_count,
    qkv_master,
    qkv_first,
    qkv_second,
    out_master,
    out_first,
    out_second,
    up_master,
    up_first,
    up_second,
    down_master,
    down_first,
    down_second,
    norm_gains,
    gain_first,
    gain_second,
    shifts,
    shift_first,
    shift_second,
):
    tensor_id = lax.axis_index("tensor")
    local_rows = patches.shape[0]
    total_rows = 4 * local_rows
    lanes = qkv_master.shape[2]
    hidden_lanes = up_master.shape[1]
    big_rows = count_big[0] * BIG_LEN
    used_rows = big_rows + (total_rows - big_rows) // SMALL_LEN * SMALL_LEN
    first_row = tensor_id * local_rows

    in_kernels = up_master.shape[0] % ALIGN == 0 and lax.axis_size("dp") == 8
    bounds = image_bounds(count_big[0], first_row, local_rows, total_rows)
    dp_id = lax.axis_index("dp")
    ids = jnp.stack(
        [tensor_id, lax.bitwise_and(dp_id, 1), lax.shift_right_logical(dp_id, 1)]
    ).astype(jnp.int32)
    own = slice(HALO, HALO + local_rows)
    correction = 1.0 - jnp.power(jnp.float32(0.5), step_count[0].astype(F32))

    down_state = (down_master.T, down_first.T, down_second.T)

    local_a = pack_weights(ids, qkv_master, out_master)
    with jax.named_scope("wa"):
        z_a = gather_z(local_a)
    payload = jnp.concatenate(
        [patches, jnp.broadcast_to(mask_rows[:, None].astype(BF), (local_rows, 128))], axis=1
    )
    up_hops, down_hops = [(0, 1), (1, 2), (2, 3)], [(1, 0), (2, 1), (3, 2)]
    with jax.named_scope("halo"):
        halo_before = lax.ppermute(payload[-HALO:], "tensor", up_hops)
        halo_after = lax.ppermute(payload[:HALO], "tensor", down_hops)
    local_bc = pack_down(after(ids, local_a), up_master, down_state[0])

    z_a, halo_before, halo_after, local_bc = gate(z_a, halo_before, halo_after, local_bc)
    (z_a,) = place_z(ids, z_a)
    with jax.named_scope("wbc"):
        z_bc = gather_z(after(local_bc, z_a))
    with jax.named_scope("wa"):
        plane_a = send_plane(z_a, z_a, z_a)
    payload = jnp.concatenate([halo_before, payload, halo_after], axis=0)
    ext_rows = payload.shape[0]
    row_ids = first_row - HALO + jnp.arange(ext_rows, dtype=jnp.int32)
    remainder = row_ids - big_rows
    is_big = (row_ids >= 0) & (row_ids < big_rows)
    is_valid = (row_ids >= 0) & (row_ids < used_rows)
    is_small = is_valid & jnp.logical_not(is_big)
    position = jnp.where(is_big, row_ids % BIG_LEN, remainder % SMALL_LEN)
    masked_ext = (payload[:, D] == 1) & is_valid
    pick_big = (
        (position[:, None] == jnp.arange(BIG_LEN, dtype=jnp.int32)[None, :]) & is_big[:, None]
    ).astype(BF)
    pick_small = (
        (position[:, None] == jnp.arange(SMALL_LEN, dtype=jnp.int32)[None, :]) & is_small[:, None]
    ).astype(BF)
    placed = dot_nn(pick_big, pos_big) + dot_nn(pick_small, pos_small)
    start_ext = (
        jnp.where(masked_ext[:, None], shifts[6][None, :], payload[:, :D].astype(F32)) + placed
    )
    normed_ext = norm_rows(start_ext, norm_gains[0], shifts[0]).astype(BF)
    start_rows, masked, valid_local = start_ext[own], masked_ext[own], is_valid[own]
    normed = normed_ext[own]
    masked = jnp.broadcast_to(masked[:, None].astype(F32), (local_rows, 128))
    grad_out = cotangent.astype(F32) * valid_local[:, None].astype(F32)
    grad_branch = (norm_gains[3] * grad_out).astype(BF)
    biases = jnp.stack(
        [
            jnp.concatenate(
                [
                    lax.dynamic_slice_in_dim(shifts[1], (tensor_id ^ i) * lanes, lanes),
                    jnp.zeros((lanes,), F32),
                    lax.dynamic_slice_in_dim(shifts[2], (tensor_id ^ i) * lanes, lanes),
                    jnp.zeros((lanes,), F32),
                ]
            )
            for i in range(4)
        ]
    )

    z_a, plane_a, z_bc, normed_ext, start_rows, grad_branch, normed, biases = gate(
        z_a, plane_a, z_bc, normed_ext, start_rows, grad_branch, normed, biases
    )
    z_b, z_c = place_z(ids, z_bc, 2)
    with jax.named_scope("wb"):
        plane_b = send_plane(z_b, z_b, z_b)
    own_a = place_x(ids, z_a, *plane_a)
    with jax.named_scope("wa/core"):
        a_all = [own_a, send_core(own_a)]
    with jax.named_scope("pair"):
        grad_branch_other = send_core(grad_branch)
    qkv, branch_attn, middle, normed_two = attention_block(
        after(bounds, z_b), normed_ext, a_all, biases, start_rows, norm_gains, shifts
    )

    plane_b, z_b, z_c, normed_two, grad_branch_other = gate(
        plane_b, z_b, z_c, normed_two, grad_branch_other
    )
    own_b = place_x(ids, z_b, *plane_b)
    with jax.named_scope("wb/core"):
        b_all = [own_b, send_core(own_b)]
    with jax.named_scope("pair"):
        normed_two_other = send_core(normed_two)
    with jax.named_scope("wc"):
        plane_c = send_plane(z_c, z_c, z_c)
    found = mlp_up(ids, normed_two, shifts, b_all[0], 0, 40)
    other = mlp_up(after(ids, found), normed_two, shifts, b_all[1], 1, 0)
    hidden, slopes = zip(found, other)
    (hidden_other,) = mlp_up(after(ids, other), normed_two_other, shifts, own_b, 0, 0, False)
    chunk_c = first_hop(ids, (grad_branch, grad_branch_other), hidden[0], hidden_other, 0)

    plane_c, normed, chunk_c = gate(plane_c, normed, chunk_c)
    own_c = place_x(ids, z_c, *plane_c)
    with jax.named_scope("wc/core"):
        c_all = [own_c, send_core(own_c)]

    with jax.named_scope("gc"):
        first_c = send_first(*chunk_c[0])
    with jax.named_scope("pair"):
        normed_other = send_core(normed)
    pre_grad, grad_middle, grad_attn, mlp_sums = mlp_back(
        ids, grad_branch, norm_gains, c_all, b_all, slopes, grad_out, middle, branch_attn
    )
    first_c, normed_other, pre_grad, grad_attn = gate(first_c, normed_other, pre_grad, grad_attn)
    with jax.named_scope("gb"):
        pre_grad_other = send_core(pre_grad[1])
    with jax.named_scope("halo"):
        halo_before = lax.ppermute(grad_attn[-HALO:], "tensor", up_hops)
        halo_after = lax.ppermute(grad_attn[:HALO], "tensor", down_hops)
    with jax.named_scope("pair"):
        grad_attn_other = send_core(grad_attn)
    sent_c, kept_c = second_hop(ids, ((first_c, chunk_c[1]),))
    chunk_b = first_hop(
        after(ids, sent_c), (normed_two, normed_two_other), pre_grad[0], pre_grad_other
    )
    halo_before, halo_after, chunk_b, sent_c, grad_attn, grad_attn_other = gate(
        halo_before, halo_after, chunk_b, sent_c, grad_attn, grad_attn_other
    )
    with jax.named_scope("gc"):
        second_c = send_second(*sent_c)
    with jax.named_scope("gb"):
        first_b = send_first(*chunk_b[0])
    grad_qkv = attention_backward(
        after(bounds, chunk_b[0]), [halo_before, grad_attn, halo_after], qkv, a_all
    )
    second_c, first_b, grad_qkv = gate(second_c, first_b, grad_qkv)
    sent_b, kept_b = second_hop(ids, ((first_b, chunk_b[1]),))
    with jax.named_scope("gb"):
        second_b = send_second(*sent_b)
    with jax.named_scope("ga"):
        grad_qkv_other = send_core(grad_qkv[1])
    chunk_a = weight_grad(
        after(ids, sent_b),
        (normed, normed_other, grad_attn, grad_attn_other),
        grad_qkv[0],
        grad_qkv_other,
        ((0, 0, 2 * lanes), (0, 2 * lanes, lanes), (1, 3 * lanes, lanes)),
    )
    x_b, chunk_a, grad_qkv = gate(second_b[0], chunk_a, grad_qkv)
    with jax.named_scope("gbc"):
        parts = zip((*kept_c, *kept_b), (*second_c, x_b, second_b[1]))
        sent, sum_bc = plane_sum(ids, [(kept, (value,)) for kept, value in parts])
        early_bc, sum_bc = last_hop(sent, sum_bc, (1, 2))
    with jax.named_scope("ga"):
        plane_a = send_plane(*chunk_a[0])
    patch_grad, small = qkv_back(
        after(ids, sent), masked, norm_gains, grad_qkv, a_all, start_rows, grad_middle, mlp_sums
    )
    hidden = after(hidden, chunk_a)
    branch_mlp = shifts[5] + sum(
        dot_nt(hidden[i // 2][i % 2], c_all[i // 2][i % 2]) for i in range(4)
    )
    layer_out = (middle + norm_gains[3] * branch_mlp).astype(BF)
    extra = [jnp.sum(grad_out * branch_mlp, axis=0), jnp.sum(grad_branch.astype(F32), axis=0)]
    early_bc, sent, small, layer_out, extra, x_a = gate(
        early_bc, sent, small, layer_out, extra, plane_a[0]
    )
    is_row = [lax.broadcasted_iota(jnp.int32, small.shape, 0) == row for row in (3, 9)]
    small = jnp.where(is_row[0], extra[0], jnp.where(is_row[1], extra[1], small))
    with jax.named_scope("small"):
        if not in_kernels:
            small = sum_over_z(small)
    with jax.named_scope("gbc"):
        late_bc, sum_bc = last_hop(sent, sum_bc, (3,))
    last_bc = [*early_bc, *late_bc]
    with jax.named_scope("small"):
        small = sum_over_plane(small)
    *plane_a, small = gate(x_a, *plane_a[1:], small)
    with jax.named_scope("ga"):
        sent, sum_a = plane_sum(ids, [(chunk_a[1], plane_a)], small if in_kernels else None)
        last_a, sum_a = last_hop(sent, sum_a, (1, 2, 3))
    vectors = ((norm_gains, gain_first, gain_second), (shifts, shift_first, shift_second))
    if not in_kernels:
        gain_res = adamw_step(*vectors[0], small[:4], 0.1, 0.0, correction)
        shift_res = adamw_step(*vectors[1], small[4:15], 0.3, 0.0, correction)
    correction = jnp.broadcast_to(correction, (8, 128))
    middle_lane = sum_bc.shape[1] // 2

    def pick_bc(total, i):
        return total[:, middle_lane:] if i == 0 else total[:, :middle_lane]

    def pick_a(total, i):
        if i == 1:
            return total[:, 3 * lanes :].T
        return jnp.stack([total[:, at * lanes : (at + 1) * lanes] for at in range(3)])

    up_down = update_weights(
        after(ids, sent, sum_a),
        correction,
        last_bc,
        sum_bc,
        ((up_master, up_first, up_second), down_state),
        (D ** (-0.5), FF ** (-0.5)),
        pick_bc,
    )
    qkv_out = update_weights(
        after(ids, up_down),
        correction,
        last_a,
        sum_a,
        ((qkv_master, qkv_first, qkv_second), (out_master, out_first, out_second)),
        (D ** (-0.5), (D // 16) ** (-0.5)),
        pick_a,
        *((small, vectors) if in_kernels else ()),
    )
    if in_kernels:
        qkv_out, gain_res, shift_res = qkv_out[:8], qkv_out[8:12], qkv_out[12:]
    down_out = [value.T for value in up_down[4:]]
    return (layer_out, patch_grad, *qkv_out, *up_down[:4], *down_out, *gain_res, *shift_res)


def solution(mesh):
    rows = P(("dp", "tensor"), None)
    qkv = (P(None, "dp", "tensor"),)
    tensor_first, dp_first, whole = (P("tensor", "dp"),), (P("dp", "tensor"),), (P(),)
    weights = tuple(
        spec * 3 for spec in (qkv, tensor_first, dp_first, tensor_first)
    )
    results = tuple(
        spec * 4 for spec in (qkv, tensor_first, dp_first, tensor_first)
    )
    return jax.shard_map(
        on_device,
        mesh=mesh,
        in_specs=(rows, rows, P(("dp", "tensor")), P("dp")) + whole * 3 + sum(weights, ()) + whole * 6,
        out_specs=(rows, rows) + sum(results, ()) + whole * 8,
        check_vma=False,
    )
```

```python
import functools

import jax
import jax.numpy as jnp
import numpy as np
from jax import lax
from jax.experimental import pallas as pl
from jax.experimental.pallas import tpu as pltpu
from jax.sharding import PartitionSpec as P

D = 768
HEAD_DIM = 64
FF = 3072
BIG_LEN = 197
SMALL_LEN = 101
HALO = 208
ALIGN = 16
PARTS = (0, 2, 1, 3)
QUERIES, KEYS = 256, 224
ROW_BLOCK = 256

EPS_NORM = 1e-06
ADAM_EPS = 1e-08
DECAY = 0.05
NEGATIVE = -1e30
FACTOR = HEAD_DIM ** (-0.5)
BF = jnp.bfloat16
F32 = jnp.float32


def send_dp(value, target):
    count = lax.axis_size("dp")
    return lax.ppermute(value, "dp", [(i, target(i)) for i in range(count)])


def send_x(value):
    return send_dp(value, lambda i: i ^ 1)


def send_tensor(value, mask):
    return lax.ppermute(value, "tensor", [(i, i ^ mask) for i in range(4)])


def send_y(value):
    return send_tensor(value, 2)


def send_core(value):
    return send_tensor(value, 1)


def z_digits():
    left = lax.axis_size("dp") // 2
    stride, digits = 1, []
    while left > 1:
        radix = 4 if left % 4 == 0 else 2
        digits.append((stride, radix))
        stride, left = stride * radix, left // radix
    return digits


def send_digit(value, stride, radix, step):
    def target(i):
        z, x = i // 2, i % 2
        digit = z // stride % radix
        return 2 * (z + ((digit + step) % radix - digit) * stride) + x

    return send_dp(value, target)


def gather_z(block):
    block = block[None]
    digits = z_digits()
    for stride, radix in digits[:-1]:
        pieces = [send_digit(block, stride, radix, step) for step in range(1, radix)]
        block = place([block] + pieces, stride, radix)
    stride, radix = digits[-1]
    return [block] + [send_digit(block, stride, radix, step) for step in range(1, radix)]


def place(parts, stride, radix):
    z = lax.shift_right_logical(lax.axis_index("dp"), 1)
    digit = lax.bitwise_and(lax.div(z, stride), radix - 1)
    out = jnp.zeros((radix,) + parts[0].shape, parts[0].dtype)
    for step, piece in enumerate(parts):
        at = lax.bitwise_and(digit - step, radix - 1)
        out = lax.dynamic_update_slice(out, piece[None], (at, 0, 0, 0))
    return out.reshape((-1,) + parts[0].shape[1:])


def scatter_z(partial):
    z = lax.axis_index("dp") // 2
    for stride, radix in reversed(z_digits()):
        digit = z // stride % radix
        parts = partial.reshape((radix, -1) + partial.shape[1:])
        own = lax.dynamic_index_in_dim(parts, digit, 0, keepdims=False)
        pieces = [
            send_digit(
                lax.dynamic_index_in_dim(
                    parts, (digit + step) % radix, 0, keepdims=False
                ).astype(BF),
                stride,
                radix,
                step,
            )
            for step in range(1, radix)
        ]
        for piece in pieces:
            own = own + piece.astype(F32)
        partial = own
    return partial[0]


def after(value, *others):
    return lax.optimization_barrier((value, others))[0]


def gate(*values):
    return lax.optimization_barrier(values)


def send_far(value):
    count = lax.axis_size("dp")
    pairs = [(4 * i + j, 4 * (i ^ 1) + (j ^ 2)) for i in range(count) for j in range(4)]
    return lax.ppermute(value, ("dp", "tensor"), pairs)


def send_near(to_x, to_y):
    with jax.named_scope("x"):
        from_x = send_x(to_x)
    with jax.named_scope("y"):
        return from_x, send_y(to_y)


def send_first(to_y, to_x):
    with jax.named_scope("g1y"):
        from_y = send_y(to_y)
    with jax.named_scope("g1x"):
        return from_y, send_x(to_x)


def send_second(to_x, to_y):
    with jax.named_scope("g2x"):
        from_x = send_x(to_x)
    with jax.named_scope("g2y"):
        return from_x, send_y(to_y)


def send_plane(to_x, to_y, to_far):
    near = send_near(to_x, to_y)
    with jax.named_scope("far"):
        return (*near, send_far(to_far))


def sum_over_z(value):
    bit = 2
    while bit < lax.axis_size("dp"):
        value = value + send_dp(value, lambda i, b=bit: i ^ b)
        bit *= 2
    return value


def sum_over_plane(value):
    for send in (send_core, send_y, send_x):
        value = value + send(value)
    return value


def dot_nt(left, right):
    return lax.dot_general(left, right, (((1,), (1,)), ((), ())), preferred_element_type=F32)


def dot_tn(left, right):
    return lax.dot_general(left, right, (((0,), (0,)), ((), ())), preferred_element_type=F32)


def dot_nn(left, right):
    return jnp.dot(left, right, preferred_element_type=F32)


def array(shape, dtype):
    return jax.ShapeDtypeStruct(shape, dtype)


def column_sum(values):
    return jnp.sum(values, axis=0, keepdims=True)


class Held:
    def __init__(self, held):
        self.held = held

    def __call__(self):
        return self.held

    def done(self, first=None):
        pass


def call(body, name, scalars, inputs, outputs, scratch=(), grant=10, cover=10):
    flat, places = [], []
    for value in inputs:
        group = value if isinstance(value, list) else [value[0] if isinstance(value, tuple) else value]
        places.append([])
        for item in group:
            found = [i for i, other in enumerate(flat) if other is item]
            places[-1].append(found[0] if found else len(flat))
            if not found:
                flat.append(item)
    boxes = [
        pltpu.VMEM((sum(v.shape[0] for v in value),) + value[0].shape[1:], value[0].dtype)
        for value in inputs
        if isinstance(value, list)
    ]

    def kernel(scalar_ref, *refs):
        sources, refs = refs[: len(flat)], refs[len(flat) :]
        targets, refs = refs[: len(outputs)], refs[len(outputs) :]
        joined, extra = iter(refs[: len(boxes)]), refs[len(boxes) :]
        ins = []
        for value, place in zip(inputs, places):
            if isinstance(value, list):
                box, row = next(joined), 0
                for at in place:
                    rows = sources[at].shape[0]
                    box[row : row + rows] = sources[at][...]
                    row += rows
                ins.append(Held(box))
            elif isinstance(value, tuple):
                ins.append(Held(sources[place[0]].at[value[1]]))
            else:
                ins.append(Held(sources[place[0]]))
        body(scalar_ref, ins, [Held(target) for target in targets], extra)

    in_vmem = pl.BlockSpec(memory_space=pltpu.VMEM)
    return pl.pallas_call(
        kernel,
        name=name,
        in_specs=[pl.BlockSpec(memory_space=pltpu.SMEM)] + [in_vmem] * len(flat),
        out_specs=[in_vmem] * len(outputs),
        out_shape=list(outputs),
        scratch_shapes=boxes + [pltpu.VMEM(*box) for box in scratch],
        compiler_params=pltpu.CompilerParams(vmem_limit_bytes=grant << 20),
        cost_estimate=pl.CostEstimate(
            flops=0, transcendentals=0, bytes_accessed=cover * 3 * 10**6
        ),
    )(scalars, *flat)


def move(name, scalars, inputs, outputs, plan, cover=2):
    def kernel(scalar_ref, *refs):
        pairs = plan(scalar_ref, refs[: len(inputs)], refs[len(inputs) : -1])
        copies = [
            pltpu.make_async_copy(source, target, refs[-1].at[i])
            for i, (source, target) in enumerate(pairs)
        ]
        for copy in copies:
            copy.start()
        for copy in copies:
            copy.wait()

    return pl.pallas_call(
        kernel,
        name=name,
        in_specs=[pl.BlockSpec(memory_space=pltpu.SMEM)]
        + [pl.BlockSpec(memory_space=pl.ANY)] * len(inputs),
        out_specs=[pl.BlockSpec(memory_space=pltpu.VMEM)] * len(outputs),
        out_shape=list(outputs),
        scratch_shapes=[pltpu.SemaphoreType.DMA((len(inputs) * len(outputs),))],
        compiler_params=pltpu.CompilerParams(vmem_limit_bytes=1 << 20),
        cost_estimate=pl.CostEstimate(flops=0, transcendentals=0, bytes_accessed=cover * 3 * 10**6),
    )(scalars, *inputs)


def place_z(ids, parts, split=1):
    stride, radix = z_digits()[-1]
    _, rows, n = parts[0].shape
    each = n // split
    if rows % ALIGN or stride != 1:
        whole = place(parts, stride, radix)
        return [whole[..., i * each : (i + 1) * each] for i in range(split)]

    def plan(ids, ins, outs):
        return [
            (
                piece.at[0, :, pl.ds(i * each, each)],
                outs[i].at[lax.bitwise_and(ids[2] - step, radix - 1)],
            )
            for i in range(split)
            for step, piece in enumerate(ins)
        ]

    return move("place_z", ids, parts, [array((radix, rows, each), BF)] * split, plan)


def place_x(ids, mine, from_x, from_y, from_far, cover=2):
    count, rows, n = mine.shape
    if rows % ALIGN:
        x = ids[1]

        def merge(near, far):
            pair = [jnp.where(x == 0, near, far), jnp.where(x == 0, far, near)]
            return jnp.stack(pair, axis=1).reshape(-1, n)

        return jnp.stack([merge(mine, from_x), merge(from_y, from_far)])

    def plan(ids, ins, outs):
        x = ids[1]
        return [
            (ins[0], outs[0].at[0, :, x]),
            (ins[1], outs[0].at[0, :, 1 - x]),
            (ins[2], outs[0].at[1, :, x]),
            (ins[3], outs[0].at[1, :, 1 - x]),
        ]

    shape = (2, count, 2, rows, n)
    inputs = [mine, from_x, from_y, from_far]
    out = move("place_x", ids, inputs, [array(shape, BF)], plan, cover)[0]
    return out.reshape(2, -1, n)


def image_loop(bounds, window):
    big_from, big_count, small_from, count, big_rows, _, total = (bounds[i] for i in range(7))

    def one(index, carry):
        is_big = index < big_count
        big_start = (big_from + index) * BIG_LEN
        small_start = big_rows + (small_from + 2 * (index - big_count)) * SMALL_LEN
        start = jnp.where(is_big, big_start, small_start)
        stop = start + jnp.where(is_big, BIG_LEN, 2 * SMALL_LEN)
        window(start, start + jnp.where(is_big, BIG_LEN, SMALL_LEN), jnp.minimum(stop, total))
        return carry

    lax.fori_loop(0, count, one, 0)


def image_bounds(count_big, first_row, local_rows, total_rows):
    big_rows = count_big * BIG_LEN
    last_row = first_row + local_rows - 1
    big_from = jnp.minimum(first_row // BIG_LEN, count_big)
    big_count = jnp.minimum(last_row // BIG_LEN + 1, count_big) - big_from
    small_from = jnp.maximum(first_row - big_rows, 0) // SMALL_LEN
    small_to = jnp.where(last_row >= big_rows, (last_row - big_rows) // SMALL_LEN + 1, small_from)
    count = big_count + (small_to - small_from + 1) // 2
    base = first_row - HALO
    return jnp.stack(
        [big_from, big_count, small_from, count, big_rows, base, jnp.int32(total_rows), base]
    ).astype(jnp.int32)


class Window:
    def __init__(self, start, middle, stop, base, ext_rows):
        aligned = (start - base) // ALIGN * ALIGN
        at_q = pl.multiple_of(jnp.minimum(aligned, ext_rows - QUERIES), ALIGN)
        at_k = pl.multiple_of(jnp.minimum(aligned, ext_rows - KEYS), ALIGN)

        def ids(offset, shape, axis):
            return lax.broadcasted_iota(jnp.int32, shape, axis) + (offset + base)

        def inside(rows):
            return (rows >= start) & (rows < stop)

        key, query = ids(at_k, (KEYS, 1), 0), ids(at_q, (1, QUERIES), 1)
        self.queries, self.keys = pl.ds(at_q, QUERIES), pl.ds(at_k, KEYS)
        self.query_down = inside(ids(at_q, (QUERIES, 1), 0))
        self.key_down = inside(key)
        key_side = jnp.where(self.key_down, (key >= middle).astype(jnp.int32), 2)
        query_side = (query >= middle).astype(jnp.int32)
        self.same = key_side == query_side
        self.both = key_side == jnp.where(inside(query), query_side, 3)


def softmax_down(key, query, same):
    scores = jnp.where(same, dot_nt(key, query), NEGATIVE)
    exps = jnp.exp(scores - jnp.max(scores, axis=0, keepdims=True))
    return exps * (1.0 / jnp.sum(exps, axis=0, keepdims=True))


def attention_block(bounds, rows, weights, biases, start, gains, shifts):
    ext_rows, width = rows.shape
    lanes = width // 4
    local_rows = start.shape[0]

    def body(bounds, ins, outs, _):
        rows, biases = ins[0](), ins[1]()
        held = outs[0].held
        weights = []
        for i, part in enumerate(PARTS):
            weights.append(ins[2 + i // 2]().at[i % 2])

            def project(index, carry):
                at = pl.ds(index * (ext_rows // 2), ext_rows // 2)
                found = dot_nn(rows[at, :], weights[i][:, : 3 * lanes])
                found = found + biases[part : part + 1, : 3 * lanes]
                held[i, at, : 3 * lanes] = found.astype(BF)
                return carry

            lax.fori_loop(0, 2, project, 0)

        def window(start, middle, stop):
            at = Window(start, middle, stop, bounds[5], ext_rows)

            def pair(index, carry):
                for source in (held.at[index],):
                    parts = []
                    for lane in range(0, lanes, HEAD_DIM):
                        query = source[at.queries, lane : lane + HEAD_DIM] * BF(FACTOR)
                        key = source[at.keys, lanes + lane : lanes + lane + HEAD_DIM]
                        value = source[at.keys, 2 * lanes + lane : 2 * lanes + lane + HEAD_DIM]
                        probs = softmax_down(key, query, at.same)
                        parts.append(dot_nn(value.T, probs.astype(BF)))
                    mixed = jnp.concatenate(parts, axis=0).T.astype(BF)
                    old = source[at.queries, 3 * lanes :]
                    source[at.queries, 3 * lanes :] = jnp.where(at.query_down, mixed, old)
                return carry

            lax.fori_loop(0, 4, pair, 0)

        image_loop(bounds, window)
        outs[0].done()
        start, gains, shifts = (item() for item in ins[4:7])

        def finish(index, carry):
            at = pl.ds(index * 128, 128)
            ext = pl.ds(HALO + index * 128, 128)
            found = shifts[3:4, :]
            for i in range(4):
                found = found + dot_nt(held[i, ext, 3 * lanes :], weights[i][:, 3 * lanes :])
            outs[1].held[at, :] = found
            found = start[at, :] + gains[2:3, :] * found
            outs[2].held[at, :] = found
            outs[3].held[at, :] = norm_rows(found, gains[1:2, :], shifts[4:5, :]).astype(BF)
            return carry

        lax.fori_loop(0, local_rows // 128, finish, 0)

    return call(
        body,
        "attention_block",
        bounds,
        [rows, biases, *weights, start, gains, shifts],
        [array((4, ext_rows, width), BF)]
        + [array((local_rows, width), F32)] * 2
        + [array((local_rows, width), BF)],
        cover=40,
    )


def attention_backward(bounds, grad_attn, qkv, weights):
    _, ext_rows, width = qkv.shape
    lanes = width // 4
    local_rows = ext_rows - 2 * HALO

    def body(bounds, ins, outs, scratch):
        ext, grads = scratch
        grad_attn = ins[0]()
        for i in range(4):
            weight = ins[1 + i // 2]()
            grads[i] = dot_nn(grad_attn[...], weight[i % 2, :, 3 * lanes :]).astype(BF)
        held = ins[3]()

        def window(start, middle, stop):
            at = Window(start, middle, stop, bounds[5], ext_rows)

            def pair(index, carry):
                for part in (2 * index, 2 * index + 1):
                    source, grad, out = held.at[part], grads.at[part], ext.at[part]
                    query_parts, key_parts, value_parts = [], [], []
                    for lane in range(0, lanes, HEAD_DIM):
                        query = source[at.queries, lane : lane + HEAD_DIM] * BF(FACTOR)
                        key = source[at.keys, lanes + lane : lanes + lane + HEAD_DIM]
                        value = source[at.keys, 2 * lanes + lane : 2 * lanes + lane + HEAD_DIM]
                        grad_rows = grad[at.queries, lane : lane + HEAD_DIM]
                        probs = jnp.where(at.both, softmax_down(key, query, at.same), 0.0)
                        weighted = probs * dot_nt(value, grad_rows)
                        inner = jnp.sum(weighted, axis=0, keepdims=True)
                        grad_scores = (weighted - probs * inner).astype(BF)
                        query_parts.append(dot_nn((key * BF(FACTOR)).T, grad_scores))
                        key_parts.append(dot_nn(grad_scores, query))
                        value_parts.append(dot_nn(probs.astype(BF), grad_rows))
                    grad_query = jnp.concatenate(query_parts, axis=0).T.astype(BF)
                    old = out[at.queries, :lanes]
                    out[at.queries, :lanes] = jnp.where(at.query_down, grad_query, old)
                    grad_kv = jnp.concatenate(key_parts + value_parts, axis=1).astype(BF)
                    old = out[at.keys, lanes:]
                    out[at.keys, lanes:] = jnp.where(at.key_down, grad_kv, old)
                return carry

            lax.fori_loop(0, 2, pair, 0)

        image_loop(bounds, window)
        at = slice(HALO, HALO + local_rows)
        for i in (2, 3, 0, 1):
            out = outs[i // 2]
            out.held[i % 2, :, : 3 * lanes] = ext[i, at, :]
            out.held[i % 2, :, 3 * lanes :] = held[i, at, 3 * lanes :]
            if i % 2:
                out.done()

    return call(
        body,
        "attention_backward",
        bounds,
        [grad_attn, *weights, qkv],
        [array((2, local_rows, width), BF)] * 2,
        [((4, ext_rows, 3 * lanes), BF), ((4, ext_rows, lanes), BF)],
        grant=16,
        cover=40,
    )


def mlp_up(ids, rows, shifts, weights, pair, cover, slopes=True):
    def body(ids, ins, outs, _):
        rows, weights, shifts = (item() for item in ins)
        for i in range(2):

            def block(index, carry):
                at = pl.ds(index * ROW_BLOCK, ROW_BLOCK)
                pre = dot_nn(rows[at, :], weights[i])
                pre = pre + shifts[pl.ds(7 + (ids[0] ^ PARTS[2 * pair + i]), 1), :]
                share = 0.5 * (1.0 + lax.erf(pre * 0.5**0.5))
                outs[0].held[i, at, :] = (pre * share).astype(BF)
                if slopes:
                    density = jnp.exp(-0.5 * pre * pre) * (2.0 * jnp.pi) ** -0.5
                    outs[1].held[i, at, :] = share + pre * density
                return carry

            lax.fori_loop(0, rows.shape[0] // ROW_BLOCK, block, 0)

    shape = (2, rows.shape[0], weights.shape[2])
    return call(
        body,
        "mlp_up",
        ids,
        [rows, weights, shifts],
        [array(shape, BF)] + [array(shape, F32)] * slopes,
        cover=cover,
    )


def norm_back_rows(grad, rows, gain):
    average = jnp.mean(rows, axis=-1, keepdims=True)
    centered = rows - average
    inverse = lax.rsqrt(jnp.mean(centered * centered, axis=-1, keepdims=True) + EPS_NORM)
    normal = centered * inverse
    scaled = grad * gain
    back = inverse * (
        scaled
        - jnp.mean(scaled, axis=-1, keepdims=True)
        - normal * jnp.mean(scaled * normal, axis=-1, keepdims=True)
    )
    return normal, back


def mlp_back(ids, grad_branch, gains, down, up, slopes, grad_out, middle, branch):
    rows, width = grad_branch.shape
    hidden = up[0].shape[2]

    def body(ids, ins, outs, scratch):
        total, sums = scratch[0], outs[4].held
        grad_branch = ins[0]()
        for i in range(4):
            down, slope, up = (item() for item in ins[1 + 3 * i : 4 + 3 * i])
            pre_grads = outs[i // 2]

            def block(index, carry):
                at = pl.ds(index * ROW_BLOCK, ROW_BLOCK)
                back = dot_nn(grad_branch[at, :], down[...])
                pre_grad = (slope[at, :] * back).astype(BF)
                pre_grads.held[i % 2, at, :] = pre_grad
                product = dot_nt(pre_grad, up[...])
                total[at, :] = product if i == 0 else total[at, :] + product
                return carry + column_sum(pre_grad.astype(F32))

            start = jnp.zeros((1, hidden), F32)
            found = lax.fori_loop(0, rows // ROW_BLOCK, block, start)
            sums[pl.ds(4 + (ids[0] ^ PARTS[i]), 1), :] = found
            if i % 2:
                pre_grads.done()
        gains, grad_out, middle, branch = (item() for item in ins[13:])

        def finish(index, carry):
            at = pl.ds(index * 128, 128)
            grad = total[at, :]
            normal, back = norm_back_rows(grad, middle[at, :], gains[1:2, :])
            found = grad_out[at, :] + back
            scaled = (gains[2:3, :] * found).astype(BF)
            outs[2].held[at, :] = found
            outs[3].held[at, :] = scaled
            return (
                carry[0] + column_sum(grad * normal),
                carry[1] + column_sum(grad),
                carry[2] + column_sum(found * branch[at, :]),
                carry[3] + column_sum(scaled.astype(F32)),
            )

        zero = jnp.zeros((1, width), F32)
        found = lax.fori_loop(0, rows // 128, finish, (zero,) * 4)
        for i in range(4):
            sums[i : i + 1, :] = found[i]

    outs = call(
        body,
        "mlp_back",
        ids,
        [grad_branch]
        + [(kind[i // 2], i % 2) for i in range(4) for kind in (down, slopes, up)]
        + [gains, grad_out, middle, branch],
        [array((2, rows, hidden), BF)] * 2
        + [array((rows, width), F32), array((rows, width), BF), array((8, width), F32)],
        [((rows, width), F32)],
        grant=10,
        cover=40,
    )
    return (list(outs[:2]), *outs[2:])


def qkv_back(ids, masked, gains, grads, weights, start, grad_middle, mlp_sums):
    rows, width = start.shape
    lanes = width // 4

    def body(ids, ins, outs, scratch):
        total, sides = scratch
        small = outs[1].held
        grads = [ins[2 + i // 2]().at[i % 2] for i in range(4)]
        for i, part in enumerate(PARTS):
            sides[part : part + 1, :] = column_sum(grads[i][:, :lanes].astype(F32))
            found = column_sum(grads[i][:, 2 * lanes : 3 * lanes].astype(F32))
            sides[4 + part : 5 + part, :] = found
        for i in range(4):
            at = slice(i * lanes, (i + 1) * lanes)
            small[5:6, at] = sides[pl.ds(ids[0] ^ i, 1), :]
            small[6:7, at] = sides[pl.ds(4 + (ids[0] ^ i), 1), :]
        for i in range(4):
            weight = ins[4 + i // 2]().at[i % 2]

            def block(index, carry):
                at = pl.ds(index * ROW_BLOCK, ROW_BLOCK)
                product = dot_nt(grads[i][at, : 3 * lanes], weight[:, : 3 * lanes])
                total[at, :] = product if i == 0 else total[at, :] + product
                return carry

            lax.fori_loop(0, rows // ROW_BLOCK, block, 0)
        masked, gains = ins[0](), ins[1]()
        start, grad_middle, mlp_sums = (item() for item in ins[6:9])

        def finish(index, carry):
            at = pl.ds(index * 128, 128)
            grad = total[at, :]
            normal, back = norm_back_rows(grad, start[at, :], gains[0:1, :])
            found = grad_middle[at, :] + back
            hidden = masked[at, 0:1] > 0.5
            outs[0].held[at, :] = jnp.where(hidden, 0.0, found)
            return (
                carry[0] + column_sum(grad * normal),
                carry[1] + column_sum(grad),
                carry[2] + column_sum(jnp.where(hidden, found, 0.0)),
            )

        zero = jnp.zeros((1, width), F32)
        found = lax.fori_loop(0, rows // 128, finish, (zero,) * 3)
        small[0:1, :], small[4:5, :], small[10:11, :] = found
        small[1:2, :], small[2:3, :] = mlp_sums[0:1, :], mlp_sums[2:3, :]
        small[7:8, :], small[8:9, :] = mlp_sums[3:4, :], mlp_sums[1:2, :]
        small[3:4, :], small[9:10, :] = zero, zero
        small[11:15, :] = mlp_sums[4:8, :]
        small[15:16, :] = zero

    return call(
        body,
        "qkv_back",
        ids,
        [masked, gains, *grads, *weights, start, grad_middle, mlp_sums],
        [array((rows, width), F32), array((16, width), F32)],
        [((rows, width), F32), ((8, lanes), F32)],
        grant=10,
        cover=40,
    )


def weight_grad(ids, lefts, right, other, segments):
    rows, width = lefts[0].shape
    count = lax.axis_size("dp")
    z_count, block = count // 2, width // count
    total = right.shape[2]
    if block % ALIGN:
        found = []
        for which in range(2):
            parts = [
                dot_tn(lefts[2 * left], right[which, :, lane : lane + n])
                + dot_tn(lefts[2 * left + 1], other[which, :, lane : lane + n])
                for left, lane, n in segments
            ]
            found.append(jnp.concatenate(parts, axis=1).reshape(z_count, 2, block, total))
        x = ids[1]

        def at_x(value, which):
            return lax.dynamic_index_in_dim(value, which, 1, keepdims=False)

        own, across = found
        sent = at_x(own, 1 - x), at_x(across, x), at_x(across, 1 - x)
        return tuple(value.astype(BF) for value in sent), at_x(own, x)

    def body(ids, ins, outs, scratch):
        turned, product = scratch
        for i in range(len(lefts)):
            turned[i] = ins[i]()[...].T
        right, other = ins[-2](), ins[-1]()
        to_x, to_y, to_far, kept = outs
        for which, near_out, far_out in ((1, to_y, to_far), (0, kept, to_x)):
            for left, lane, n in segments:
                lanes = slice(lane, lane + n)
                product[:, lanes] = dot_nn(
                    turned[2 * left], right[which, :, lanes]
                ) + dot_nn(turned[2 * left + 1], other[which, :, lanes])
            for z in range(z_count):
                far = pl.multiple_of((2 * z + 1 - ids[1]) * block, ALIGN)
                near = pl.multiple_of((2 * z + ids[1]) * block, ALIGN)
                far_out.held[z] = product[pl.ds(far, block), :].astype(BF)
                near_out.held[z] = product[pl.ds(near, block), :].astype(near_out.held.dtype)
            near_out.done()
            far_out.done()

    shape = (z_count, block, total)
    *sent, kept = call(
        body,
        "weight_grad",
        ids,
        [*lefts, right, other],
        [array(shape, BF)] * 3 + [array(shape, F32)],
        [((len(lefts), width, rows), BF), ((width, total), F32)],
        grant=12,
    )
    return tuple(sent), kept


def first_hop(ids, lefts, right, other, cover=10):
    rows, width = lefts[0].shape
    count, total = lax.axis_size("dp"), right.shape[2]
    z_count, block, half = count // 2, width // count, total // 2
    if block % ALIGN:
        own, across = (
            (dot_tn(lefts[0], right[which]) + dot_tn(lefts[1], other[which])).reshape(
                z_count, 2, block, total
            )
            for which in range(2)
        )
        x = ids[1]

        def at_x(value, which):
            return lax.dynamic_index_in_dim(value[..., half:], which, 1, keepdims=False)

        over_x = jnp.stack([at_x(own, 1 - x), at_x(across, 1 - x)])
        kept = own[..., :half], at_x(across, x), at_x(own, x)
        return (across[..., :half].astype(BF), over_x.astype(BF)), kept

    def body(ids, ins, outs, scratch):
        turned, product = scratch
        for i in range(2):
            turned[i] = ins[i]()[...].T
        right, other = ins[2](), ins[3]()
        over_y, over_x, low, across_high, own_high = (out.held for out in outs)

        def compute(which, lanes):
            return dot_nn(turned[0], right[which, :, lanes]) + dot_nn(
                turned[1], other[which, :, lanes]
            )

        over_y[...] = compute(1, slice(0, half)).astype(BF)
        low[...] = compute(0, slice(0, half))
        for which, kept in ((1, across_high), (0, own_high)):
            product[...] = compute(which, slice(half, total))
            for z in range(z_count):
                far = pl.multiple_of((2 * z + 1 - ids[1]) * block, ALIGN)
                near = pl.multiple_of((2 * z + ids[1]) * block, ALIGN)
                over_x[which, z] = product[pl.ds(far, block), :].astype(BF)
                kept[z] = product[pl.ds(near, block), :]

    high = (z_count, block, half)
    outs = call(
        body,
        "first_hop",
        ids,
        [*lefts, right, other],
        [
            array((width, half), BF),
            array((2,) + high, BF),
            array((width, half), F32),
            array(high, F32),
            array(high, F32),
        ],
        [((2, width, rows), BF), ((width, half), F32)],
        grant=12,
        cover=cover,
    )
    return tuple(outs[:2]), tuple(outs[2:])


def second_hop(ids, chunks):
    z_count, block, half = chunks[0][1][2].shape
    if block % ALIGN:
        x, results = ids[1], []
        for (over_y, over_x), (low, across_high, own_high) in chunks:
            low = low + over_y.astype(F32)
            far, near = (
                lax.dynamic_index_in_dim(low, which, 1, keepdims=False) for which in (1 - x, x)
            )
            high = across_high + over_x[1].astype(F32)
            results.append(
                (far.astype(BF), high.astype(BF), near, own_high + over_x[0].astype(F32))
            )
        joined = [jnp.concatenate(parts, axis=-1) for parts in zip(*results)]
        return tuple(joined[:2]), tuple(joined[2:])

    def body(ids, ins, outs, _):
        sent_x, sent_y, kept_low, kept_high = (out.held for out in outs)
        for i in range(len(chunks)):
            lanes = slice(i * half, (i + 1) * half)
            low, across_high, own_high, over_y, over_x = (
                item() for item in ins[5 * i : 5 * i + 5]
            )
            for z in range(z_count):
                far = pl.ds(pl.multiple_of((2 * z + 1 - ids[1]) * block, ALIGN), block)
                near = pl.ds(pl.multiple_of((2 * z + ids[1]) * block, ALIGN), block)
                sent_x[z, :, lanes] = (low[far, :] + over_y[far, :].astype(F32)).astype(BF)
                kept_low[z, :, lanes] = low[near, :] + over_y[near, :].astype(F32)
                sent_y[z, :, lanes] = (across_high[z] + over_x[1, z].astype(F32)).astype(BF)
                kept_high[z, :, lanes] = own_high[z] + over_x[0, z].astype(F32)

    high = (z_count, block, half * len(chunks))
    outs = call(
        body,
        "second_hop",
        ids,
        [value for received, kept in chunks for value in (*kept, *received)],
        [array(high, BF)] * 2 + [array(high, F32)] * 2,
        cover=2,
    )
    return tuple(outs[:2]), tuple(outs[2:])


def in_halves(value):
    high = value.astype(BF)
    return high, (value - high.astype(F32)).astype(BF)


def plane_sum(ids, parts, vectors=None):
    z_count, block, _ = parts[0][0].shape
    widths = [kept.shape[2] for kept, _ in parts]
    if z_count == 4 and block % ALIGN == 0:

        def body(ids, ins, outs, _):
            for step in (1, 2, 3, 0):
                at, place, lane = lax.rem(ids[2] + step, z_count), 0, 0
                out = outs[step].held
                for (_, received), n in zip(parts, widths):
                    found = ins[place]()[at]
                    for item in ins[place + 1 : place + 1 + len(received)]:
                        found = found + item()[at].astype(F32)
                    out[:block, lane : lane + n] = found.astype(out.dtype)
                    place, lane = place + 1 + len(received), lane + n
                if step and vectors is not None:
                    for i, part in enumerate(in_halves(ins[-1]()[...])):
                        out[block + 16 * i : block + 16 * (i + 1), :] = part

        below = [] if vectors is None else [vectors]
        shape = (block, sum(widths))
        longer = (block + 32 * len(below), sum(widths))
        own, *sent = call(
            body,
            "plane_sum",
            ids,
            [value for kept, received in parts for value in (kept, *received)] + below,
            [array(shape, F32)] + [array(longer, BF)] * 3,
            cover=2,
        )
        return tuple(sent), own
    sums = [sum((value.astype(F32) for value in received), kept) for kept, received in parts]
    return (), jnp.concatenate(sums, axis=-1)


def last_hop(sent, own, steps):
    if not sent:
        return [], own if own.ndim == 2 else scatter_z(own)
    with jax.named_scope("g3z"):
        return [send_digit(sent[step - 1], 1, 4, step) for step in steps], own


def adamw_step(master, first, second, gradient, rate, decay, correction):
    first_new = 0.5 * first + 0.5 * gradient
    second_new = 0.5 * second + 0.5 * gradient * gradient
    update = first_new / correction / (jnp.sqrt(second_new / correction) + ADAM_EPS)
    master_new = master - rate * (update + decay * master)
    return (master_new, first_new, second_new, master_new.astype(BF))


def update_weights(ids, correction, received, own, states, rates, pick, vectors=None, others=()):
    block = own.shape[0]
    if block % ALIGN:
        results = []
        for i, (state, rate) in enumerate(zip(states, rates)):
            results += adamw_step(*state, pick(own, i), rate, DECAY, correction[0, 0])
        return results
    places = list(states) + list(others)

    def body(ids, ins, outs, scratch):
        correction, total = ins[0]()[0:1, 0:1], scratch[0]
        received_refs = [item() for item in ins[2 : 2 + len(received)]]
        found = ins[1]()[...]
        for item in received_refs:
            found = found + item[:block, :].astype(F32)
        total[...] = found
        grads = [(pick, i, rate, DECAY) for i, rate in enumerate(rates)]
        if vectors is not None:
            by_z = scratch[1]
            by_z[ids[2]] = sum(part.astype(F32) for part in in_halves(ins[-1]()[...]))
            for step, item in enumerate(received_refs, 1):
                halves = (item[block + 16 * i : block + 16 * (i + 1), :] for i in range(2))
                at = lax.bitwise_and(ids[2] - step, 3)
                by_z[at] = sum(part.astype(F32) for part in halves)
            sums = (by_z[0] + by_z[1]) + (by_z[2] + by_z[3])
            grads += [
                (lambda _, i: sums[0:4, :], 0, 0.1, 0.0),
                (lambda _, i: sums[4:15, :], 0, 0.3, 0.0),
            ]
        at = 2 + len(received)
        for i, (choose, which, rate, decay) in enumerate(grads):
            master, first, second = (item()[...] for item in ins[at + 3 * i : at + 3 * i + 3])
            results = adamw_step(
                master, first, second, choose(total, which), rate, decay, correction
            )
            for out, value in zip(outs[4 * i : 4 * i + 4], results):
                out.held[...] = value

    outputs = []
    for state in places:
        outputs += [array(state[0].shape, F32)] * 3 + [array(state[0].shape, BF)]
    flat = [value for state in places for value in state]
    scratch = [(own.shape, F32)]
    if vectors is not None:
        flat.append(vectors)
        scratch.append(((4,) + vectors.shape, F32))
    return call(
        body,
        "update_weights",
        ids,
        [correction, own, *received, *flat],
        outputs,
        scratch,
    )


def pack_weights(ids, qkv_master, out_master):
    count, rows, lanes = qkv_master.shape
    if rows % ALIGN:
        parts = [qkv_master[i] for i in range(count)] + [out_master.T]
        return jnp.concatenate(parts, axis=1).astype(BF)

    def body(ids, ins, outs, _):
        qkv = ins[0]()
        for i in range(count):
            outs[0].held[:, i * lanes : (i + 1) * lanes] = qkv[i].astype(BF)
        outs[0].held[:, count * lanes :] = ins[1]()[...].T.astype(BF)

    return call(
        body,
        "pack_weights",
        ids,
        [qkv_master, out_master],
        [array((rows, (count + 1) * lanes), BF)],
    )[0]


def pack_down(ids, up_master, down_turned):
    rows, width = up_master.shape
    if rows % ALIGN:
        return jnp.concatenate([up_master, down_turned], axis=1).astype(BF)

    def body(ids, ins, outs, _):
        outs[0].held[:, :width] = ins[0]()[...].astype(BF)
        outs[0].held[:, width:] = ins[1]()[...].astype(BF)

    return call(
        body, "pack_down", ids, [up_master, down_turned], [array((rows, 2 * width), BF)]
    )[0]


def norm_rows(values, gain, shift):
    average = jnp.mean(values, axis=-1, keepdims=True)
    centered = values - average
    inverse = lax.rsqrt(jnp.mean(centered * centered, axis=-1, keepdims=True) + EPS_NORM)
    return centered * inverse * gain + shift


def on_device(
    patches,
    cotangent,
    mask_rows,
    count_big,
    pos_big,
    pos_small,
    step_count,
    qkv_master,
    qkv_first,
    qkv_second,
    out_master,
    out_first,
    out_second,
    up_master,
    up_first,
    up_second,
    down_master,
    down_first,
    down_second,
    norm_gains,
    gain_first,
    gain_second,
    shifts,
    shift_first,
    shift_second,
):
    tensor_id = lax.axis_index("tensor")
    local_rows = patches.shape[0]
    total_rows = 4 * local_rows
    lanes = qkv_master.shape[2]
    hidden_lanes = up_master.shape[1]
    big_rows = count_big[0] * BIG_LEN
    used_rows = big_rows + (total_rows - big_rows) // SMALL_LEN * SMALL_LEN
    first_row = tensor_id * local_rows

    in_kernels = up_master.shape[0] % ALIGN == 0 and lax.axis_size("dp") == 8
    bounds = image_bounds(count_big[0], first_row, local_rows, total_rows)
    dp_id = lax.axis_index("dp")
    ids = jnp.stack(
        [tensor_id, lax.bitwise_and(dp_id, 1), lax.shift_right_logical(dp_id, 1)]
    ).astype(jnp.int32)
    own = slice(HALO, HALO + local_rows)
    correction = 1.0 - jnp.power(jnp.float32(0.5), step_count[0].astype(F32))

    down_state = (down_master.T, down_first.T, down_second.T)

    local_a = pack_weights(ids, qkv_master, out_master)
    with jax.named_scope("wa"):
        z_a = gather_z(local_a)
    payload = jnp.concatenate(
        [patches, jnp.broadcast_to(mask_rows[:, None].astype(BF), (local_rows, 128))], axis=1
    )
    up_hops, down_hops = [(0, 1), (1, 2), (2, 3)], [(1, 0), (2, 1), (3, 2)]
    with jax.named_scope("halo"):
        halo_before = lax.ppermute(payload[-HALO:], "tensor", up_hops)
        halo_after = lax.ppermute(payload[:HALO], "tensor", down_hops)
    local_bc = pack_down(after(ids, local_a), up_master, down_state[0])

    z_a, halo_before, halo_after, local_bc = gate(z_a, halo_before, halo_after, local_bc)
    (z_a,) = place_z(ids, z_a)
    with jax.named_scope("wbc"):
        z_bc = gather_z(after(local_bc, z_a))
    with jax.named_scope("wa"):
        plane_a = send_plane(z_a, z_a, z_a)
    payload = jnp.concatenate([halo_before, payload, halo_after], axis=0)
    ext_rows = payload.shape[0]
    row_ids = first_row - HALO + jnp.arange(ext_rows, dtype=jnp.int32)
    remainder = row_ids - big_rows
    is_big = (row_ids >= 0) & (row_ids < big_rows)
    is_valid = (row_ids >= 0) & (row_ids < used_rows)
    is_small = is_valid & jnp.logical_not(is_big)
    position = jnp.where(is_big, row_ids % BIG_LEN, remainder % SMALL_LEN)
    masked_ext = (payload[:, D] == 1) & is_valid
    pick_big = (
        (position[:, None] == jnp.arange(BIG_LEN, dtype=jnp.int32)[None, :]) & is_big[:, None]
    ).astype(BF)
    pick_small = (
        (position[:, None] == jnp.arange(SMALL_LEN, dtype=jnp.int32)[None, :]) & is_small[:, None]
    ).astype(BF)
    placed = dot_nn(pick_big, pos_big) + dot_nn(pick_small, pos_small)
    start_ext = (
        jnp.where(masked_ext[:, None], shifts[6][None, :], payload[:, :D].astype(F32)) + placed
    )
    normed_ext = norm_rows(start_ext, norm_gains[0], shifts[0]).astype(BF)
    start_rows, masked, valid_local = start_ext[own], masked_ext[own], is_valid[own]
    normed = normed_ext[own]
    masked = jnp.broadcast_to(masked[:, None].astype(F32), (local_rows, 128))
    grad_out = cotangent.astype(F32) * valid_local[:, None].astype(F32)
    grad_branch = (norm_gains[3] * grad_out).astype(BF)
    biases = jnp.stack(
        [
            jnp.concatenate(
                [
                    lax.dynamic_slice_in_dim(shifts[1], (tensor_id ^ i) * lanes, lanes),
                    jnp.zeros((lanes,), F32),
                    lax.dynamic_slice_in_dim(shifts[2], (tensor_id ^ i) * lanes, lanes),
                    jnp.zeros((lanes,), F32),
                ]
            )
            for i in range(4)
        ]
    )

    z_a, plane_a, z_bc, normed_ext, start_rows, grad_branch, normed, biases = gate(
        z_a, plane_a, z_bc, normed_ext, start_rows, grad_branch, normed, biases
    )
    z_b, z_c = place_z(ids, z_bc, 2)
    with jax.named_scope("wb"):
        plane_b = send_plane(z_b, z_b, z_b)
    own_a = place_x(ids, z_a, *plane_a)
    with jax.named_scope("wa/core"):
        a_all = [own_a, send_core(own_a)]
    with jax.named_scope("pair"):
        grad_branch_other = send_core(grad_branch)
    qkv, branch_attn, middle, normed_two = attention_block(
        after(bounds, z_b), normed_ext, a_all, biases, start_rows, norm_gains, shifts
    )

    plane_b, z_b, z_c, normed_two, grad_branch_other = gate(
        plane_b, z_b, z_c, normed_two, grad_branch_other
    )
    own_b = place_x(ids, z_b, *plane_b)
    with jax.named_scope("wb/core"):
        b_all = [own_b, send_core(own_b)]
    with jax.named_scope("pair"):
        normed_two_other = send_core(normed_two)
    with jax.named_scope("wc"):
        plane_c = send_plane(z_c, z_c, z_c)
    found = mlp_up(ids, normed_two, shifts, b_all[0], 0, 40)
    other = mlp_up(after(ids, found), normed_two, shifts, b_all[1], 1, 0)
    hidden, slopes = zip(found, other)
    (hidden_other,) = mlp_up(after(ids, other), normed_two_other, shifts, own_b, 0, 0, False)
    chunk_c = first_hop(ids, (grad_branch, grad_branch_other), hidden[0], hidden_other, 0)

    plane_c, normed, chunk_c = gate(plane_c, normed, chunk_c)
    own_c = place_x(ids, z_c, *plane_c)
    with jax.named_scope("wc/core"):
        c_all = [own_c, send_core(own_c)]

    with jax.named_scope("gc"):
        first_c = send_first(*chunk_c[0])
    with jax.named_scope("pair"):
        normed_other = send_core(normed)
    pre_grad, grad_middle, grad_attn, mlp_sums = mlp_back(
        ids, grad_branch, norm_gains, c_all, b_all, slopes, grad_out, middle, branch_attn
    )
    first_c, normed_other, pre_grad, grad_attn = gate(first_c, normed_other, pre_grad, grad_attn)
    with jax.named_scope("gb"):
        pre_grad_other = send_core(pre_grad[1])
    with jax.named_scope("halo"):
        halo_before = lax.ppermute(grad_attn[-HALO:], "tensor", up_hops)
        halo_after = lax.ppermute(grad_attn[:HALO], "tensor", down_hops)
    with jax.named_scope("pair"):
        grad_attn_other = send_core(grad_attn)
    sent_c, kept_c = second_hop(ids, ((first_c, chunk_c[1]),))
    chunk_b = first_hop(
        after(ids, sent_c), (normed_two, normed_two_other), pre_grad[0], pre_grad_other
    )
    halo_before, halo_after, chunk_b, sent_c, grad_attn, grad_attn_other = gate(
        halo_before, halo_after, chunk_b, sent_c, grad_attn, grad_attn_other
    )
    with jax.named_scope("gc"):
        second_c = send_second(*sent_c)
    with jax.named_scope("gb"):
        first_b = send_first(*chunk_b[0])
    grad_qkv = attention_backward(
        after(bounds, chunk_b[0]), [halo_before, grad_attn, halo_after], qkv, a_all
    )
    second_c, first_b, grad_qkv = gate(second_c, first_b, grad_qkv)
    sent_b, kept_b = second_hop(ids, ((first_b, chunk_b[1]),))
    with jax.named_scope("gb"):
        second_b = send_second(*sent_b)
    with jax.named_scope("ga"):
        grad_qkv_other = send_core(grad_qkv[1])
    chunk_a = weight_grad(
        after(ids, sent_b),
        (normed, normed_other, grad_attn, grad_attn_other),
        grad_qkv[0],
        grad_qkv_other,
        ((0, 0, 2 * lanes), (0, 2 * lanes, lanes), (1, 3 * lanes, lanes)),
    )
    x_b, chunk_a, grad_qkv = gate(second_b[0], chunk_a, grad_qkv)
    with jax.named_scope("gbc"):
        parts = zip((*kept_c, *kept_b), (*second_c, x_b, second_b[1]))
        sent, sum_bc = plane_sum(ids, [(kept, (value,)) for kept, value in parts])
        early_bc, sum_bc = last_hop(sent, sum_bc, (2,))
    with jax.named_scope("ga"):
        plane_a = send_plane(*chunk_a[0])
    patch_grad, small = qkv_back(
        after(ids, sent), masked, norm_gains, grad_qkv, a_all, start_rows, grad_middle, mlp_sums
    )
    hidden = after(hidden, chunk_a)
    branch_mlp = shifts[5] + sum(
        dot_nt(hidden[i // 2][i % 2], c_all[i // 2][i % 2]) for i in range(4)
    )
    layer_out = (middle + norm_gains[3] * branch_mlp).astype(BF)
    extra = [jnp.sum(grad_out * branch_mlp, axis=0), jnp.sum(grad_branch.astype(F32), axis=0)]
    early_bc, sent, small, layer_out, extra, x_a = gate(
        early_bc, sent, small, layer_out, extra, plane_a[0]
    )
    is_row = [lax.broadcasted_iota(jnp.int32, small.shape, 0) == row for row in (3, 9)]
    small = jnp.where(is_row[0], extra[0], jnp.where(is_row[1], extra[1], small))
    with jax.named_scope("small"):
        if not in_kernels:
            small = sum_over_z(small)
    with jax.named_scope("gbc"):
        late_bc, sum_bc = last_hop(sent, sum_bc, (1, 3))
    last_bc = [*early_bc, *late_bc]
    with jax.named_scope("small"):
        small = sum_over_plane(small)
    *plane_a, small = gate(x_a, *plane_a[1:], small)
    with jax.named_scope("ga"):
        sent, sum_a = plane_sum(ids, [(chunk_a[1], plane_a)], small if in_kernels else None)
        last_a, sum_a = last_hop(sent, sum_a, (1, 2, 3))
    vectors = ((norm_gains, gain_first, gain_second), (shifts, shift_first, shift_second))
    if not in_kernels:
        gain_res = adamw_step(*vectors[0], small[:4], 0.1, 0.0, correction)
        shift_res = adamw_step(*vectors[1], small[4:15], 0.3, 0.0, correction)
    correction = jnp.broadcast_to(correction, (8, 128))
    middle_lane = sum_bc.shape[1] // 2

    def pick_bc(total, i):
        return total[:, middle_lane:] if i == 0 else total[:, :middle_lane]

    def pick_a(total, i):
        if i == 1:
            return total[:, 3 * lanes :].T
        return jnp.stack([total[:, at * lanes : (at + 1) * lanes] for at in range(3)])

    up_down = update_weights(
        after(ids, sent, sum_a),
        correction,
        last_bc,
        sum_bc,
        ((up_master, up_first, up_second), down_state),
        (D ** (-0.5), FF ** (-0.5)),
        pick_bc,
    )
    qkv_out = update_weights(
        after(ids, up_down),
        correction,
        last_a,
        sum_a,
        ((qkv_master, qkv_first, qkv_second), (out_master, out_first, out_second)),
        (D ** (-0.5), (D // 16) ** (-0.5)),
        pick_a,
        *((small, vectors) if in_kernels else ()),
    )
    if in_kernels:
        qkv_out, gain_res, shift_res = qkv_out[:8], qkv_out[8:12], qkv_out[12:]
    down_out = [value.T for value in up_down[4:]]
    return (layer_out, patch_grad, *qkv_out, *up_down[:4], *down_out, *gain_res, *shift_res)


def solution(mesh):
    rows = P(("dp", "tensor"), None)
    qkv = (P(None, "dp", "tensor"),)
    tensor_first, dp_first, whole = (P("tensor", "dp"),), (P("dp", "tensor"),), (P(),)
    weights = tuple(
        spec * 3 for spec in (qkv, tensor_first, dp_first, tensor_first)
    )
    results = tuple(
        spec * 4 for spec in (qkv, tensor_first, dp_first, tensor_first)
    )
    return jax.shard_map(
        on_device,
        mesh=mesh,
        in_specs=(rows, rows, P(("dp", "tensor")), P("dp")) + whole * 3 + sum(weights, ()) + whole * 6,
        out_specs=(rows, rows) + sum(results, ()) + whole * 8,
        check_vma=False,
    )
```

```python
import functools

import jax
import jax.numpy as jnp
import numpy as np
from jax import lax
from jax.experimental import pallas as pl
from jax.experimental.pallas import tpu as pltpu
from jax.sharding import PartitionSpec as P

D = 768
HEAD_DIM = 64
FF = 3072
BIG_LEN = 197
SMALL_LEN = 101
HALO = 208
ALIGN = 16
PARTS = (0, 2, 1, 3)
QUERIES, KEYS = 256, 224
ROW_BLOCK = 512

EPS_NORM = 1e-06
ADAM_EPS = 1e-08
DECAY = 0.05
NEGATIVE = -1e30
FACTOR = HEAD_DIM ** (-0.5)
BF = jnp.bfloat16
F32 = jnp.float32


def send_dp(value, target):
    count = lax.axis_size("dp")
    return lax.ppermute(value, "dp", [(i, target(i)) for i in range(count)])


def send_x(value):
    return send_dp(value, lambda i: i ^ 1)


def send_tensor(value, mask):
    return lax.ppermute(value, "tensor", [(i, i ^ mask) for i in range(4)])


def send_y(value):
    return send_tensor(value, 2)


def send_core(value):
    return send_tensor(value, 1)


def z_digits():
    left = lax.axis_size("dp") // 2
    stride, digits = 1, []
    while left > 1:
        radix = 4 if left % 4 == 0 else 2
        digits.append((stride, radix))
        stride, left = stride * radix, left // radix
    return digits


def send_digit(value, stride, radix, step):
    def target(i):
        z, x = i // 2, i % 2
        digit = z // stride % radix
        return 2 * (z + ((digit + step) % radix - digit) * stride) + x

    return send_dp(value, target)


def gather_z(block):
    block = block[None]
    digits = z_digits()
    for stride, radix in digits[:-1]:
        pieces = [send_digit(block, stride, radix, step) for step in range(1, radix)]
        block = place([block] + pieces, stride, radix)
    stride, radix = digits[-1]
    return [block] + [send_digit(block, stride, radix, step) for step in range(1, radix)]


def place(parts, stride, radix):
    z = lax.shift_right_logical(lax.axis_index("dp"), 1)
    digit = lax.bitwise_and(lax.div(z, stride), radix - 1)
    out = jnp.zeros((radix,) + parts[0].shape, parts[0].dtype)
    for step, piece in enumerate(parts):
        at = lax.bitwise_and(digit - step, radix - 1)
        out = lax.dynamic_update_slice(out, piece[None], (at, 0, 0, 0))
    return out.reshape((-1,) + parts[0].shape[1:])


def scatter_z(partial):
    z = lax.axis_index("dp") // 2
    for stride, radix in reversed(z_digits()):
        digit = z // stride % radix
        parts = partial.reshape((radix, -1) + partial.shape[1:])
        own = lax.dynamic_index_in_dim(parts, digit, 0, keepdims=False)
        pieces = [
            send_digit(
                lax.dynamic_index_in_dim(
                    parts, (digit + step) % radix, 0, keepdims=False
                ).astype(BF),
                stride,
                radix,
                step,
            )
            for step in range(1, radix)
        ]
        for piece in pieces:
            own = own + piece.astype(F32)
        partial = own
    return partial[0]


def after(value, *others):
    return lax.optimization_barrier((value, others))[0]


def gate(*values):
    return lax.optimization_barrier(values)


def send_far(value):
    count = lax.axis_size("dp")
    pairs = [(4 * i + j, 4 * (i ^ 1) + (j ^ 2)) for i in range(count) for j in range(4)]
    return lax.ppermute(value, ("dp", "tensor"), pairs)


def send_near(to_x, to_y):
    with jax.named_scope("x"):
        from_x = send_x(to_x)
    with jax.named_scope("y"):
        return from_x, send_y(to_y)


def send_first(to_y, to_x):
    with jax.named_scope("g1y"):
        from_y = send_y(to_y)
    with jax.named_scope("g1x"):
        return from_y, send_x(to_x)


def send_second(to_x, to_y):
    with jax.named_scope("g2x"):
        from_x = send_x(to_x)
    with jax.named_scope("g2y"):
        return from_x, send_y(to_y)


def send_plane(to_x, to_y, to_far):
    near = send_near(to_x, to_y)
    with jax.named_scope("far"):
        return (*near, send_far(to_far))


def sum_over_z(value):
    bit = 2
    while bit < lax.axis_size("dp"):
        value = value + send_dp(value, lambda i, b=bit: i ^ b)
        bit *= 2
    return value


def sum_over_plane(value):
    for send in (send_core, send_y, send_x):
        value = value + send(value)
    return value


def dot_nt(left, right):
    return lax.dot_general(left, right, (((1,), (1,)), ((), ())), preferred_element_type=F32)


def dot_tn(left, right):
    return lax.dot_general(left, right, (((0,), (0,)), ((), ())), preferred_element_type=F32)


def dot_nn(left, right):
    return jnp.dot(left, right, preferred_element_type=F32)


def array(shape, dtype):
    return jax.ShapeDtypeStruct(shape, dtype)


def column_sum(values):
    return jnp.sum(values, axis=0, keepdims=True)


class Held:
    def __init__(self, held):
        self.held = held

    def __call__(self):
        return self.held

    def done(self, first=None):
        pass


def call(body, name, scalars, inputs, outputs, scratch=(), grant=10, cover=10):
    flat, places = [], []
    for value in inputs:
        group = value if isinstance(value, list) else [value[0] if isinstance(value, tuple) else value]
        places.append([])
        for item in group:
            found = [i for i, other in enumerate(flat) if other is item]
            places[-1].append(found[0] if found else len(flat))
            if not found:
                flat.append(item)
    boxes = [
        pltpu.VMEM((sum(v.shape[0] for v in value),) + value[0].shape[1:], value[0].dtype)
        for value in inputs
        if isinstance(value, list)
    ]

    def kernel(scalar_ref, *refs):
        sources, refs = refs[: len(flat)], refs[len(flat) :]
        targets, refs = refs[: len(outputs)], refs[len(outputs) :]
        joined, extra = iter(refs[: len(boxes)]), refs[len(boxes) :]
        ins = []
        for value, place in zip(inputs, places):
            if isinstance(value, list):
                box, row = next(joined), 0
                for at in place:
                    rows = sources[at].shape[0]
                    box[row : row + rows] = sources[at][...]
                    row += rows
                ins.append(Held(box))
            elif isinstance(value, tuple):
                ins.append(Held(sources[place[0]].at[value[1]]))
            else:
                ins.append(Held(sources[place[0]]))
        body(scalar_ref, ins, [Held(target) for target in targets], extra)

    in_vmem = pl.BlockSpec(memory_space=pltpu.VMEM)
    return pl.pallas_call(
        kernel,
        name=name,
        in_specs=[pl.BlockSpec(memory_space=pltpu.SMEM)] + [in_vmem] * len(flat),
        out_specs=[in_vmem] * len(outputs),
        out_shape=list(outputs),
        scratch_shapes=boxes + [pltpu.VMEM(*box) for box in scratch],
        compiler_params=pltpu.CompilerParams(vmem_limit_bytes=grant << 20),
        cost_estimate=pl.CostEstimate(
            flops=0, transcendentals=0, bytes_accessed=cover * 3 * 10**6
        ),
    )(scalars, *flat)


def move(name, scalars, inputs, outputs, plan, cover=2):
    def kernel(scalar_ref, *refs):
        pairs = plan(scalar_ref, refs[: len(inputs)], refs[len(inputs) : -1])
        copies = [
            pltpu.make_async_copy(source, target, refs[-1].at[i])
            for i, (source, target) in enumerate(pairs)
        ]
        for copy in copies:
            copy.start()
        for copy in copies:
            copy.wait()

    return pl.pallas_call(
        kernel,
        name=name,
        in_specs=[pl.BlockSpec(memory_space=pltpu.SMEM)]
        + [pl.BlockSpec(memory_space=pl.ANY)] * len(inputs),
        out_specs=[pl.BlockSpec(memory_space=pltpu.VMEM)] * len(outputs),
        out_shape=list(outputs),
        scratch_shapes=[pltpu.SemaphoreType.DMA((len(inputs) * len(outputs),))],
        compiler_params=pltpu.CompilerParams(vmem_limit_bytes=1 << 20),
        cost_estimate=pl.CostEstimate(flops=0, transcendentals=0, bytes_accessed=cover * 3 * 10**6),
    )(scalars, *inputs)


def place_z(ids, parts, split=1):
    stride, radix = z_digits()[-1]
    _, rows, n = parts[0].shape
    each = n // split
    if rows % ALIGN or stride != 1:
        whole = place(parts, stride, radix)
        return [whole[..., i * each : (i + 1) * each] for i in range(split)]

    def plan(ids, ins, outs):
        return [
            (
                piece.at[0, :, pl.ds(i * each, each)],
                outs[i].at[lax.bitwise_and(ids[2] - step, radix - 1)],
            )
            for i in range(split)
            for step, piece in enumerate(ins)
        ]

    return move("place_z", ids, parts, [array((radix, rows, each), BF)] * split, plan)


def place_x(ids, mine, from_x, from_y, from_far, cover=2):
    count, rows, n = mine.shape
    if rows % ALIGN:
        x = ids[1]

        def merge(near, far):
            pair = [jnp.where(x == 0, near, far), jnp.where(x == 0, far, near)]
            return jnp.stack(pair, axis=1).reshape(-1, n)

        return jnp.stack([merge(mine, from_x), merge(from_y, from_far)])

    def plan(ids, ins, outs):
        x = ids[1]
        return [
            (ins[0], outs[0].at[0, :, x]),
            (ins[1], outs[0].at[0, :, 1 - x]),
            (ins[2], outs[0].at[1, :, x]),
            (ins[3], outs[0].at[1, :, 1 - x]),
        ]

    shape = (2, count, 2, rows, n)
    inputs = [mine, from_x, from_y, from_far]
    out = move("place_x", ids, inputs, [array(shape, BF)], plan, cover)[0]
    return out.reshape(2, -1, n)


def image_loop(bounds, window):
    big_from, big_count, small_from, count, big_rows, _, total = (bounds[i] for i in range(7))

    def one(index, carry):
        is_big = index < big_count
        big_start = (big_from + index) * BIG_LEN
        small_start = big_rows + (small_from + 2 * (index - big_count)) * SMALL_LEN
        start = jnp.where(is_big, big_start, small_start)
        stop = start + jnp.where(is_big, BIG_LEN, 2 * SMALL_LEN)
        window(start, start + jnp.where(is_big, BIG_LEN, SMALL_LEN), jnp.minimum(stop, total))
        return carry

    lax.fori_loop(0, count, one, 0)


def image_bounds(count_big, first_row, local_rows, total_rows):
    big_rows = count_big * BIG_LEN
    last_row = first_row + local_rows - 1
    big_from = jnp.minimum(first_row // BIG_LEN, count_big)
    big_count = jnp.minimum(last_row // BIG_LEN + 1, count_big) - big_from
    small_from = jnp.maximum(first_row - big_rows, 0) // SMALL_LEN
    small_to = jnp.where(last_row >= big_rows, (last_row - big_rows) // SMALL_LEN + 1, small_from)
    count = big_count + (small_to - small_from + 1) // 2
    base = first_row - HALO
    return jnp.stack(
        [big_from, big_count, small_from, count, big_rows, base, jnp.int32(total_rows), base]
    ).astype(jnp.int32)


class Window:
    def __init__(self, start, middle, stop, base, ext_rows):
        aligned = (start - base) // ALIGN * ALIGN
        at_q = pl.multiple_of(jnp.minimum(aligned, ext_rows - QUERIES), ALIGN)
        at_k = pl.multiple_of(jnp.minimum(aligned, ext_rows - KEYS), ALIGN)

        def ids(offset, shape, axis):
            return lax.broadcasted_iota(jnp.int32, shape, axis) + (offset + base)

        def inside(rows):
            return (rows >= start) & (rows < stop)

        key, query = ids(at_k, (KEYS, 1), 0), ids(at_q, (1, QUERIES), 1)
        self.queries, self.keys = pl.ds(at_q, QUERIES), pl.ds(at_k, KEYS)
        self.query_down = inside(ids(at_q, (QUERIES, 1), 0))
        self.key_down = inside(key)
        key_side = jnp.where(self.key_down, (key >= middle).astype(jnp.int32), 2)
        query_side = (query >= middle).astype(jnp.int32)
        self.same = key_side == query_side
        self.both = key_side == jnp.where(inside(query), query_side, 3)


def softmax_down(key, query, same):
    scores = jnp.where(same, dot_nt(key, query), NEGATIVE)
    exps = jnp.exp(scores - jnp.max(scores, axis=0, keepdims=True))
    return exps * (1.0 / jnp.sum(exps, axis=0, keepdims=True))


def attention_block(bounds, rows, weights, biases, start, gains, shifts):
    ext_rows, width = rows.shape
    lanes = width // 4
    local_rows = start.shape[0]

    def body(bounds, ins, outs, _):
        rows, biases = ins[0](), ins[1]()
        held = outs[0].held
        weights = []
        for i, part in enumerate(PARTS):
            weights.append(ins[2 + i // 2]().at[i % 2])

            def project(index, carry):
                at = pl.ds(index * (ext_rows // 2), ext_rows // 2)
                found = dot_nn(rows[at, :], weights[i][:, : 3 * lanes])
                found = found + biases[part : part + 1, : 3 * lanes]
                held[i, at, : 3 * lanes] = found.astype(BF)
                return carry

            lax.fori_loop(0, 2, project, 0)

        def window(start, middle, stop):
            at = Window(start, middle, stop, bounds[5], ext_rows)

            def pair(index, carry):
                for source in (held.at[index],):
                    parts = []
                    for lane in range(0, lanes, HEAD_DIM):
                        query = source[at.queries, lane : lane + HEAD_DIM] * BF(FACTOR)
                        key = source[at.keys, lanes + lane : lanes + lane + HEAD_DIM]
                        value = source[at.keys, 2 * lanes + lane : 2 * lanes + lane + HEAD_DIM]
                        probs = softmax_down(key, query, at.same)
                        parts.append(dot_nn(value.T, probs.astype(BF)))
                    mixed = jnp.concatenate(parts, axis=0).T.astype(BF)
                    old = source[at.queries, 3 * lanes :]
                    source[at.queries, 3 * lanes :] = jnp.where(at.query_down, mixed, old)
                return carry

            lax.fori_loop(0, 4, pair, 0)

        image_loop(bounds, window)
        outs[0].done()
        start, gains, shifts = (item() for item in ins[4:7])

        def finish(index, carry):
            at = pl.ds(index * 128, 128)
            ext = pl.ds(HALO + index * 128, 128)
            found = shifts[3:4, :]
            for i in range(4):
                found = found + dot_nt(held[i, ext, 3 * lanes :], weights[i][:, 3 * lanes :])
            outs[1].held[at, :] = found
            found = start[at, :] + gains[2:3, :] * found
            outs[2].held[at, :] = found
            outs[3].held[at, :] = norm_rows(found, gains[1:2, :], shifts[4:5, :]).astype(BF)
            return carry

        lax.fori_loop(0, local_rows // 128, finish, 0)

    return call(
        body,
        "attention_block",
        bounds,
        [rows, biases, *weights, start, gains, shifts],
        [array((4, ext_rows, width), BF)]
        + [array((local_rows, width), F32)] * 2
        + [array((local_rows, width), BF)],
        cover=40,
    )


def attention_backward(bounds, grad_attn, qkv, weights):
    _, ext_rows, width = qkv.shape
    lanes = width // 4
    local_rows = ext_rows - 2 * HALO

    def body(bounds, ins, outs, scratch):
        ext, grads = scratch
        grad_attn = ins[0]()
        for i in range(4):
            weight = ins[1 + i // 2]()
            grads[i] = dot_nn(grad_attn[...], weight[i % 2, :, 3 * lanes :]).astype(BF)
        held = ins[3]()

        def window(start, middle, stop):
            at = Window(start, middle, stop, bounds[5], ext_rows)

            def pair(index, carry):
                for part in (2 * index, 2 * index + 1):
                    source, grad, out = held.at[part], grads.at[part], ext.at[part]
                    query_parts, key_parts, value_parts = [], [], []
                    for lane in range(0, lanes, HEAD_DIM):
                        query = source[at.queries, lane : lane + HEAD_DIM] * BF(FACTOR)
                        key = source[at.keys, lanes + lane : lanes + lane + HEAD_DIM]
                        value = source[at.keys, 2 * lanes + lane : 2 * lanes + lane + HEAD_DIM]
                        grad_rows = grad[at.queries, lane : lane + HEAD_DIM]
                        probs = jnp.where(at.both, softmax_down(key, query, at.same), 0.0)
                        weighted = probs * dot_nt(value, grad_rows)
                        inner = jnp.sum(weighted, axis=0, keepdims=True)
                        grad_scores = (weighted - probs * inner).astype(BF)
                        query_parts.append(dot_nn((key * BF(FACTOR)).T, grad_scores))
                        key_parts.append(dot_nn(grad_scores, query))
                        value_parts.append(dot_nn(probs.astype(BF), grad_rows))
                    grad_query = jnp.concatenate(query_parts, axis=0).T.astype(BF)
                    old = out[at.queries, :lanes]
                    out[at.queries, :lanes] = jnp.where(at.query_down, grad_query, old)
                    grad_kv = jnp.concatenate(key_parts + value_parts, axis=1).astype(BF)
                    old = out[at.keys, lanes:]
                    out[at.keys, lanes:] = jnp.where(at.key_down, grad_kv, old)
                return carry

            lax.fori_loop(0, 2, pair, 0)

        image_loop(bounds, window)
        at = slice(HALO, HALO + local_rows)
        for i in (2, 3, 0, 1):
            out = outs[i // 2]
            out.held[i % 2, :, : 3 * lanes] = ext[i, at, :]
            out.held[i % 2, :, 3 * lanes :] = held[i, at, 3 * lanes :]
            if i % 2:
                out.done()

    return call(
        body,
        "attention_backward",
        bounds,
        [grad_attn, *weights, qkv],
        [array((2, local_rows, width), BF)] * 2,
        [((4, ext_rows, 3 * lanes), BF), ((4, ext_rows, lanes), BF)],
        grant=16,
        cover=40,
    )


def mlp_up(ids, rows, shifts, weights, pair, cover, slopes=True):
    def body(ids, ins, outs, _):
        rows, weights, shifts = (item() for item in ins)
        for i in range(2):

            def block(index, carry):
                at = pl.ds(index * ROW_BLOCK, ROW_BLOCK)
                pre = dot_nn(rows[at, :], weights[i])
                pre = pre + shifts[pl.ds(7 + (ids[0] ^ PARTS[2 * pair + i]), 1), :]
                share = 0.5 * (1.0 + lax.erf(pre * 0.5**0.5))
                outs[0].held[i, at, :] = (pre * share).astype(BF)
                if slopes:
                    density = jnp.exp(-0.5 * pre * pre) * (2.0 * jnp.pi) ** -0.5
                    outs[1].held[i, at, :] = share + pre * density
                return carry

            lax.fori_loop(0, rows.shape[0] // ROW_BLOCK, block, 0)

    shape = (2, rows.shape[0], weights.shape[2])
    return call(
        body,
        "mlp_up",
        ids,
        [rows, weights, shifts],
        [array(shape, BF)] + [array(shape, F32)] * slopes,
        cover=cover,
    )


def norm_back_rows(grad, rows, gain):
    average = jnp.mean(rows, axis=-1, keepdims=True)
    centered = rows - average
    inverse = lax.rsqrt(jnp.mean(centered * centered, axis=-1, keepdims=True) + EPS_NORM)
    normal = centered * inverse
    scaled = grad * gain
    back = inverse * (
        scaled
        - jnp.mean(scaled, axis=-1, keepdims=True)
        - normal * jnp.mean(scaled * normal, axis=-1, keepdims=True)
    )
    return normal, back


def mlp_back(ids, grad_branch, gains, down, up, slopes, grad_out, middle, branch):
    rows, width = grad_branch.shape
    hidden = up[0].shape[2]

    def body(ids, ins, outs, scratch):
        total, sums = scratch[0], outs[4].held
        grad_branch = ins[0]()
        for i in range(4):
            down, slope, up = (item() for item in ins[1 + 3 * i : 4 + 3 * i])
            pre_grads = outs[i // 2]

            def block(index, carry):
                at = pl.ds(index * ROW_BLOCK, ROW_BLOCK)
                back = dot_nn(grad_branch[at, :], down[...])
                pre_grad = (slope[at, :] * back).astype(BF)
                pre_grads.held[i % 2, at, :] = pre_grad
                product = dot_nt(pre_grad, up[...])
                total[at, :] = product if i == 0 else total[at, :] + product
                return carry + column_sum(pre_grad.astype(F32))

            start = jnp.zeros((1, hidden), F32)
            found = lax.fori_loop(0, rows // ROW_BLOCK, block, start)
            sums[pl.ds(4 + (ids[0] ^ PARTS[i]), 1), :] = found
            if i % 2:
                pre_grads.done()
        gains, grad_out, middle, branch = (item() for item in ins[13:])

        def finish(index, carry):
            at = pl.ds(index * 128, 128)
            grad = total[at, :]
            normal, back = norm_back_rows(grad, middle[at, :], gains[1:2, :])
            found = grad_out[at, :] + back
            scaled = (gains[2:3, :] * found).astype(BF)
            outs[2].held[at, :] = found
            outs[3].held[at, :] = scaled
            return (
                carry[0] + column_sum(grad * normal),
                carry[1] + column_sum(grad),
                carry[2] + column_sum(found * branch[at, :]),
                carry[3] + column_sum(scaled.astype(F32)),
            )

        zero = jnp.zeros((1, width), F32)
        found = lax.fori_loop(0, rows // 128, finish, (zero,) * 4)
        for i in range(4):
            sums[i : i + 1, :] = found[i]

    outs = call(
        body,
        "mlp_back",
        ids,
        [grad_branch]
        + [(kind[i // 2], i % 2) for i in range(4) for kind in (down, slopes, up)]
        + [gains, grad_out, middle, branch],
        [array((2, rows, hidden), BF)] * 2
        + [array((rows, width), F32), array((rows, width), BF), array((8, width), F32)],
        [((rows, width), F32)],
        grant=10,
        cover=40,
    )
    return (list(outs[:2]), *outs[2:])


def qkv_back(ids, masked, gains, grads, weights, start, grad_middle, mlp_sums):
    rows, width = start.shape
    lanes = width // 4

    def body(ids, ins, outs, scratch):
        total, sides = scratch
        small = outs[1].held
        grads = [ins[2 + i // 2]().at[i % 2] for i in range(4)]
        for i, part in enumerate(PARTS):
            sides[part : part + 1, :] = column_sum(grads[i][:, :lanes].astype(F32))
            found = column_sum(grads[i][:, 2 * lanes : 3 * lanes].astype(F32))
            sides[4 + part : 5 + part, :] = found
        for i in range(4):
            at = slice(i * lanes, (i + 1) * lanes)
            small[5:6, at] = sides[pl.ds(ids[0] ^ i, 1), :]
            small[6:7, at] = sides[pl.ds(4 + (ids[0] ^ i), 1), :]
        for i in range(4):
            weight = ins[4 + i // 2]().at[i % 2]

            def block(index, carry):
                at = pl.ds(index * ROW_BLOCK, ROW_BLOCK)
                product = dot_nt(grads[i][at, : 3 * lanes], weight[:, : 3 * lanes])
                total[at, :] = product if i == 0 else total[at, :] + product
                return carry

            lax.fori_loop(0, rows // ROW_BLOCK, block, 0)
        masked, gains = ins[0](), ins[1]()
        start, grad_middle, mlp_sums = (item() for item in ins[6:9])

        def finish(index, carry):
            at = pl.ds(index * 128, 128)
            grad = total[at, :]
            normal, back = norm_back_rows(grad, start[at, :], gains[0:1, :])
            found = grad_middle[at, :] + back
            hidden = masked[at, 0:1] > 0.5
            outs[0].held[at, :] = jnp.where(hidden, 0.0, found)
            return (
                carry[0] + column_sum(grad * normal),
                carry[1] + column_sum(grad),
                carry[2] + column_sum(jnp.where(hidden, found, 0.0)),
            )

        zero = jnp.zeros((1, width), F32)
        found = lax.fori_loop(0, rows // 128, finish, (zero,) * 3)
        small[0:1, :], small[4:5, :], small[10:11, :] = found
        small[1:2, :], small[2:3, :] = mlp_sums[0:1, :], mlp_sums[2:3, :]
        small[7:8, :], small[8:9, :] = mlp_sums[3:4, :], mlp_sums[1:2, :]
        small[3:4, :], small[9:10, :] = zero, zero
        small[11:15, :] = mlp_sums[4:8, :]
        small[15:16, :] = zero

    return call(
        body,
        "qkv_back",
        ids,
        [masked, gains, *grads, *weights, start, grad_middle, mlp_sums],
        [array((rows, width), F32), array((16, width), F32)],
        [((rows, width), F32), ((8, lanes), F32)],
        grant=10,
        cover=40,
    )


def weight_grad(ids, lefts, right, other, segments):
    rows, width = lefts[0].shape
    count = lax.axis_size("dp")
    z_count, block = count // 2, width // count
    total = right.shape[2]
    if block % ALIGN:
        found = []
        for which in range(2):
            parts = [
                dot_tn(lefts[2 * left], right[which, :, lane : lane + n])
                + dot_tn(lefts[2 * left + 1], other[which, :, lane : lane + n])
                for left, lane, n in segments
            ]
            found.append(jnp.concatenate(parts, axis=1).reshape(z_count, 2, block, total))
        x = ids[1]

        def at_x(value, which):
            return lax.dynamic_index_in_dim(value, which, 1, keepdims=False)

        own, across = found
        sent = at_x(own, 1 - x), at_x(across, x), at_x(across, 1 - x)
        return tuple(value.astype(BF) for value in sent), at_x(own, x)

    def body(ids, ins, outs, scratch):
        turned, product = scratch
        for i in range(len(lefts)):
            turned[i] = ins[i]()[...].T
        right, other = ins[-2](), ins[-1]()
        to_x, to_y, to_far, kept = outs
        for which, near_out, far_out in ((1, to_y, to_far), (0, kept, to_x)):
            for left, lane, n in segments:
                lanes = slice(lane, lane + n)
                product[:, lanes] = dot_nn(
                    turned[2 * left], right[which, :, lanes]
                ) + dot_nn(turned[2 * left + 1], other[which, :, lanes])
            for z in range(z_count):
                far = pl.multiple_of((2 * z + 1 - ids[1]) * block, ALIGN)
                near = pl.multiple_of((2 * z + ids[1]) * block, ALIGN)
                far_out.held[z] = product[pl.ds(far, block), :].astype(BF)
                near_out.held[z] = product[pl.ds(near, block), :].astype(near_out.held.dtype)
            near_out.done()
            far_out.done()

    shape = (z_count, block, total)
    *sent, kept = call(
        body,
        "weight_grad",
        ids,
        [*lefts, right, other],
        [array(shape, BF)] * 3 + [array(shape, F32)],
        [((len(lefts), width, rows), BF), ((width, total), F32)],
        grant=12,
    )
    return tuple(sent), kept


def first_hop(ids, lefts, right, other, cover=10):
    rows, width = lefts[0].shape
    count, total = lax.axis_size("dp"), right.shape[2]
    z_count, block, half = count // 2, width // count, total // 2
    if block % ALIGN:
        own, across = (
            (dot_tn(lefts[0], right[which]) + dot_tn(lefts[1], other[which])).reshape(
                z_count, 2, block, total
            )
            for which in range(2)
        )
        x = ids[1]

        def at_x(value, which):
            return lax.dynamic_index_in_dim(value[..., half:], which, 1, keepdims=False)

        over_x = jnp.stack([at_x(own, 1 - x), at_x(across, 1 - x)])
        kept = own[..., :half], at_x(across, x), at_x(own, x)
        return (across[..., :half].astype(BF), over_x.astype(BF)), kept

    def body(ids, ins, outs, scratch):
        turned, product = scratch
        for i in range(2):
            turned[i] = ins[i]()[...].T
        right, other = ins[2](), ins[3]()
        over_y, over_x, low, across_high, own_high = (out.held for out in outs)

        def compute(which, lanes):
            return dot_nn(turned[0], right[which, :, lanes]) + dot_nn(
                turned[1], other[which, :, lanes]
            )

        over_y[...] = compute(1, slice(0, half)).astype(BF)
        low[...] = compute(0, slice(0, half))
        for which, kept in ((1, across_high), (0, own_high)):
            product[...] = compute(which, slice(half, total))
            for z in range(z_count):
                far = pl.multiple_of((2 * z + 1 - ids[1]) * block, ALIGN)
                near = pl.multiple_of((2 * z + ids[1]) * block, ALIGN)
                over_x[which, z] = product[pl.ds(far, block), :].astype(BF)
                kept[z] = product[pl.ds(near, block), :]

    high = (z_count, block, half)
    outs = call(
        body,
        "first_hop",
        ids,
        [*lefts, right, other],
        [
            array((width, half), BF),
            array((2,) + high, BF),
            array((width, half), F32),
            array(high, F32),
            array(high, F32),
        ],
        [((2, width, rows), BF), ((width, half), F32)],
        grant=12,
        cover=cover,
    )
    return tuple(outs[:2]), tuple(outs[2:])


def second_hop(ids, chunks):
    z_count, block, half = chunks[0][1][2].shape
    if block % ALIGN:
        x, results = ids[1], []
        for (over_y, over_x), (low, across_high, own_high) in chunks:
            low = low + over_y.astype(F32)
            far, near = (
                lax.dynamic_index_in_dim(low, which, 1, keepdims=False) for which in (1 - x, x)
            )
            high = across_high + over_x[1].astype(F32)
            results.append(
                (far.astype(BF), high.astype(BF), near, own_high + over_x[0].astype(F32))
            )
        joined = [jnp.concatenate(parts, axis=-1) for parts in zip(*results)]
        return tuple(joined[:2]), tuple(joined[2:])

    def body(ids, ins, outs, _):
        sent_x, sent_y, kept_low, kept_high = (out.held for out in outs)
        for i in range(len(chunks)):
            lanes = slice(i * half, (i + 1) * half)
            low, across_high, own_high, over_y, over_x = (
                item() for item in ins[5 * i : 5 * i + 5]
            )
            for z in range(z_count):
                far = pl.ds(pl.multiple_of((2 * z + 1 - ids[1]) * block, ALIGN), block)
                near = pl.ds(pl.multiple_of((2 * z + ids[1]) * block, ALIGN), block)
                sent_x[z, :, lanes] = (low[far, :] + over_y[far, :].astype(F32)).astype(BF)
                kept_low[z, :, lanes] = low[near, :] + over_y[near, :].astype(F32)
                sent_y[z, :, lanes] = (across_high[z] + over_x[1, z].astype(F32)).astype(BF)
                kept_high[z, :, lanes] = own_high[z] + over_x[0, z].astype(F32)

    high = (z_count, block, half * len(chunks))
    outs = call(
        body,
        "second_hop",
        ids,
        [value for received, kept in chunks for value in (*kept, *received)],
        [array(high, BF)] * 2 + [array(high, F32)] * 2,
        cover=2,
    )
    return tuple(outs[:2]), tuple(outs[2:])


def in_halves(value):
    high = value.astype(BF)
    return high, (value - high.astype(F32)).astype(BF)


def plane_sum(ids, parts, vectors=None):
    z_count, block, _ = parts[0][0].shape
    widths = [kept.shape[2] for kept, _ in parts]
    if z_count == 4 and block % ALIGN == 0:

        def body(ids, ins, outs, _):
            for step in (1, 2, 3, 0):
                at, place, lane = lax.rem(ids[2] + step, z_count), 0, 0
                out = outs[step].held
                for (_, received), n in zip(parts, widths):
                    found = ins[place]()[at]
                    for item in ins[place + 1 : place + 1 + len(received)]:
                        found = found + item()[at].astype(F32)
                    out[:block, lane : lane + n] = found.astype(out.dtype)
                    place, lane = place + 1 + len(received), lane + n
                if step and vectors is not None:
                    for i, part in enumerate(in_halves(ins[-1]()[...])):
                        out[block + 16 * i : block + 16 * (i + 1), :] = part

        below = [] if vectors is None else [vectors]
        shape = (block, sum(widths))
        longer = (block + 32 * len(below), sum(widths))
        own, *sent = call(
            body,
            "plane_sum",
            ids,
            [value for kept, received in parts for value in (kept, *received)] + below,
            [array(shape, F32)] + [array(longer, BF)] * 3,
            cover=2,
        )
        return tuple(sent), own
    sums = [sum((value.astype(F32) for value in received), kept) for kept, received in parts]
    return (), jnp.concatenate(sums, axis=-1)


def last_hop(sent, own, steps):
    if not sent:
        return [], own if own.ndim == 2 else scatter_z(own)
    with jax.named_scope("g3z"):
        return [send_digit(sent[step - 1], 1, 4, step) for step in steps], own


def adamw_step(master, first, second, gradient, rate, decay, correction):
    first_new = 0.5 * first + 0.5 * gradient
    second_new = 0.5 * second + 0.5 * gradient * gradient
    update = first_new / correction / (jnp.sqrt(second_new / correction) + ADAM_EPS)
    master_new = master - rate * (update + decay * master)
    return (master_new, first_new, second_new, master_new.astype(BF))


def update_weights(ids, correction, received, own, states, rates, pick, vectors=None, others=()):
    block = own.shape[0]
    if block % ALIGN:
        results = []
        for i, (state, rate) in enumerate(zip(states, rates)):
            results += adamw_step(*state, pick(own, i), rate, DECAY, correction[0, 0])
        return results
    places = list(states) + list(others)

    def body(ids, ins, outs, scratch):
        correction, total = ins[0]()[0:1, 0:1], scratch[0]
        received_refs = [item() for item in ins[2 : 2 + len(received)]]
        found = ins[1]()[...]
        for item in received_refs:
            found = found + item[:block, :].astype(F32)
        total[...] = found
        grads = [(pick, i, rate, DECAY) for i, rate in enumerate(rates)]
        if vectors is not None:
            by_z = scratch[1]
            by_z[ids[2]] = sum(part.astype(F32) for part in in_halves(ins[-1]()[...]))
            for step, item in enumerate(received_refs, 1):
                halves = (item[block + 16 * i : block + 16 * (i + 1), :] for i in range(2))
                at = lax.bitwise_and(ids[2] - step, 3)
                by_z[at] = sum(part.astype(F32) for part in halves)
            sums = (by_z[0] + by_z[1]) + (by_z[2] + by_z[3])
            grads += [
                (lambda _, i: sums[0:4, :], 0, 0.1, 0.0),
                (lambda _, i: sums[4:15, :], 0, 0.3, 0.0),
            ]
        at = 2 + len(received)
        for i, (choose, which, rate, decay) in enumerate(grads):
            master, first, second = (item()[...] for item in ins[at + 3 * i : at + 3 * i + 3])
            results = adamw_step(
                master, first, second, choose(total, which), rate, decay, correction
            )
            for out, value in zip(outs[4 * i : 4 * i + 4], results):
                out.held[...] = value

    outputs = []
    for state in places:
        outputs += [array(state[0].shape, F32)] * 3 + [array(state[0].shape, BF)]
    flat = [value for state in places for value in state]
    scratch = [(own.shape, F32)]
    if vectors is not None:
        flat.append(vectors)
        scratch.append(((4,) + vectors.shape, F32))
    return call(
        body,
        "update_weights",
        ids,
        [correction, own, *received, *flat],
        outputs,
        scratch,
    )


def pack_weights(ids, qkv_master, out_master):
    count, rows, lanes = qkv_master.shape
    if rows % ALIGN:
        parts = [qkv_master[i] for i in range(count)] + [out_master.T]
        return jnp.concatenate(parts, axis=1).astype(BF)

    def body(ids, ins, outs, _):
        qkv = ins[0]()
        for i in range(count):
            outs[0].held[:, i * lanes : (i + 1) * lanes] = qkv[i].astype(BF)
        outs[0].held[:, count * lanes :] = ins[1]()[...].T.astype(BF)

    return call(
        body,
        "pack_weights",
        ids,
        [qkv_master, out_master],
        [array((rows, (count + 1) * lanes), BF)],
    )[0]


def pack_down(ids, up_master, down_turned):
    rows, width = up_master.shape
    if rows % ALIGN:
        return jnp.concatenate([up_master, down_turned], axis=1).astype(BF)

    def body(ids, ins, outs, _):
        outs[0].held[:, :width] = ins[0]()[...].astype(BF)
        outs[0].held[:, width:] = ins[1]()[...].astype(BF)

    return call(
        body, "pack_down", ids, [up_master, down_turned], [array((rows, 2 * width), BF)]
    )[0]


def norm_rows(values, gain, shift):
    average = jnp.mean(values, axis=-1, keepdims=True)
    centered = values - average
    inverse = lax.rsqrt(jnp.mean(centered * centered, axis=-1, keepdims=True) + EPS_NORM)
    return centered * inverse * gain + shift


def on_device(
    patches,
    cotangent,
    mask_rows,
    count_big,
    pos_big,
    pos_small,
    step_count,
    qkv_master,
    qkv_first,
    qkv_second,
    out_master,
    out_first,
    out_second,
    up_master,
    up_first,
    up_second,
    down_master,
    down_first,
    down_second,
    norm_gains,
    gain_first,
    gain_second,
    shifts,
    shift_first,
    shift_second,
):
    tensor_id = lax.axis_index("tensor")
    local_rows = patches.shape[0]
    total_rows = 4 * local_rows
    lanes = qkv_master.shape[2]
    hidden_lanes = up_master.shape[1]
    big_rows = count_big[0] * BIG_LEN
    used_rows = big_rows + (total_rows - big_rows) // SMALL_LEN * SMALL_LEN
    first_row = tensor_id * local_rows

    in_kernels = up_master.shape[0] % ALIGN == 0 and lax.axis_size("dp") == 8
    bounds = image_bounds(count_big[0], first_row, local_rows, total_rows)
    dp_id = lax.axis_index("dp")
    ids = jnp.stack(
        [tensor_id, lax.bitwise_and(dp_id, 1), lax.shift_right_logical(dp_id, 1)]
    ).astype(jnp.int32)
    own = slice(HALO, HALO + local_rows)
    correction = 1.0 - jnp.power(jnp.float32(0.5), step_count[0].astype(F32))

    down_state = (down_master.T, down_first.T, down_second.T)

    local_a = pack_weights(ids, qkv_master, out_master)
    with jax.named_scope("wa"):
        z_a = gather_z(local_a)
    payload = jnp.concatenate(
        [patches, jnp.broadcast_to(mask_rows[:, None].astype(BF), (local_rows, 128))], axis=1
    )
    up_hops, down_hops = [(0, 1), (1, 2), (2, 3)], [(1, 0), (2, 1), (3, 2)]
    with jax.named_scope("halo"):
        halo_before = lax.ppermute(payload[-HALO:], "tensor", up_hops)
        halo_after = lax.ppermute(payload[:HALO], "tensor", down_hops)
    local_bc = pack_down(after(ids, local_a), up_master, down_state[0])

    z_a, halo_before, halo_after, local_bc = gate(z_a, halo_before, halo_after, local_bc)
    (z_a,) = place_z(ids, z_a)
    with jax.named_scope("wbc"):
        z_bc = gather_z(after(local_bc, z_a))
    with jax.named_scope("wa"):
        plane_a = send_plane(z_a, z_a, z_a)
    payload = jnp.concatenate([halo_before, payload, halo_after], axis=0)
    ext_rows = payload.shape[0]
    row_ids = first_row - HALO + jnp.arange(ext_rows, dtype=jnp.int32)
    remainder = row_ids - big_rows
    is_big = (row_ids >= 0) & (row_ids < big_rows)
    is_valid = (row_ids >= 0) & (row_ids < used_rows)
    is_small = is_valid & jnp.logical_not(is_big)
    position = jnp.where(is_big, row_ids % BIG_LEN, remainder % SMALL_LEN)
    masked_ext = (payload[:, D] == 1) & is_valid
    pick_big = (
        (position[:, None] == jnp.arange(BIG_LEN, dtype=jnp.int32)[None, :]) & is_big[:, None]
    ).astype(BF)
    pick_small = (
        (position[:, None] == jnp.arange(SMALL_LEN, dtype=jnp.int32)[None, :]) & is_small[:, None]
    ).astype(BF)
    placed = dot_nn(pick_big, pos_big) + dot_nn(pick_small, pos_small)
    start_ext = (
        jnp.where(masked_ext[:, None], shifts[6][None, :], payload[:, :D].astype(F32)) + placed
    )
    normed_ext = norm_rows(start_ext, norm_gains[0], shifts[0]).astype(BF)
    start_rows, masked, valid_local = start_ext[own], masked_ext[own], is_valid[own]
    normed = normed_ext[own]
    masked = jnp.broadcast_to(masked[:, None].astype(F32), (local_rows, 128))
    grad_out = cotangent.astype(F32) * valid_local[:, None].astype(F32)
    grad_branch = (norm_gains[3] * grad_out).astype(BF)
    biases = jnp.stack(
        [
            jnp.concatenate(
                [
                    lax.dynamic_slice_in_dim(shifts[1], (tensor_id ^ i) * lanes, lanes),
                    jnp.zeros((lanes,), F32),
                    lax.dynamic_slice_in_dim(shifts[2], (tensor_id ^ i) * lanes, lanes),
                    jnp.zeros((lanes,), F32),
                ]
            )
            for i in range(4)
        ]
    )

    z_a, plane_a, z_bc, normed_ext, start_rows, grad_branch, normed, biases = gate(
        z_a, plane_a, z_bc, normed_ext, start_rows, grad_branch, normed, biases
    )
    z_b, z_c = place_z(ids, z_bc, 2)
    with jax.named_scope("wb"):
        plane_b = send_plane(z_b, z_b, z_b)
    own_a = place_x(ids, z_a, *plane_a)
    with jax.named_scope("wa/core"):
        a_all = [own_a, send_core(own_a)]
    with jax.named_scope("pair"):
        grad_branch_other = send_core(grad_branch)
    qkv, branch_attn, middle, normed_two = attention_block(
        after(bounds, z_b), normed_ext, a_all, biases, start_rows, norm_gains, shifts
    )

    plane_b, z_b, z_c, normed_two, grad_branch_other = gate(
        plane_b, z_b, z_c, normed_two, grad_branch_other
    )
    own_b = place_x(ids, z_b, *plane_b)
    with jax.named_scope("wb/core"):
        b_all = [own_b, send_core(own_b)]
    with jax.named_scope("pair"):
        normed_two_other = send_core(normed_two)
    with jax.named_scope("wc"):
        plane_c = send_plane(z_c, z_c, z_c)
    found = mlp_up(ids, normed_two, shifts, b_all[0], 0, 40)
    other = mlp_up(after(ids, found), normed_two, shifts, b_all[1], 1, 0)
    hidden, slopes = zip(found, other)
    (hidden_other,) = mlp_up(after(ids, other), normed_two_other, shifts, own_b, 0, 0, False)
    chunk_c = first_hop(ids, (grad_branch, grad_branch_other), hidden[0], hidden_other, 0)

    plane_c, normed, chunk_c = gate(plane_c, normed, chunk_c)
    own_c = place_x(ids, z_c, *plane_c)
    with jax.named_scope("wc/core"):
        c_all = [own_c, send_core(own_c)]

    with jax.named_scope("gc"):
        first_c = send_first(*chunk_c[0])
    with jax.named_scope("pair"):
        normed_other = send_core(normed)
    pre_grad, grad_middle, grad_attn, mlp_sums = mlp_back(
        ids, grad_branch, norm_gains, c_all, b_all, slopes, grad_out, middle, branch_attn
    )
    first_c, normed_other, pre_grad, grad_attn = gate(first_c, normed_other, pre_grad, grad_attn)
    with jax.named_scope("gb"):
        pre_grad_other = send_core(pre_grad[1])
    with jax.named_scope("halo"):
        halo_before = lax.ppermute(grad_attn[-HALO:], "tensor", up_hops)
        halo_after = lax.ppermute(grad_attn[:HALO], "tensor", down_hops)
    with jax.named_scope("pair"):
        grad_attn_other = send_core(grad_attn)
    sent_c, kept_c = second_hop(ids, ((first_c, chunk_c[1]),))
    chunk_b = first_hop(
        after(ids, sent_c), (normed_two, normed_two_other), pre_grad[0], pre_grad_other
    )
    halo_before, halo_after, chunk_b, sent_c, grad_attn, grad_attn_other = gate(
        halo_before, halo_after, chunk_b, sent_c, grad_attn, grad_attn_other
    )
    with jax.named_scope("gc"):
        second_c = send_second(*sent_c)
    with jax.named_scope("gb"):
        first_b = send_first(*chunk_b[0])
    grad_qkv = attention_backward(
        after(bounds, chunk_b[0]), [halo_before, grad_attn, halo_after], qkv, a_all
    )
    second_c, first_b, grad_qkv = gate(second_c, first_b, grad_qkv)
    sent_b, kept_b = second_hop(ids, ((first_b, chunk_b[1]),))
    with jax.named_scope("gb"):
        second_b = send_second(*sent_b)
    with jax.named_scope("ga"):
        grad_qkv_other = send_core(grad_qkv[1])
    chunk_a = weight_grad(
        after(ids, sent_b),
        (normed, normed_other, grad_attn, grad_attn_other),
        grad_qkv[0],
        grad_qkv_other,
        ((0, 0, 2 * lanes), (0, 2 * lanes, lanes), (1, 3 * lanes, lanes)),
    )
    x_b, chunk_a, grad_qkv = gate(second_b[0], chunk_a, grad_qkv)
    with jax.named_scope("gbc"):
        parts = zip((*kept_c, *kept_b), (*second_c, x_b, second_b[1]))
        sent, sum_bc = plane_sum(ids, [(kept, (value,)) for kept, value in parts])
        early_bc, sum_bc = last_hop(sent, sum_bc, (2,))
    with jax.named_scope("ga"):
        plane_a = send_plane(*chunk_a[0])
    patch_grad, small = qkv_back(
        after(ids, sent), masked, norm_gains, grad_qkv, a_all, start_rows, grad_middle, mlp_sums
    )
    hidden = after(hidden, chunk_a)
    branch_mlp = shifts[5] + sum(
        dot_nt(hidden[i // 2][i % 2], c_all[i // 2][i % 2]) for i in range(4)
    )
    layer_out = (middle + norm_gains[3] * branch_mlp).astype(BF)
    extra = [jnp.sum(grad_out * branch_mlp, axis=0), jnp.sum(grad_branch.astype(F32), axis=0)]
    early_bc, sent, small, layer_out, extra, x_a = gate(
        early_bc, sent, small, layer_out, extra, plane_a[0]
    )
    is_row = [lax.broadcasted_iota(jnp.int32, small.shape, 0) == row for row in (3, 9)]
    small = jnp.where(is_row[0], extra[0], jnp.where(is_row[1], extra[1], small))
    with jax.named_scope("small"):
        if not in_kernels:
            small = sum_over_z(small)
    with jax.named_scope("gbc"):
        late_bc, sum_bc = last_hop(sent, sum_bc, (1, 3))
    last_bc = [*early_bc, *late_bc]
    with jax.named_scope("small"):
        small = sum_over_plane(small)
    *plane_a, small = gate(x_a, *plane_a[1:], small)
    with jax.named_scope("ga"):
        sent, sum_a = plane_sum(ids, [(chunk_a[1], plane_a)], small if in_kernels else None)
        last_a, sum_a = last_hop(sent, sum_a, (1, 2, 3))
    vectors = ((norm_gains, gain_first, gain_second), (shifts, shift_first, shift_second))
    if not in_kernels:
        gain_res = adamw_step(*vectors[0], small[:4], 0.1, 0.0, correction)
        shift_res = adamw_step(*vectors[1], small[4:15], 0.3, 0.0, correction)
    correction = jnp.broadcast_to(correction, (8, 128))
    middle_lane = sum_bc.shape[1] // 2

    def pick_bc(total, i):
        return total[:, middle_lane:] if i == 0 else total[:, :middle_lane]

    def pick_a(total, i):
        if i == 1:
            return total[:, 3 * lanes :].T
        return jnp.stack([total[:, at * lanes : (at + 1) * lanes] for at in range(3)])

    up_down = update_weights(
        after(ids, sent, sum_a),
        correction,
        last_bc,
        sum_bc,
        ((up_master, up_first, up_second), down_state),
        (D ** (-0.5), FF ** (-0.5)),
        pick_bc,
    )
    qkv_out = update_weights(
        after(ids, up_down),
        correction,
        last_a,
        sum_a,
        ((qkv_master, qkv_first, qkv_second), (out_master, out_first, out_second)),
        (D ** (-0.5), (D // 16) ** (-0.5)),
        pick_a,
        *((small, vectors) if in_kernels else ()),
    )
    if in_kernels:
        qkv_out, gain_res, shift_res = qkv_out[:8], qkv_out[8:12], qkv_out[12:]
    down_out = [value.T for value in up_down[4:]]
    return (layer_out, patch_grad, *qkv_out, *up_down[:4], *down_out, *gain_res, *shift_res)


def solution(mesh):
    rows = P(("dp", "tensor"), None)
    qkv = (P(None, "dp", "tensor"),)
    tensor_first, dp_first, whole = (P("tensor", "dp"),), (P("dp", "tensor"),), (P(),)
    weights = tuple(
        spec * 3 for spec in (qkv, tensor_first, dp_first, tensor_first)
    )
    results = tuple(
        spec * 4 for spec in (qkv, tensor_first, dp_first, tensor_first)
    )
    return jax.shard_map(
        on_device,
        mesh=mesh,
        in_specs=(rows, rows, P(("dp", "tensor")), P("dp")) + whole * 3 + sum(weights, ()) + whole * 6,
        out_specs=(rows, rows) + sum(results, ()) + whole * 8,
        check_vma=False,
    )
```
